256 devices in a mesh: scene: 8 (over x, core), region: 32 (over z, y).
Axes of the slice: x: 4, y: 4, z: 8, core: 2. Of those that a mesh axis runs over, the one named last changes fastest.
Arguments:
- tiles: bfloat16 [8, 64, 32, 32, 256], P('scene', 'region'), may hold values from -6 to 6
- cotangent: bfloat16 [8, 64, 16, 16, 256], P('scene', 'region'), may hold values from -6 to 6
- positions: int32 [8, 64], P('scene', 'region'), may hold values from 0 to 63, each once within a row
- clear: int32 [8, 64], P('scene', 'region'), may hold values 0 or 1
- w_first: bfloat16 [2304, 256], P('scene'), may hold values from -0.125 to 0.125
- w_second: bfloat16 [2304, 256], P('scene'), may hold values from -0.125 to 0.125
Outputs:
- features: bfloat16 [8, 64, 16, 16, 256], P('scene', 'region')
- grad_first: float32 [2304, 256], P('region', 'scene')
- grad_second: float32 [2304, 256], P('region', 'scene')
The draws below stay inside these ranges and needn't reach their ends.
Inputs may be any that keep to these rules, and one draw needn't show every extreme that they name: Each scene's row is a permutation of the grid positions 0 to 63.
All inputs are finite; a program needn't handle non-finite values. No bound on the sum of `clear` on one device may be relied on, other than what follows from the above.
Results may differ from the reference program's by a relative error of at most 0.005.
Values may be sent and summed in bfloat16 or wider, within the bound.
A program may use at most 128 MiB of HBM per device.

```python
import math
import jax
import jax.numpy as jnp
from jax import lax

C = 256
P_SIZE = 32
GW = 4
SCENES = 8
NTILE = 64
GH = 16


def touch_ends(array, stream_key, smallest, top_value):
    dims = array.shape
    place = [jax.random.randint(jax.random.fold_in(stream_key, axis), (), 0, dims[axis]) for axis in range(len(dims))]
    array = array.at[tuple(place)].set(smallest)
    longest = dims.index(max(dims))
    place[longest] = (place[longest] + 1) % dims[longest]
    return array.at[tuple(place)].set(top_value)


def shard_levels(own_key, extent, shards, low, largest):
    def one(axis_at, shards_of):
        steps = jax.random.uniform(jax.random.fold_in(jax.random.fold_in(own_key, 6), axis_at), (shards_of,), jnp.float32, low / len(shards), largest / len(shards))
        return jnp.repeat(jnp.exp(steps), extent[axis_at] // shards_of).reshape((-1,) + (1,) * (len(extent) - axis_at - 1))

    gain = one(*shards[0])
    for cut in shards[1:]:
        gain = gain * one(*cut)
    return gain


def noise(stream_key, shape, scale, reach, split=(), held_as=jnp.bfloat16):
    values = scale * jax.random.normal(stream_key, shape, jnp.float32)
    if split:
        values = values * shard_levels(stream_key, shape, split, -0.22, 0.18)
    return jnp.clip(values, -reach, reach).astype(held_as)


def setup_inputs(seed: int = 0) -> dict:
    keys = jax.random.split(jax.random.key(seed), 7)
    return {
        "tiles": noise(keys[0], (SCENES, NTILE, P_SIZE, P_SIZE, C), 1.0, 6.0, ((0, 8), (1, 32))),
        "cotangent": noise(keys[1], (SCENES, NTILE, P_SIZE // 2, P_SIZE // 2, C), 1.0, 6.0, ((0, 8), (1, 32))),
        "positions": jax.vmap(lambda own: jax.random.permutation(own, NTILE))(jax.random.split(keys[2], SCENES)).reshape((SCENES, NTILE)).astype(jnp.int32),
        "clear": touch_ends((jax.random.randint(keys[3], (SCENES, NTILE), 0, 4) < 3).astype(jnp.int32), jax.random.fold_in(keys[3], 1), 0, 1),
        "w_first": noise(keys[4], (9 * C, C), (9 * C) ** -0.5, 0.125, ((0, 8),)),
        "w_second": noise(keys[5], (9 * C, C), (9 * C) ** -0.5, 0.125, ((0, 8),)),
    }


def silu_slope(pre_act):
    sigmoid_v = jax.nn.sigmoid(pre_act)
    return sigmoid_v * (1.0 + pre_act * (1.0 - sigmoid_v))

def to_image(tiles_now, positions_now, tile_side):
    channels = tiles_now.shape[-1]
    order = jnp.argsort(positions_now).astype(jnp.int32)
    placed = jnp.take(tiles_now, order, axis=0)
    placed = placed.reshape(GH, GW, tile_side, tile_side, channels)
    return placed.transpose(0, 2, 1, 3, 4).reshape(GH * tile_side, GW * tile_side, channels)

def from_image(image_full, positions_now, tile_side):
    channels = image_full.shape[-1]
    blocks = image_full.reshape(GH, tile_side, GW, tile_side, channels).transpose(0, 2, 1, 3, 4)
    blocks = blocks.reshape(GH * GW, tile_side, tile_side, channels)
    return jnp.take(blocks, positions_now.astype(jnp.int32), axis=0)

def convolve(image_full, kernel, stride):
    channels = image_full.shape[-1]
    taps = kernel.astype(jnp.float32).reshape(3, 3, channels, channels)
    result = lax.conv_general_dilated(image_full.astype(jnp.float32)[None], taps, (stride, stride), ((1, 1), (1, 1)), dimension_numbers=('NHWC', 'HWIO', 'NHWC'), precision=lax.Precision.HIGHEST)
    return result[0]

def one_scene(tiles_now, cotangent_now, positions_now, clear_now, w_first, w_second):
    channels = tiles_now.shape[-1]
    height = GH * P_SIZE
    across = GW * P_SIZE
    image_full = to_image(tiles_now, positions_now, P_SIZE)
    pre_act = convolve(image_full, w_first, 1)
    hidden = jax.nn.silu(pre_act).astype(jnp.bfloat16)
    output_image = convolve(hidden, w_second, 2).astype(jnp.bfloat16)
    features = from_image(output_image, positions_now, P_SIZE // 2)
    masked = (cotangent_now.astype(jnp.float32) * clear_now.astype(jnp.float32)[:, None, None, None]).astype(jnp.bfloat16)
    grad_image = to_image(masked, positions_now, P_SIZE // 2).astype(jnp.float32)
    hidden_pad = jnp.pad(hidden.astype(jnp.float32), ((1, 1), (1, 1), (0, 0)))
    input_pad = jnp.pad(image_full.astype(jnp.float32), ((1, 1), (1, 1), (0, 0)))
    second_taps = w_second.astype(jnp.float32).reshape(9, channels, channels)
    spread = jnp.zeros((height + 2, across + 2, channels), jnp.float32)
    second_parts = []
    for tap_row in range(3):
        for tap_col in range(3):
            window = hidden_pad[tap_row:tap_row + height:2, tap_col:tap_col + across:2]
            second_parts.append(jnp.einsum('hwc,hwd->cd', window, grad_image, precision=lax.Precision.HIGHEST))
            added = jnp.einsum('hwd,cd->hwc', grad_image, second_taps[3 * tap_row + tap_col], precision=lax.Precision.HIGHEST)
            spread = spread.at[tap_row:tap_row + height:2, tap_col:tap_col + across:2].add(added)
    dhidden = spread[1:height + 1, 1:across + 1]
    dpre = (dhidden * silu_slope(pre_act)).astype(jnp.bfloat16).astype(jnp.float32)
    first_parts = []
    for tap_row in range(3):
        for tap_col in range(3):
            window = input_pad[tap_row:tap_row + height, tap_col:tap_col + across]
            first_parts.append(jnp.einsum('hwc,hwd->cd', window, dpre, precision=lax.Precision.HIGHEST))
    grad_first = jnp.stack(first_parts, axis=0).reshape(9 * channels, channels)
    grad_second = jnp.stack(second_parts, axis=0).reshape(9 * channels, channels)
    return (features, grad_first, grad_second)

def reference(tiles, cotangent, positions, clear, w_first, w_second):

    def scene_step(packed):
        return one_scene(packed[0], packed[1], packed[2], packed[3], w_first, w_second)
    features, grad_first, grad_second = lax.map(scene_step, (tiles, cotangent, positions, clear))
    sum_sq = lax.optimization_barrier(jnp.sum(grad_first * grad_first, axis=(1, 2))) + lax.optimization_barrier(jnp.sum(grad_second * grad_second, axis=(1, 2)))
    factor = 3.0 * C * math.sqrt(2.0) / (jnp.sqrt(sum_sq) + 0.01)
    out_first = lax.optimization_barrier(jnp.sum(factor[:, None, None] * grad_first, axis=0)) / SCENES
    out_second = lax.optimization_barrier(jnp.sum(factor[:, None, None] * grad_second, axis=0)) / SCENES
    return (features, out_first, out_second)
```

```python
import math

import jax
import jax.numpy as jnp
import ml_dtypes
import numpy as np
from jax import lax
from jax.experimental import pallas as pl
from jax.experimental.pallas import tpu as pltpu
from jax.sharding import PartitionSpec as P

MESH = pl.DeviceIdType.MESH
BF = jnp.bfloat16
F32 = jnp.float32
GW, GH = 4, 16
C = 256
REG, ZN, YN, SC = 32, 8, 4, 8
WROWS = 288
LEFT = 48
VMEM_LIMIT = 56 * 1024 * 1024


def hot(rows, cols, pairs):
    out = np.zeros((rows, cols), np.float32)
    for row, col in pairs:
        out[row, col] = 1.0
    return out.astype(ml_dtypes.bfloat16)


def halo_row(k, t, q):
    return k * 16 + t * 8 + q


def place_tables():
    cols = lambda blk, b: 2 * b - 1 + blk
    body = hot(512, 256, [
        (blk * 128 + h * 16 + b, h * 32 + cols(blk, b))
        for blk in range(4) for h in range(8) for b in range(16) if 0 <= cols(blk, b) < 32
    ])
    sides = np.stack([
        hot(512, 128, [(h * 16, halo_row(h, t, 2)) for h in range(8)]
            + [(3 * 128 + h * 16 + 15, halo_row(h, t, 5)) for h in range(8)])
        for t in range(2)
    ])
    edge_q = (1, 0, 4)
    corner_left, corner_right = (1, 3, 7), (4, 5, 8)

    def edge_source(t, sel, col):
        if col < 0:
            return halo_row(corner_left[sel], t, 7)
        if col > 31:
            return halo_row(corner_right[sel], t, 7)
        return halo_row(col, t, edge_q[sel])

    edges = np.stack([
        hot(192, 512, [
            (sel * 64 + blk * 16 + b, edge_source(t, sel, cols(blk, b)))
            for sel in range(3) for blk in range(4) for b in range(16)
        ])
        for t in range(2)
    ])

    def left_source(t, hh, j):
        if 0 <= hh < 32:
            return halo_row(hh, t, (3, 2)[j]) if j < 2 else None
        sel = {-2: 0, -1: 1, 32: 2}[hh]
        if j < 2:
            return halo_row(((0, 1), (2, 3), (6, 7))[sel][j], t, 7)
        return halo_row(0, t, edge_q[sel])

    left = np.stack([
        hot(9 * LEFT, 512, [
            ((3 * i + j) * LEFT + g, left_source(t, g + i - 2, j))
            for i in range(3) for j in range(3) for g in range(33)
            if left_source(t, g + i - 2, j) is not None
        ])
        for t in range(2)
    ])
    first_col = hot(3 * LEFT, 1024, [
        (i * LEFT + g, (g + i - 2) * 32) for i in range(3) for g in range(33) if 0 <= g + i - 2 < 32
    ])
    shift = hot(272, 272, [(a * 16 + b, a * 16 + b - 1) for a in range(17) for b in range(1, 16)])
    from_left = np.stack([
        hot(272, 2 * LEFT, [
            (a * 16, t * LEFT + 2 * a + par) for a in range(17 - par)
        ])
        for t in range(2) for par in range(2)
    ])
    back = hot(272, 256, [(a * 16 + b, a * 16 + b + 1) for a in range(16) for b in range(15)])
    below = np.stack([hot(16, 512, [(b, halo_row(b, t, 6)) for b in range(16)]) for t in range(2)])
    beside = np.stack([
        hot(272, 512, [(a * 16 + 15, halo_row(16 + a, t, 6)) for a in range(16)]
            + [(256 + b, halo_row(b + 1, t, 6)) for b in range(15)] + [(271, halo_row(9, t, 7))])
        for t in range(2)
    ])
    return body, sides, edges, left, first_col, shift, from_left, back, below, beside


def dot(a, b):
    return jnp.dot(a, b, preferred_element_type=F32)


def dot_t(a, b):
    return lax.dot_general(a, b, (((1,), (1,)), ((), ())), preferred_element_type=F32)


def exchange_kernel(send1, w1, w2, halo_out, w1_out, w2_out,
                    recv1, send2, recv2, s1, r1, s2, r2, ws, wr, fs, fr, ls):
    s = lax.axis_index("scene")
    r = lax.axis_index("region")
    sib = s + 1 - 2 * (s % 2)

    barrier = pltpu.get_barrier_semaphore()

    def greet(o, carry):
        pl.semaphore_signal(barrier, inc=1, device_id={"region": (r + o) % REG}, device_id_type=MESH)
        return carry

    lax.fori_loop(1, REG, greet, 0)
    for o in range(1, 4):
        pl.semaphore_signal(barrier, inc=1, device_id={"scene": (s + 2 * o) % SC}, device_id_type=MESH)
    pl.semaphore_signal(barrier, inc=1, device_id={"scene": sib}, device_id_type=MESH)
    pl.semaphore_wait(barrier, REG - 1 + 4)

    def first(o, carry):
        to = (r + o) % REG
        pltpu.make_async_remote_copy(
            src_ref=send1.at[to], dst_ref=recv1.at[r], send_sem=s1, recv_sem=r1,
            device_id={"region": to}, device_id_type=MESH).start()
        return carry

    lax.fori_loop(1, REG, first, 0)
    weights = ((w1, w1_out), (w2, w2_out))
    far = []
    near = []
    own = []
    for n, (src, dst) in enumerate(weights):
        for o in range(1, 4):
            far.append(pltpu.make_async_remote_copy(
                src_ref=src, dst_ref=dst.at[s], send_sem=ws.at[n, o - 1], recv_sem=wr.at[n, o - 1],
                device_id={"scene": (s + 2 * o) % SC}, device_id_type=MESH))
        near.append(pltpu.make_async_remote_copy(
            src_ref=src, dst_ref=dst.at[s], send_sem=fs.at[n, 0], recv_sem=fr.at[n, 0],
            device_id={"scene": sib}, device_id_type=MESH))
        own.append(pltpu.make_async_copy(src, dst.at[s], ls.at[n]))
    for copy in far + near + own:
        copy.start()

    recv1[r] = send1[r]
    pltpu.make_async_copy(recv1.at[pl.ds(0, REG - 1)], recv1.at[pl.ds(0, REG - 1)], r1).wait()

    held = recv1[...].reshape(512, 384)
    pixels = held[:, :256]
    pos = held[:, 256:].astype(F32)
    lane = lax.broadcasted_iota(jnp.int32, (512, 128), 1).astype(F32)
    q = lax.broadcasted_iota(jnp.int32, (512, 128), 0) % 8
    zero = jnp.zeros((512, 128), F32)
    k = zero.astype(jnp.int32) + r
    grad_row = jnp.where(k < 16, 1.0, 0.0)
    corner_row = jnp.where(k < 6, -1.0, 1.0)
    corner_col = jnp.where((k < 4) | (k == 6) | (k == 7), -1.0, 1.0)
    d_row = jnp.where(q < 2, -1.0, jnp.where(q == 4, 1.0, zero))
    d_row = jnp.where(q == 6, grad_row, jnp.where(q == 7, corner_row, d_row))
    d_col = jnp.where((q == 2) | (q == 3), -1.0, jnp.where(q == 5, 1.0, zero))
    d_col = jnp.where(q == 6, 1.0 - grad_row, jnp.where(q == 7, corner_col, d_col))
    p_row = jnp.floor(pos * 0.25)
    n_row = p_row + d_row
    n_col = pos - 4.0 * p_row + d_col
    inside = (n_row >= 0.0) & (n_row < GH) & (n_col >= 0.0) & (n_col < GW)
    want = jnp.where(inside, 4.0 * n_row + n_col, -1.0)
    has = jnp.where(pos == lane, 1.0, 0.0).astype(BF)
    wants = jnp.where(want == lane, 1.0, 0.0).astype(BF)
    same = (lax.broadcasted_iota(jnp.int32, (512, 512), 0) % 8) == (
        lax.broadcasted_iota(jnp.int32, (512, 512), 1) % 8)
    route = jnp.where(same, dot_t(wants, has), 0.0).astype(BF)
    send2[...] = dot(route, pixels).astype(BF).reshape(REG, 16, 256)

    def second(o, carry):
        to = (r + o) % REG
        pltpu.make_async_remote_copy(
            src_ref=send2.at[to], dst_ref=recv2.at[r], send_sem=s2, recv_sem=r2,
            device_id={"region": to}, device_id_type=MESH).start()
        return carry

    lax.fori_loop(1, REG, second, 0)
    recv2[r] = send2[r]

    forward = []
    for o in range(1, 4):
        came = (s - 2 * o + SC) % SC
        for n, (src, dst) in enumerate(weights):
            far[3 * n + o - 1].wait_recv()
            copy = pltpu.make_async_remote_copy(
                src_ref=dst.at[came], dst_ref=dst.at[came], send_sem=fs.at[n, o], recv_sem=fr.at[n, o],
                device_id={"scene": sib}, device_id_type=MESH)
            copy.start()
            forward.append(copy)
    pltpu.make_async_copy(recv2.at[pl.ds(0, REG - 1)], recv2.at[pl.ds(0, REG - 1)], r2).wait()
    halo_out[...] = recv2[...]
    for copy in near + forward:
        copy.wait_recv()
    for copy in own:
        copy.wait()
    for copy in far + near + forward:
        copy.wait_send()
    pltpu.make_async_copy(send1.at[pl.ds(0, REG - 1)], send1.at[pl.ds(0, REG - 1)], s1).wait()
    pltpu.make_async_copy(send2.at[pl.ds(0, REG - 1)], send2.at[pl.ds(0, REG - 1)], s2).wait()


def exchange(send1, w1, w2):
    vmem = pl.BlockSpec(memory_space=pltpu.VMEM)
    anywhere = pl.BlockSpec(memory_space=pl.ANY)
    full = jax.ShapeDtypeStruct((SC, WROWS, C), BF)
    return pl.pallas_call(
        exchange_kernel,
        name="exchange",
        out_shape=(jax.ShapeDtypeStruct((REG, 16, C), BF), full, full),
        in_specs=[vmem, anywhere, anywhere],
        out_specs=(vmem, anywhere, anywhere),
        scratch_shapes=[
            pltpu.VMEM((REG, 16, 384), BF),
            pltpu.VMEM((REG, 16, C), BF),
            pltpu.VMEM((REG, 16, C), BF),
            pltpu.SemaphoreType.DMA, pltpu.SemaphoreType.DMA,
            pltpu.SemaphoreType.DMA, pltpu.SemaphoreType.DMA,
            pltpu.SemaphoreType.DMA((2, 3)), pltpu.SemaphoreType.DMA((2, 3)),
            pltpu.SemaphoreType.DMA((2, 4)), pltpu.SemaphoreType.DMA((2, 4)),
            pltpu.SemaphoreType.DMA((2,)),
        ],
        compiler_params=pltpu.CompilerParams(
            collective_id=0, has_side_effects=True, vmem_limit_bytes=VMEM_LIMIT),
    )(send1, w1, w2)


def sigmoid(v):
    return 1.0 / (1.0 + jnp.exp(-v))


def compute_kernel(pos, tiles, masked, halo, w1, w2, body, sides, edges, left, first_col, shift,
                   from_left, back, below, beside, feat, grads,
                   x4, h_odd, h_even, left_x, grad_t, g_both):
    halo_px = halo[...].reshape(512, C)
    for t in range(2):
        for c in range(4):
            chunk = tiles[t, 8 * c:8 * c + 8].reshape(256, C)
            got = dot(body[...], chunk) + dot(sides[t], halo[8 * c:8 * c + 8].reshape(128, C))
            got = got.astype(BF)
            for blk in range(4):
                x4[t, 4 * c + 1:4 * c + 5, :, :, blk * C:(blk + 1) * C] = (
                    got[blk * 128:(blk + 1) * 128].reshape(4, 2, 16, C))
        rim = dot(edges[t], halo_px).astype(BF)
        for sel, (pair, par) in enumerate(((0, 0), (0, 1), (17, 0))):
            for blk in range(4):
                start = sel * 64 + blk * 16
                x4[t, pair, par, :, blk * C:(blk + 1) * C] = rim[start:start + 16]
        side = dot(left[t], halo_px)
        inner = dot(first_col[...], tiles[t].reshape(1024, C))
        for i in range(3):
            for j in range(3):
                tap = 3 * i + j
                part = side[tap * LEFT:(tap + 1) * LEFT]
                if j == 2:
                    part = part + inner[i * LEFT:(i + 1) * LEFT]
                left_x[t * LEFT:(t + 1) * LEFT, tap * C:(tap + 1) * C] = part.astype(BF)

    pre_left = dot(left_x[...], w1[...])
    row_id = lax.broadcasted_iota(jnp.int32, (LEFT, C), 0)
    kept = []
    above = []
    for t in range(2):
        here = pos[0, t]
        has_left = jnp.where(here % GW > 0, 1.0, 0.0)
        has_above = jnp.where(here >= GW, 1.0, 0.0)
        above.append(has_above)
        v = pre_left[t * LEFT:(t + 1) * LEFT]
        keep = jnp.where(row_id == 0, has_left * has_above, has_left)
        kept.append((v * sigmoid(v) * keep).astype(BF))
    hidden_left = jnp.concatenate(kept, axis=0)

    m_t = jnp.concatenate(
        [masked[t].reshape(256, C).astype(F32).T.astype(BF) for t in range(2)], axis=1)

    def window(t, par, i, cp, lo):
        row = 2 * lo + par + i
        n = 17 if (par == 0 and lo == 0) else 16
        return x4[t, row // 2:row // 2 + n, row % 2, :, cp * C:cp * C + 768].reshape(n * 16, 768)

    for t in range(2):
        m0 = masked[t].reshape(256, C)
        m0 = jnp.concatenate([m0, dot(below[t], halo_px).astype(BF)], axis=0)
        m1 = (dot(back[...], m0[:256]) + dot(beside[t], halo_px)).astype(BF)

        def second(tap):
            return w2[tap * C:(tap + 1) * C, :]

        up, down = slice(0, 256), slice(16, 272)
        spread = {
            (1, 0): lambda: dot_t(m0[up], second(4)),
            (1, 1): lambda: dot_t(m0[up], second(5)) + dot_t(m1[up], second(3)),
            (0, 0): lambda: dot_t(m0[up], second(7)) + dot_t(m0[down], second(1)),
            (0, 1): lambda: (dot_t(m0[up], second(8)) + dot_t(m1[up], second(6))
                             + dot_t(m0[down], second(2)) + dot_t(m1[down], second(0))),
        }
        for par in range(2):
            store = h_odd if par == 0 else h_even
            n = 17 - par
            for cp in range(2):
                patch = jnp.concatenate([window(t, par, i, cp, 0) for i in range(3)], axis=1)
                pre = dot(patch, w1[...])
                sig = sigmoid(pre)
                act = pre * sig
                if par == 0:
                    own_row = lax.broadcasted_iota(jnp.int32, (272, C), 0) >= 16
                    act = jnp.where(own_row, act, act * above[t])
                act = act.astype(BF)
                if cp == 0:
                    store[t, :, :, C:2 * C] = act.reshape(n, 16, C)
                else:
                    store[t, :, :, 2 * C:] = act.reshape(n, 16, C)
                    moved = dot(shift[:n * 16, :n * 16], act)
                    moved = moved + dot(from_left[2 * t + par][:n * 16], hidden_left)
                    store[t, :, :, :C] = moved.astype(BF).reshape(n, 16, C)
                if par == 0:
                    pre, sig = pre[16:], sig[16:]
                slope = sig * (1.0 + pre * (1.0 - sig))
                d_pre = spread[par, cp]() * slope
                group = 4 * t + 2 * par + cp
                grad_t[:, group * 256:(group + 1) * 256] = d_pre.T.astype(BF)

    def hidden_rows(t, i):
        if i == 1:
            return h_even[t].reshape(256, 768)
        return h_odd[t, i // 2:i // 2 + 16].reshape(256, 768)

    for t in range(2):
        patch = jnp.concatenate([hidden_rows(t, i) for i in range(3)], axis=1)
        feat[t] = dot(patch, w2[...]).astype(BF).reshape(16, 16, C)

    def own_rows(t, par, i, cp, j):
        row = (2 if par == 0 else 1) + i
        lanes = (cp + j) * C
        return x4[t, row // 2:row // 2 + 16, row % 2, :, lanes:lanes + C].reshape(256, C)

    for i in range(3):
        for j in range(3):
            tap = 3 * i + j
            seen = jnp.concatenate([hidden_rows(t, i)[:, j * C:(j + 1) * C] for t in range(2)], axis=0)
            g_both[1, tap * C:(tap + 1) * C, :] = dot(m_t, seen).T
            seen = jnp.concatenate(
                [own_rows(t, par, i, cp, j) for t in range(2) for par in range(2) for cp in range(2)], axis=0)
            g_both[0, tap * C:(tap + 1) * C, :] = dot(grad_t[...], seen).T

    for y in range(YN):
        for z in range(ZN):
            start = 72 * (z * YN + y)
            both = jnp.concatenate([g_both[0, start:start + 72, :], g_both[1, start:start + 72, :]], axis=0)
            grads[y, z] = both.astype(BF)


def compute(pos, tiles, masked, halo, w1, w2):
    tables = place_tables()
    vmem = pl.BlockSpec(memory_space=pltpu.VMEM)
    return pl.pallas_call(
        compute_kernel,
        name="compute",
        out_shape=(jax.ShapeDtypeStruct((2, 16, 16, C), BF), jax.ShapeDtypeStruct((YN, ZN, 144, C), BF)),
        in_specs=[pl.BlockSpec(memory_space=pltpu.SMEM)] + [vmem] * 15,
        out_specs=(vmem, vmem),
        scratch_shapes=[
            pltpu.VMEM((2, 18, 2, 16, 4 * C), BF),
            pltpu.VMEM((2, 17, 16, 3 * C), BF),
            pltpu.VMEM((2, 16, 16, 3 * C), BF),
            pltpu.VMEM((2 * LEFT, 9 * C), BF),
            pltpu.VMEM((C, 2048), BF),
            pltpu.VMEM((2, 9 * C, C), F32),
        ],
        compiler_params=pltpu.CompilerParams(vmem_limit_bytes=VMEM_LIMIT),
    )(pos, tiles, masked, halo, w1, w2, *[jnp.asarray(table) for table in tables])


Z_ORDER = (4, 3, 5, 2, 6, 1, 7, 0)


def reduce_kernel(g, out, y_buf, z_send, z_buf, n_send, n_buf, x_send, x_buf,
                  ys, yr, zs, zr, ns, nr, xs, xr):
    s = lax.axis_index("scene")
    r = lax.axis_index("region")
    z, y = r // YN, r % YN

    def at_y(o):
        return {"region": z * YN + (y + o) % YN}

    def at_z(o):
        return {"region": ((z + o) % ZN) * YN + y}

    barrier = pltpu.get_barrier_semaphore()
    for o in range(1, YN):
        pl.semaphore_signal(barrier, inc=1, device_id=at_y(o), device_id_type=MESH)
    for o in range(1, ZN):
        pl.semaphore_signal(barrier, inc=1, device_id=at_z(o), device_id_type=MESH)
    for o in range(1, SC):
        pl.semaphore_signal(barrier, inc=1, device_id={"scene": (s + o) % SC}, device_id_type=MESH)
    pl.semaphore_wait(barrier, YN + ZN + SC - 3)

    y_copies = {}
    for oz in Z_ORDER:
        zz = (z + oz) % ZN
        for o in range(1, YN):
            copy = pltpu.make_async_remote_copy(
                src_ref=g.at[(y + o) % YN, zz], dst_ref=y_buf.at[o - 1, oz],
                send_sem=ys.at[o - 1, oz], recv_sem=yr.at[o - 1, oz],
                device_id=at_y(o), device_id_type=MESH)
            copy.start()
            y_copies[o, oz] = copy
    z_copies = []
    for oz in Z_ORDER:
        zz = (z + oz) % ZN
        total = g[y, zz].astype(F32)
        for o in range(1, YN):
            y_copies[o, oz].wait_recv()
            total = total + y_buf[o - 1, oz].astype(F32)
        if oz:
            z_send[oz - 1] = total.astype(BF)
            copy = pltpu.make_async_remote_copy(
                src_ref=z_send.at[oz - 1], dst_ref=z_buf.at[oz - 1],
                send_sem=zs.at[oz - 1], recv_sem=zr.at[oz - 1],
                device_id=at_z(oz), device_id_type=MESH)
            copy.start()
            z_copies.append(copy)
    for n, copy in enumerate(z_copies):
        copy.wait_recv()
        total = total + z_buf[Z_ORDER[n] - 1].astype(F32)

    squares = jnp.sum((total * total).reshape(18, 8, C), axis=0)
    n_send[0] = squares[:, :128] + squares[:, 128:]
    n_copies = []
    for o in range(1, YN):
        copy = pltpu.make_async_remote_copy(
            src_ref=n_send.at[0], dst_ref=n_buf.at[o - 1], send_sem=ns.at[o - 1], recv_sem=nr.at[o - 1],
            device_id=at_y(o), device_id_type=MESH)
        copy.start()
        n_copies.append(copy)
    turned = total.T
    part = n_send[0]
    for o in range(1, YN):
        n_copies[o - 1].wait_recv()
        part = part + n_buf[o - 1]
    n_send[1] = part
    for o in range(1, ZN):
        copy = pltpu.make_async_remote_copy(
            src_ref=n_send.at[1], dst_ref=n_buf.at[o + 2], send_sem=ns.at[o + 2], recv_sem=nr.at[o + 2],
            device_id=at_z(o), device_id_type=MESH)
        copy.start()
        n_copies.append(copy)
    for o in range(1, ZN):
        n_copies[o + 2].wait_recv()
        part = part + n_buf[o + 2]
    sum_sq = jnp.sum(part, keepdims=True)
    factor = (3.0 * C * math.sqrt(2.0) / SC) / (jnp.sqrt(sum_sq) + 0.01)
    x_send[...] = (turned * factor).reshape(SC, 32, 144)
    x_copies = []
    for o in range(1, SC):
        to = (s + o) % SC
        copy = pltpu.make_async_remote_copy(
            src_ref=x_send.at[to], dst_ref=x_buf.at[o - 1], send_sem=xs.at[o - 1], recv_sem=xr.at[o - 1],
            device_id={"scene": to}, device_id_type=MESH)
        copy.start()
        x_copies.append(copy)
    result = x_send[s]
    for o in range(1, SC):
        x_copies[o - 1].wait_recv()
        result = result + x_buf[o - 1]
    out[...] = result
    for copy in list(y_copies.values()) + z_copies + n_copies + x_copies:
        copy.wait_send()


def reduce(g):
    vmem = pl.BlockSpec(memory_space=pltpu.VMEM)
    dma = pltpu.SemaphoreType.DMA
    return pl.pallas_call(
        reduce_kernel,
        name="reduce",
        out_shape=jax.ShapeDtypeStruct((32, 144), F32),
        in_specs=[vmem],
        out_specs=vmem,
        scratch_shapes=[
            pltpu.VMEM((YN - 1, ZN, 144, C), BF),
            pltpu.VMEM((ZN - 1, 144, C), BF),
            pltpu.VMEM((ZN - 1, 144, C), BF),
            pltpu.VMEM((2, 8, 128), F32),
            pltpu.VMEM((YN + ZN - 2, 8, 128), F32),
            pltpu.VMEM((SC, 32, 144), F32),
            pltpu.VMEM((SC - 1, 32, 144), F32),
            dma((YN - 1, ZN)), dma((YN - 1, ZN)), dma((ZN - 1,)), dma((ZN - 1,)),
            dma((YN + ZN - 2,)), dma((YN + ZN - 2,)), dma((SC - 1,)), dma((SC - 1,)),
        ],
        compiler_params=pltpu.CompilerParams(
            collective_id=1, has_side_effects=True, vmem_limit_bytes=VMEM_LIMIT),
    )(g)


def local(tiles, cotangent, positions, clear, w_first, w_second):
    tiles_here = tiles[0]
    masked = cotangent[0] * clear[0].astype(BF)[:, None, None, None]
    grad_px = jnp.concatenate([masked[:, 0], masked[:, :, 0]], axis=1)
    corner = jnp.concatenate([
        tiles_here[:, 30:32, 30:32].reshape(2, 4, C),
        tiles_here[:, 30:32, 0],
        tiles_here[:, 0, 30:32],
        tiles_here[:, 0, 0:1],
        masked[:, 0, 0:1],
        jnp.zeros((2, 22, C), BF),
    ], axis=1)
    rims = jnp.stack([
        tiles_here[:, 31], tiles_here[:, 30], tiles_here[:, :, 31], tiles_here[:, :, 30],
        tiles_here[:, 0], tiles_here[:, :, 0], grad_px, corner,
    ], axis=2)
    rims = rims.transpose(1, 0, 2, 3).reshape(REG, 16, C)
    where = jnp.broadcast_to(positions[0].astype(BF)[None, :, None, None], (REG, 2, 8, 128))
    send1 = jnp.concatenate([rims, where.reshape(REG, 16, 128)], axis=2)
    halo, w1, w2 = exchange(send1, w_first, w_second)
    feat, grads = compute(
        positions, tiles_here, masked, halo, w1.reshape(9 * C, C), w2.reshape(9 * C, C))
    out = reduce(grads)
    return feat[None], out[:, :72].T, out[:, 72:].T


def solution(mesh):
    in_specs = (
        P("scene", "region", None, None, None),
        P("scene", "region", None, None, None),
        P("scene", "region"),
        P("scene", "region"),
        P("scene", None),
        P("scene", None),
    )
    out_specs = (P("scene", "region", None, None, None), P("region", "scene"), P("region", "scene"))
    return jax.shard_map(local, mesh=mesh, in_specs=in_specs, out_specs=out_specs, check_vma=False)
```

```python
import math

import jax
import jax.numpy as jnp
import ml_dtypes
import numpy as np
from jax import lax
from jax.experimental import pallas as pl
from jax.experimental.pallas import tpu as pltpu
from jax.sharding import PartitionSpec as P

MESH = pl.DeviceIdType.MESH
BF = jnp.bfloat16
F32 = jnp.float32
GW, GH = 4, 16
C = 256
REG, ZN, YN, SC = 32, 8, 4, 8
WROWS = 288
LEFT = 48
ROWS = 9 * C
OWN_ROWS = ROWS // REG
VMEM_LIMIT = 56 * 1024 * 1024


def hot(rows, cols, pairs):
    out = np.zeros((rows, cols), np.float32)
    for row, col in pairs:
        out[row, col] = 1.0
    return out.astype(ml_dtypes.bfloat16)


def place_tables():
    tile = lambda h, w: 32 * h + w
    corner = ((30, 30), (30, 31), (31, 30), (31, 31), (30, 0), (31, 0), (0, 30), (0, 31), (0, 0))
    rim = hot(256, 1024, [
        (8 * k + q, px) for k in range(32) for q, px in enumerate((
            tile(31, k), tile(30, k), tile(k, 31), tile(k, 30), tile(0, k), tile(k, 0)))
    ] + [(8 * k + 7, tile(*at)) for k, at in enumerate(corner)])
    rim_grad = hot(256, 256, [(8 * k + 6, k if k < 16 else 16 * (k - 16)) for k in range(32)] + [(79, 0)])

    cols = lambda blk, b: 2 * b - 1 + blk
    order = (1, 2, 0, 3)
    body = hot(512, 256, [
        (at * 128 + h * 16 + b, h * 32 + cols(blk, b))
        for at, blk in enumerate(order) for h in range(8) for b in range(16) if 0 <= cols(blk, b) < 32
    ])
    sides = hot(256, 64, [(h * 16, 8 * h + 2) for h in range(8)]
                + [(128 + h * 16 + 15, 8 * h + 5) for h in range(8)])
    edge_q = (1, 0, 4)
    corner_left, corner_right = (1, 3, 7), (4, 5, 8)

    def edge_source(sel, col):
        if col < 0:
            return 8 * corner_left[sel] + 7
        if col > 31:
            return 8 * corner_right[sel] + 7
        return 8 * col + edge_q[sel]

    edges = hot(192, 256, [
        (sel * 64 + blk * 16 + b, edge_source(sel, cols(blk, b)))
        for sel in range(3) for blk in range(4) for b in range(16)
    ])

    def left_source(hh, j):
        if 0 <= hh < 32:
            return 8 * hh + (3, 2)[j] if j < 2 else None
        sel = {-2: 0, -1: 1, 32: 2}[hh]
        if j < 2:
            return 8 * ((0, 1), (2, 3), (6, 7))[sel][j] + 7
        return edge_q[sel]

    left = hot(9 * LEFT, 256, [
        ((3 * i + j) * LEFT + g, left_source(g + i - 2, j))
        for i in range(3) for j in range(3) for g in range(33)
        if left_source(g + i - 2, j) is not None
    ])
    first_col = hot(3 * LEFT, 256, [
        (i * LEFT + g, 8 * (g + i - 2) + 5) for i in range(3) for g in range(33) if 0 <= g + i - 2 < 32
    ])
    shift = hot(272, 272, [(a * 16 + b, a * 16 + b - 1) for a in range(17) for b in range(1, 16)])
    from_left = np.stack([
        hot(272, LEFT, [(a * 16, 2 * a + par) for a in range(17 - par)]) for par in range(2)
    ])
    back = hot(272, 256, [(a * 16 + b, a * 16 + b + 1) for a in range(16) for b in range(15)])
    below = hot(16, 256, [(b, 8 * b + 6) for b in range(16)])
    beside = hot(272, 256, [(a * 16 + 15, 8 * (16 + a) + 6) for a in range(16)]
                 + [(256 + b, 8 * (b + 1) + 6) for b in range(15)] + [(271, 79)])
    return rim, rim_grad, body, sides, edges, left, first_col, shift, from_left, back, below, beside


def dot(a, b):
    return jnp.dot(a, b, preferred_element_type=F32)


def dot_t(a, b):
    return lax.dot_general(a, b, (((1,), (1,)), ((), ())), preferred_element_type=F32)


def sigmoid(v):
    return 1.0 / (1.0 + jnp.exp(-v))


def route_rows(pos, r):
    lane = lax.broadcasted_iota(jnp.int32, (512, 128), 1).astype(F32)
    q = lax.broadcasted_iota(jnp.int32, (512, 128), 0) % 8
    zero = jnp.zeros((512, 128), F32)
    k = zero.astype(jnp.int32) + r
    grad_row = jnp.where(k < 16, 1.0, 0.0)
    corner_row = jnp.where(k < 6, -1.0, 1.0)
    corner_col = jnp.where((k < 4) | (k == 6) | (k == 7), -1.0, 1.0)
    d_row = jnp.where(q < 2, -1.0, jnp.where(q == 4, 1.0, zero))
    d_row = jnp.where(q == 6, grad_row, jnp.where(q == 7, corner_row, d_row))
    d_col = jnp.where((q == 2) | (q == 3), -1.0, jnp.where(q == 5, 1.0, zero))
    d_col = jnp.where(q == 6, 1.0 - grad_row, jnp.where(q == 7, corner_col, d_col))
    p_row = jnp.floor(pos * 0.25)
    n_row = p_row + d_row
    n_col = pos - 4.0 * p_row + d_col
    inside = (n_row >= 0.0) & (n_row < GH) & (n_col >= 0.0) & (n_col < GW)
    want = jnp.where(inside, 4.0 * n_row + n_col, -1.0)
    has = jnp.where(pos == lane, 1.0, 0.0).astype(BF)
    wants = jnp.where(want == lane, 1.0, 0.0).astype(BF)
    same = (lax.broadcasted_iota(jnp.int32, (512, 512), 0) % 8) == (
        lax.broadcasted_iota(jnp.int32, (512, 512), 1) % 8)
    return jnp.where(same, dot_t(wants, has), 0.0).astype(BF)


Z_ORDER = (4, 3, 5, 2, 6, 1, 7, 0)


def level_kernel(positions, clear, tiles, cotangent, w1_here, w2_here, *refs):
    names = list(TABLES)
    table_hbm = dict(zip(names, refs[:len(names)]))
    feat, out = refs[len(names):len(names) + 2]
    refs = refs[len(names) + 2:]
    table = dict(zip(names, refs[:len(names)]))
    (table_sem, pos_send, pos_buf, send1, recv1, send2, recv2, masked, own_rim, halo, w1, w2,
     x4, h_odd, h_even, left_x, slopes, grad_t, g_f, g, f_buf, o_buf, s_buf, s_send, z_send, z_buf,
     n_send, n_buf, x_send, x_buf, c_send, c_buf,
     a2a_s, a2a_r, w_s, w_r, v_s, v_r, y_s, y_r, zs, zr, xs, xr, cs, cr, own_sem) = refs[len(names):]

    s = lax.axis_index("scene")
    r = lax.axis_index("region")
    z, y = r // YN, r % YN
    sib = s + 1 - 2 * (s % 2)

    loads = {name: pltpu.make_async_copy(table_hbm[name], table[name], table_sem.at[n])
             for n, name in enumerate(names)}
    for name in names:
        loads[name].start()

    barrier = pltpu.get_barrier_semaphore()

    def greet(o, carry):
        pl.semaphore_signal(barrier, inc=1, device_id={"region": (r + o) % REG}, device_id_type=MESH)
        return carry

    lax.fori_loop(1, REG, greet, 0)
    for o in range(1, SC):
        pl.semaphore_signal(barrier, inc=1, device_id={"scene": (s + o) % SC}, device_id_type=MESH)

    def w_rows(ref, who):
        return ref.at[pl.ds(pl.multiple_of(who * WROWS, 32), WROWS)]

    weights = ((w1_here, w1), (w2_here, w2))
    own = [pltpu.make_async_copy(src, w_rows(dst, s), own_sem.at[n]) for n, (src, dst) in enumerate(weights)]
    for copy in own:
        copy.start()

    def all_to_all(n, src, dst):
        def send(o, carry):
            to = (r + o) % REG
            pltpu.make_async_remote_copy(
                src_ref=src(to), dst_ref=dst(r), send_sem=a2a_s.at[n], recv_sem=a2a_r.at[n],
                device_id={"region": to}, device_id_type=MESH).start()
            return carry

        lax.fori_loop(1, REG, send, 0)

    def await_all(buf, sem):
        pltpu.make_async_copy(buf, buf, sem).wait()

    own_pos = [positions[0:1, t:t + 1].astype(F32) for t in range(2)]
    for t in range(2):
        pos_send[t] = jnp.broadcast_to(own_pos[t], (1, 128))
        kept = clear[0:1, t:t + 1].astype(F32)
        masked[t] = (cotangent[t].reshape(256, C).astype(F32) * kept).astype(BF)
    pl.semaphore_wait(barrier, REG - 1 + SC - 1)

    right, left_chip = (s + 2) % SC, (s + 6) % SC

    def to_scene(src, dst, send_sem, recv_sem, who):
        copy = pltpu.make_async_remote_copy(
            src_ref=src, dst_ref=dst, send_sem=send_sem, recv_sem=recv_sem,
            device_id={"scene": who}, device_id_type=MESH)
        copy.start()
        return copy

    all_to_all(0, lambda to: pos_send, lambda me: pos_buf.at[pl.ds(2 * me, 2)])
    far, near = [], []
    for n, (src, dst) in enumerate(weights):
        far.append(to_scene(src, w_rows(dst, s), w_s.at[n, 0], w_r.at[n, 0], right))
        far.append(to_scene(src, w_rows(dst, s), w_s.at[n, 1], w_r.at[n, 1], left_chip))
        near.append([to_scene(src, w_rows(dst, s), v_s.at[n, 0], v_r.at[n, 0], sib)])

    loads["rim"].wait()
    loads["rim_grad"].wait()
    rims = []
    for t in range(2):
        rim = dot(table["rim"][...], tiles[t].reshape(1024, C)) + dot(table["rim_grad"][...], masked[t])
        own_rim[t] = rim.astype(BF)
        rims.append(rim.reshape(REG, 8, C))
    send1[...] = jnp.concatenate(rims, axis=1).astype(BF)
    all_to_all(1, lambda to: send1.at[to], lambda me: recv1.at[me])
    recv1[r] = send1[r]
    for t in range(2):
        pos_buf[2 * r + t] = pos_send[t]

    loads["body"].wait()
    for t in range(2):
        for c in range(4):
            chunk = tiles[t, 8 * c:8 * c + 8].reshape(256, C)
            got = dot(table["body"][:256], chunk).astype(BF)
            for at, blk in enumerate((1, 2)):
                x4[t, 4 * c + 1:4 * c + 5, :, :, blk * C:(blk + 1) * C] = (
                    got[at * 128:(at + 1) * 128].reshape(4, 2, 16, C))

    await_all(pos_buf.at[pl.ds(0, 2 * REG - 2)], a2a_r.at[0])
    route = route_rows(jnp.broadcast_to(pos_buf[...], (64, 8, 128)).reshape(512, 128), r)

    def forward(n, came, at):
        rows = w_rows(weights[n][1], came)
        return to_scene(rows, rows, v_s.at[n, at], v_r.at[n, at], sib)

    far[0].wait_recv()
    rows = w_rows(w1, left_chip)
    far.append(to_scene(rows, rows, w_s.at[0, 2], w_r.at[0, 2], right))
    near[0].append(forward(0, left_chip, 1))
    far[1].wait_recv()
    near[0].append(forward(0, right, 2))

    await_all(recv1.at[pl.ds(0, REG - 1)], a2a_r.at[1])
    send2[...] = dot(route, recv1[...].reshape(512, C)).astype(BF).reshape(REG, 16, C)
    all_to_all(2, lambda to: send2.at[to], lambda me: recv2.at[me])
    recv2[r] = send2[r]

    far[2].wait_recv()
    near[1].append(forward(1, left_chip, 1))
    far[3].wait_recv()
    rows = w_rows(w2, right)
    far.append(to_scene(rows, rows, w_s.at[1, 2], w_r.at[1, 2], left_chip))
    near[1].append(forward(1, right, 2))
    opposite = (s + 4) % SC
    far[4].wait_recv()
    near[0].append(forward(0, opposite, 3))

    m_t = jnp.concatenate([masked[t].astype(F32).T.astype(BF) for t in range(2)], axis=1)
    for name in names[3:]:
        loads[name].wait()
    far[5].wait_recv()
    near[1].append(forward(1, opposite, 3))
    await_all(recv2.at[pl.ds(0, REG - 1)], a2a_r.at[2])

    came = recv2[...].astype(F32)
    for t in range(2):
        halo[t] = came[:, 8 * t:8 * t + 8].reshape(256, C).astype(BF)
    for t in range(2):
        for c in range(4):
            chunk = tiles[t, 8 * c:8 * c + 8].reshape(256, C)
            got = dot(table["body"][256:], chunk) + dot(table["sides"][...], halo[t, 64 * c:64 * c + 64])
            got = got.astype(BF)
            for at, blk in enumerate((0, 3)):
                x4[t, 4 * c + 1:4 * c + 5, :, :, blk * C:(blk + 1) * C] = (
                    got[at * 128:(at + 1) * 128].reshape(4, 2, 16, C))
        rim = dot(table["edges"][...], halo[t]).astype(BF)
        for sel, (pair, par) in enumerate(((0, 0), (0, 1), (17, 0))):
            for blk in range(4):
                start = sel * 64 + blk * 16
                x4[t, pair, par, :, blk * C:(blk + 1) * C] = rim[start:start + 16]
        side = dot(table["left"][...], halo[t])
        inner = dot(table["first_col"][...], own_rim[t])
        for i in range(3):
            for j in range(3):
                tap = 3 * i + j
                part = side[tap * LEFT:(tap + 1) * LEFT]
                if j == 2:
                    part = part + inner[i * LEFT:(i + 1) * LEFT]
                left_x[t * LEFT:(t + 1) * LEFT, tap * C:(tap + 1) * C] = part.astype(BF)

    own[0].wait()
    for copy in near[0]:
        copy.wait_recv()

    pre_left = dot(left_x[...], w1[...])
    row_id = lax.broadcasted_iota(jnp.int32, (LEFT, C), 0)
    hidden_left, above = [], []
    for t in range(2):
        p_row = jnp.floor(own_pos[t] * 0.25)
        has_left = jnp.where(own_pos[t] - 4.0 * p_row > 0.0, 1.0, 0.0)
        has_above = jnp.where(p_row > 0.0, 1.0, 0.0)
        above.append(has_above)
        v = pre_left[t * LEFT:(t + 1) * LEFT]
        keep = jnp.where(row_id == 0, has_left * has_above, has_left)
        hidden_left.append((v * sigmoid(v) * keep).astype(BF))

    def window(t, par, i, cp):
        row = par + i
        n = 17 - par
        return x4[t, row // 2:row // 2 + n, row % 2, :, cp * C:cp * C + 768].reshape(n * 16, 768)

    for t in range(2):
        for par in range(2):
            store = h_odd if par == 0 else h_even
            n = 17 - par
            for cp in range(2):
                patch = jnp.concatenate([window(t, par, i, cp) for i in range(3)], axis=1)
                pre = dot(patch, w1[...])
                sig = sigmoid(pre)
                act = pre * sig
                if par == 0:
                    own_row = lax.broadcasted_iota(jnp.int32, (272, C), 0) >= 16
                    act = jnp.where(own_row, act, act * above[t])
                act = act.astype(BF)
                if cp == 0:
                    store[t, :, :, C:2 * C] = act.reshape(n, 16, C)
                else:
                    store[t, :, :, 2 * C:] = act.reshape(n, 16, C)
                    moved = dot(table["shift"][:n * 16, :n * 16], act)
                    moved = moved + dot(table["from_left"][par, :n * 16], hidden_left[t])
                    store[t, :, :, :C] = moved.astype(BF).reshape(n, 16, C)
                if par == 0:
                    pre, sig = pre[16:], sig[16:]
                slopes[4 * t + 2 * par + cp] = sig * (1.0 + pre * (1.0 - sig))

    def hidden_rows(t, i):
        if i == 1:
            return h_even[t].reshape(256, 768)
        return h_odd[t, i // 2:i // 2 + 16].reshape(256, 768)

    def blocks(n):
        for yy in range(YN):
            for zz in range(ZN):
                start = OWN_ROWS * (zz * YN + yy)
                rows = g_f[start:start + OWN_ROWS, :]
                g[n, yy, zz] = jnp.concatenate([rows[:, :128], rows[:, 128:]], axis=0).astype(BF)

    def to_region(src, dst, send_sem, recv_sem, who):
        copy = pltpu.make_async_remote_copy(
            src_ref=src, dst_ref=dst, send_sem=send_sem, recv_sem=recv_sem,
            device_id={"region": who}, device_id_type=MESH)
        copy.start()
        return copy

    sent = []
    y_copies = {}

    def turn(oz):
        return 1 if oz % 2 == 0 else YN - 1

    def y_first(n):
        for kind in range(2):
            for oz in Z_ORDER:
                d = turn(oz)
                block = (y + 2) % YN if kind == 0 else (y + YN - d) % YN
                who = (y + d) % YN if kind == 0 else block
                buf = f_buf if kind == 0 else o_buf
                y_copies[n, kind, oz] = to_region(
                    g.at[n, block, (z + oz) % ZN], buf.at[n, oz],
                    y_s.at[kind, n, oz], y_r.at[kind, n, oz], z * YN + who)
                sent.append(y_copies[n, kind, oz])

    def y_second(n):
        for oz in Z_ORDER:
            who = (y + turn(oz)) % YN
            y_copies[n, 0, oz].wait_recv()
            summed = g[n, who, (z + oz) % ZN].astype(F32) + f_buf[n, oz].astype(F32)
            s_send[n, oz] = summed.astype(BF)
            y_copies[n, 2, oz] = to_region(
                s_send.at[n, oz], s_buf.at[n, oz], y_s.at[2, n, oz], y_r.at[2, n, oz], z * YN + who)
            sent.append(y_copies[n, 2, oz])

    def z_first(n):
        copies = []
        for oz in Z_ORDER:
            y_copies[n, 1, oz].wait_recv()
            y_copies[n, 2, oz].wait_recv()
            total = (g[n, y, (z + oz) % ZN].astype(F32) + o_buf[n, oz].astype(F32)) + s_buf[n, oz].astype(F32)
            if oz:
                z_send[n, oz - 1] = total.astype(BF)
                copies.append(to_region(
                    z_send.at[n, oz - 1], z_buf.at[n, oz - 1], zs.at[n, oz - 1], zr.at[n, oz - 1],
                    ((z + oz) % ZN) * YN + y))
        sent.extend(copies)
        return total, copies

    def z_second(n, total, copies):
        for at, copy in enumerate(copies):
            copy.wait_recv()
            total = total + z_buf[n, Z_ORDER[at] - 1].astype(F32)
        return total

    for i in range(3):
        for j in range(3):
            tap = 3 * i + j
            seen = jnp.concatenate([hidden_rows(t, i)[:, j * C:(j + 1) * C] for t in range(2)], axis=0)
            g_f[tap * C:(tap + 1) * C, :] = dot(m_t, seen).T
    blocks(1)
    y_first(1)

    own[1].wait()
    for copy in near[1]:
        copy.wait_recv()
    for t in range(2):
        patch = jnp.concatenate([hidden_rows(t, i) for i in range(3)], axis=1)
        feat[t] = dot(patch, w2[...]).astype(BF).reshape(16, 16, C)

    def second(tap):
        return w2[tap * C:(tap + 1) * C, :]

    up, down = slice(0, 256), slice(16, 272)
    for t in range(2):
        if t == 1:
            y_second(1)
        m0 = jnp.concatenate([masked[t], dot(table["below"][...], halo[t]).astype(BF)], axis=0)
        m1 = (dot(table["back"][...], masked[t]) + dot(table["beside"][...], halo[t])).astype(BF)
        spread = (
            dot_t(m0[up], second(7)) + dot_t(m0[down], second(1)),
            (dot_t(m0[up], second(8)) + dot_t(m1[up], second(6))
             + dot_t(m0[down], second(2)) + dot_t(m1[down], second(0))),
            dot_t(m0[up], second(4)),
            dot_t(m0[up], second(5)) + dot_t(m1[up], second(3)),
        )
        for n in range(4):
            group = 4 * t + n
            grad_t[:, group * 256:(group + 1) * 256] = (spread[n] * slopes[group]).T.astype(BF)

    def own_rows(t, par, i, cp, j):
        row = (2 if par == 0 else 1) + i
        lanes = (cp + j) * C
        return x4[t, row // 2:row // 2 + 16, row % 2, :, lanes:lanes + C].reshape(256, C)

    for i in range(3):
        if i == 2:
            z_second_left = z_first(1)
        for j in range(3):
            tap = 3 * i + j
            seen = jnp.concatenate(
                [own_rows(t, par, i, cp, j) for t in range(2) for par in range(2) for cp in range(2)], axis=0)
            g_f[tap * C:(tap + 1) * C, :] = dot(grad_t[...], seen).T
    blocks(0)
    y_first(0)
    y_second(0)
    total_second = z_second(1, *z_second_left)
    total_first = z_second(0, *z_first(0))

    squares = jnp.sum(total_first * total_first + total_second * total_second, axis=0, keepdims=True)
    n_send[0] = squares
    all_to_all(3, lambda to: n_send.at[0], lambda me: n_buf.at[me])
    n_buf[r] = squares
    for n, total in enumerate((total_first, total_second)):
        turned = jnp.concatenate([total[:OWN_ROWS].T, total[OWN_ROWS:].T], axis=0)
        x_send[:, n] = turned.reshape(SC, 32, OWN_ROWS)
    x_copies = []
    for o in range(1, SC):
        to = (s + o) % SC
        x_copies.append(to_scene(x_send.at[to], x_buf.at[o - 1], xs.at[o - 1], xr.at[o - 1], to))
    await_all(n_buf.at[pl.ds(0, REG - 1)], a2a_r.at[3])
    sum_sq = jnp.sum(n_buf[...].reshape(REG, 128), keepdims=True)
    factor = (3.0 * C * math.sqrt(2.0) / SC) / (jnp.sqrt(sum_sq) + 0.01)
    c_send[0] = jnp.broadcast_to(factor, (1, 128))
    c_copies = []
    for o in range(1, SC):
        to = (s + o) % SC
        c_copies.append(to_scene(c_send.at[0], c_buf.at[o - 1], cs.at[o - 1], cr.at[o - 1], to))
    result = x_send[s] * factor.reshape(1, 1, 1)
    for o in range(1, SC):
        x_copies[o - 1].wait_recv()
        c_copies[o - 1].wait_recv()
        result = result + x_buf[o - 1] * c_buf[o - 1][:, :1].reshape(1, 1, 1)
    out[...] = result

    for copy in far + near[0] + near[1] + sent + x_copies + c_copies:
        copy.wait_send()
    await_all(pos_buf.at[pl.ds(0, 2 * REG - 2)], a2a_s.at[0])
    await_all(send1.at[pl.ds(0, REG - 1)], a2a_s.at[1])
    await_all(send2.at[pl.ds(0, REG - 1)], a2a_s.at[2])
    await_all(n_buf.at[pl.ds(0, REG - 1)], a2a_s.at[3])


NAMES = ("rim", "rim_grad", "body", "sides", "edges", "left", "first_col", "shift", "from_left",
         "back", "below", "beside")
TABLES = dict(zip(NAMES, place_tables()))


def level(positions, clear, tiles, cotangent, w1, w2):
    vmem = pl.BlockSpec(memory_space=pltpu.VMEM)
    anywhere = pl.BlockSpec(memory_space=pl.ANY)
    dma = pltpu.SemaphoreType.DMA
    tables = list(TABLES.values())
    part = (144, 128)
    return pl.pallas_call(
        level_kernel,
        name="level",
        out_shape=(jax.ShapeDtypeStruct((2, 16, 16, C), BF), jax.ShapeDtypeStruct((2, 32, OWN_ROWS), F32)),
        in_specs=[vmem] * 4 + [anywhere] * (2 + len(tables)),
        out_specs=(vmem, vmem),
        scratch_shapes=[pltpu.VMEM(t.shape, BF) for t in tables] + [
            dma((len(tables),)),
            pltpu.VMEM((2, 1, 128), F32), pltpu.VMEM((2 * REG, 1, 128), F32),
            pltpu.VMEM((REG, 16, C), BF), pltpu.VMEM((REG, 16, C), BF),
            pltpu.VMEM((REG, 16, C), BF), pltpu.VMEM((REG, 16, C), BF),
            pltpu.VMEM((2, 256, C), BF), pltpu.VMEM((2, 256, C), BF), pltpu.VMEM((2, 256, C), BF),
            pltpu.VMEM((ROWS, C), BF), pltpu.VMEM((ROWS, C), BF),
            pltpu.VMEM((2, 18, 2, 16, 4 * C), BF),
            pltpu.VMEM((2, 17, 16, 3 * C), BF), pltpu.VMEM((2, 16, 16, 3 * C), BF),
            pltpu.VMEM((2 * LEFT, ROWS), BF),
            pltpu.VMEM((8, 256, C), F32),
            pltpu.VMEM((C, 2048), BF),
            pltpu.VMEM((ROWS, C), F32),
            pltpu.VMEM((2, YN, ZN) + part, BF),
            pltpu.VMEM((2, ZN) + part, BF), pltpu.VMEM((2, ZN) + part, BF),
            pltpu.VMEM((2, ZN) + part, BF), pltpu.VMEM((2, ZN) + part, BF),
            pltpu.VMEM((2, ZN - 1) + part, BF), pltpu.VMEM((2, ZN - 1) + part, BF),
            pltpu.VMEM((1, 1, 128), F32), pltpu.VMEM((REG, 1, 128), F32),
            pltpu.VMEM((SC, 2, 32, OWN_ROWS), F32), pltpu.VMEM((SC - 1, 2, 32, OWN_ROWS), F32),
            pltpu.VMEM((1, 1, 128), F32), pltpu.VMEM((SC - 1, 1, 128), F32),
            dma((4,)), dma((4,)), dma((2, 3)), dma((2, 3)), dma((2, 4)), dma((2, 4)),
            dma((3, 2, ZN)), dma((3, 2, ZN)), dma((2, ZN - 1)), dma((2, ZN - 1)),
            dma((SC - 1,)), dma((SC - 1,)), dma((SC - 1,)), dma((SC - 1,)), dma((2,)),
        ],
        compiler_params=pltpu.CompilerParams(
            collective_id=0, has_side_effects=True, vmem_limit_bytes=VMEM_LIMIT),
    )(positions, clear, tiles, cotangent, w1, w2, *[jnp.asarray(t) for t in tables])


def local(tiles, cotangent, positions, clear, w_first, w_second):
    feat, out = level(positions, clear, tiles[0], cotangent[0], w_first, w_second)
    return feat[None], out[0].T, out[1].T


def solution(mesh):
    in_specs = (
        P("scene", "region", None, None, None),
        P("scene", "region", None, None, None),
        P("scene", "region"),
        P("scene", "region"),
        P("scene", None),
        P("scene", None),
    )
    out_specs = (P("scene", "region", None, None, None), P("region", "scene"), P("region", "scene"))
    return jax.shard_map(local, mesh=mesh, in_specs=in_specs, out_specs=out_specs, check_vma=False)
```

```python
import math

import jax
import jax.numpy as jnp
import ml_dtypes
import numpy as np
from jax import lax
from jax.experimental import pallas as pl
from jax.experimental.pallas import tpu as pltpu
from jax.sharding import PartitionSpec as P

MESH = pl.DeviceIdType.MESH
BF = jnp.bfloat16
F32 = jnp.float32
GW, GH = 4, 16
C = 256
REG, ZN, YN, SC = 32, 8, 4, 8
WROWS = 288
LEFT = 48
ROWS = 9 * C
OWN_ROWS = ROWS // REG
VMEM_LIMIT = 56 * 1024 * 1024


def hot(rows, cols, pairs):
    out = np.zeros((rows, cols), np.float32)
    for row, col in pairs:
        out[row, col] = 1.0
    return out.astype(ml_dtypes.bfloat16)


def place_tables():
    tile = lambda h, w: 32 * h + w
    corner = ((30, 30), (30, 31), (31, 30), (31, 31), (30, 0), (31, 0), (0, 30), (0, 31), (0, 0))
    rim = hot(256, 1024, [
        (8 * k + q, px) for k in range(32) for q, px in enumerate((
            tile(31, k), tile(30, k), tile(k, 31), tile(k, 30), tile(0, k), tile(k, 0)))
    ] + [(8 * k + 7, tile(*at)) for k, at in enumerate(corner)])
    rim_grad = hot(256, 256, [(8 * k + 6, k if k < 16 else 16 * (k - 16)) for k in range(32)] + [(79, 0)])

    cols = lambda blk, b: 2 * b - 1 + blk
    order = (1, 2, 0, 3)
    body = hot(512, 256, [
        (at * 128 + h * 16 + b, h * 32 + cols(blk, b))
        for at, blk in enumerate(order) for h in range(8) for b in range(16) if 0 <= cols(blk, b) < 32
    ])
    sides = hot(256, 64, [(h * 16, 8 * h + 2) for h in range(8)]
                + [(128 + h * 16 + 15, 8 * h + 5) for h in range(8)])
    edge_q = (1, 0, 4)
    corner_left, corner_right = (1, 3, 7), (4, 5, 8)

    def edge_source(sel, col):
        if col < 0:
            return 8 * corner_left[sel] + 7
        if col > 31:
            return 8 * corner_right[sel] + 7
        return 8 * col + edge_q[sel]

    edges = hot(192, 256, [
        (sel * 64 + blk * 16 + b, edge_source(sel, cols(blk, b)))
        for sel in range(3) for blk in range(4) for b in range(16)
    ])

    def left_source(hh, j):
        if 0 <= hh < 32:
            return 8 * hh + (3, 2)[j] if j < 2 else None
        sel = {-2: 0, -1: 1, 32: 2}[hh]
        if j < 2:
            return 8 * ((0, 1), (2, 3), (6, 7))[sel][j] + 7
        return edge_q[sel]

    left = hot(9 * LEFT, 256, [
        ((3 * i + j) * LEFT + g, left_source(g + i - 2, j))
        for i in range(3) for j in range(3) for g in range(33)
        if left_source(g + i - 2, j) is not None
    ])
    first_col = hot(3 * LEFT, 256, [
        (i * LEFT + g, 8 * (g + i - 2) + 5) for i in range(3) for g in range(33) if 0 <= g + i - 2 < 32
    ])
    shift = hot(272, 272, [(a * 16 + b, a * 16 + b - 1) for a in range(17) for b in range(1, 16)])
    from_left = np.stack([
        hot(272, LEFT, [(a * 16, 2 * a + par) for a in range(17 - par)]) for par in range(2)
    ])
    back = hot(272, 256, [(a * 16 + b, a * 16 + b + 1) for a in range(16) for b in range(15)])
    below = hot(16, 256, [(b, 8 * b + 6) for b in range(16)])
    beside = hot(272, 256, [(a * 16 + 15, 8 * (16 + a) + 6) for a in range(16)]
                 + [(256 + b, 8 * (b + 1) + 6) for b in range(15)] + [(271, 79)])
    return rim, rim_grad, body, sides, edges, left, first_col, shift, from_left, back, below, beside


def dot(a, b):
    return jnp.dot(a, b, preferred_element_type=F32)


def dot_t(a, b):
    return lax.dot_general(a, b, (((1,), (1,)), ((), ())), preferred_element_type=F32)


def dot_l(a, b):
    return lax.dot_general(a, b, (((0,), (0,)), ((), ())), preferred_element_type=F32)


def sigmoid(v):
    return 0.5 * jnp.tanh(0.5 * v) + 0.5


def route_rows(pos, r):
    lane = lax.broadcasted_iota(jnp.int32, (512, 128), 1).astype(F32)
    q = lax.broadcasted_iota(jnp.int32, (512, 128), 0) % 8
    zero = jnp.zeros((512, 128), F32)
    k = zero.astype(jnp.int32) + r
    grad_row = jnp.where(k < 16, 1.0, 0.0)
    corner_row = jnp.where(k < 6, -1.0, 1.0)
    corner_col = jnp.where((k < 4) | (k == 6) | (k == 7), -1.0, 1.0)
    d_row = jnp.where(q < 2, -1.0, jnp.where(q == 4, 1.0, zero))
    d_row = jnp.where(q == 6, grad_row, jnp.where(q == 7, corner_row, d_row))
    d_col = jnp.where((q == 2) | (q == 3), -1.0, jnp.where(q == 5, 1.0, zero))
    d_col = jnp.where(q == 6, 1.0 - grad_row, jnp.where(q == 7, corner_col, d_col))
    p_row = jnp.floor(pos * 0.25)
    n_row = p_row + d_row
    n_col = pos - 4.0 * p_row + d_col
    inside = (n_row >= 0.0) & (n_row < GH) & (n_col >= 0.0) & (n_col < GW)
    want = jnp.where(inside, 4.0 * n_row + n_col, -1.0)
    has = jnp.where(pos == lane, 1.0, 0.0).astype(BF)
    wants = jnp.where(want == lane, 1.0, 0.0).astype(BF)
    same = (lax.broadcasted_iota(jnp.int32, (512, 512), 0) % 8) == (
        lax.broadcasted_iota(jnp.int32, (512, 512), 1) % 8)
    return jnp.where(same, dot_t(wants, has), 0.0).astype(BF)


Z_ORDER = (4, 3, 5, 2, 6, 1, 7, 0)


def level_kernel(positions_hbm, clear_hbm, tiles_hbm, cotangent_hbm, w1_here, w2_here, *refs):
    names = list(TABLES)
    table_hbm = dict(zip(names, refs[:len(names)]))
    feat, out = refs[len(names):len(names) + 2]
    refs = refs[len(names) + 2:]
    table = dict(zip(names, refs[:len(names)]))
    (positions, clear, tiles, cotangent, in_sem, table_sem, pos_send, pos_buf, send1, recv1, send2, recv2, masked, own_rim, halo, w1, w2,
     x4, h_odd, h_even, left_x, slopes, d_pre, g_f, g, f_buf, o_buf, s_buf, s_send, z_send, z_buf,
     n_send, n_buf, x_send, x_buf, c_send, c_buf,
     a2a_s, a2a_r, w_s, w_r, v_s, v_r, y_s, y_r, zs, zr, xs, xr, cs, cr, own_sem) = refs[len(names):]

    s = lax.axis_index("scene")
    r = lax.axis_index("region")
    z, y = r // YN, r % YN
    sib = s + 1 - 2 * (s % 2)

    arrays = [pltpu.make_async_copy(src, dst, in_sem.at[n]) for n, (src, dst) in enumerate((
        (positions_hbm, positions), (clear_hbm, clear), (tiles_hbm, tiles), (cotangent_hbm, cotangent)))]
    for copy in arrays:
        copy.start()
    loads = {name: pltpu.make_async_copy(table_hbm[name], table[name], table_sem.at[n])
             for n, name in enumerate(names)}
    for name in names:
        loads[name].start()

    barrier = pltpu.get_barrier_semaphore()

    def greet(o, carry):
        pl.semaphore_signal(barrier, inc=1, device_id={"region": (r + o) % REG}, device_id_type=MESH)
        return carry

    lax.fori_loop(1, REG, greet, 0)
    for o in range(1, SC):
        pl.semaphore_signal(barrier, inc=1, device_id={"scene": (s + o) % SC}, device_id_type=MESH)

    def w_rows(ref, who):
        return ref.at[pl.ds(pl.multiple_of(who * WROWS, 32), WROWS)]

    weights = ((w1_here, w1), (w2_here, w2))
    own = [pltpu.make_async_copy(src, w_rows(dst, s), own_sem.at[n]) for n, (src, dst) in enumerate(weights)]
    for copy in own:
        copy.start()

    def all_to_all(n, src, dst):
        def send(o, carry):
            step, turn_y = o // YN, o % YN
            dz = ZN // 2 + ((step + 1) // 2) * (1 - 2 * (step % 2))
            dy = YN // 2 + ((turn_y + 1) // 2) * (1 - 2 * (turn_y % 2))
            to = ((z + dz) % ZN) * YN + (y + dy) % YN
            pltpu.make_async_remote_copy(
                src_ref=src(to), dst_ref=dst(r), send_sem=a2a_s.at[n], recv_sem=a2a_r.at[n],
                device_id={"region": to}, device_id_type=MESH).start()
            return carry

        lax.fori_loop(0, REG - 1, send, 0)

    def await_all(buf, sem):
        pltpu.make_async_copy(buf, buf, sem).wait()

    for copy in arrays[:2]:
        copy.wait()
    own_pos = [positions[0:1, t:t + 1].astype(F32) for t in range(2)]
    for t in range(2):
        pos_send[t] = jnp.broadcast_to(own_pos[t], (1, 128))
    pl.semaphore_wait(barrier, REG - 1 + SC - 1)

    right, left_chip = (s + 2) % SC, (s + 6) % SC

    def to_scene(src, dst, send_sem, recv_sem, who):
        copy = pltpu.make_async_remote_copy(
            src_ref=src, dst_ref=dst, send_sem=send_sem, recv_sem=recv_sem,
            device_id={"scene": who}, device_id_type=MESH)
        copy.start()
        return copy

    all_to_all(0, lambda to: pos_send, lambda me: pos_buf.at[pl.ds(2 * me, 2)])
    far, near = [], []

    def send_weights(n):
        src, dst = weights[n]
        far.append(to_scene(src, w_rows(dst, s), w_s.at[n, 0], w_r.at[n, 0], right))
        far.append(to_scene(src, w_rows(dst, s), w_s.at[n, 1], w_r.at[n, 1], left_chip))
        near.append([to_scene(src, w_rows(dst, s), v_s.at[n, 0], v_r.at[n, 0], sib)])

    send_weights(0)

    for copy in arrays[2:]:
        copy.wait()
    for t in range(2):
        kept = clear[0:1, t:t + 1].astype(F32)
        masked[t] = (cotangent[t].reshape(256, C).astype(F32) * kept).astype(BF)
    loads["rim"].wait()
    loads["rim_grad"].wait()
    rims = []
    for t in range(2):
        rim = dot(table["rim"][...], tiles[t].reshape(1024, C)) + dot(table["rim_grad"][...], masked[t])
        own_rim[t] = rim.astype(BF)
        rims.append(rim.reshape(REG, 8, C))
    send1[...] = jnp.concatenate(rims, axis=1).astype(BF)
    all_to_all(1, lambda to: send1.at[to], lambda me: recv1.at[me])
    recv1[r] = send1[r]
    for t in range(2):
        pos_buf[2 * r + t] = pos_send[t]

    loads["body"].wait()
    for t in range(2):
        for c in range(4):
            chunk = tiles[t, 8 * c:8 * c + 8].reshape(256, C)
            got = dot(table["body"][:256], chunk).astype(BF)
            for at, blk in enumerate((1, 2)):
                x4[t, 4 * c + 1:4 * c + 5, :, :, blk * C:(blk + 1) * C] = (
                    got[at * 128:(at + 1) * 128].reshape(4, 2, 16, C))

    def forward(n, came, at):
        rows = w_rows(weights[n][1], came)
        return to_scene(rows, rows, v_s.at[n, at], v_r.at[n, at], sib)

    opposite = (s + 4) % SC
    far[0].wait_recv()
    rows = w_rows(w1, left_chip)
    far.append(to_scene(rows, rows, w_s.at[0, 2], w_r.at[0, 2], right))
    near[0].append(forward(0, left_chip, 1))
    far[1].wait_recv()
    near[0].append(forward(0, right, 2))
    send_weights(1)
    await_all(pos_buf.at[pl.ds(0, 2 * REG - 2)], a2a_r.at[0])
    route = route_rows(jnp.broadcast_to(pos_buf[...], (64, 8, 128)).reshape(512, 128), r)
    await_all(recv1.at[pl.ds(0, REG - 1)], a2a_r.at[1])
    send2[...] = dot(route, recv1[...].reshape(512, C)).astype(BF).reshape(REG, 16, C)
    all_to_all(2, lambda to: send2.at[to], lambda me: recv2.at[me])
    recv2[r] = send2[r]

    for name in names[3:]:
        loads[name].wait()
    far[2].wait_recv()
    near[0].append(forward(0, opposite, 3))
    far[3].wait_recv()
    near[1].append(forward(1, left_chip, 1))
    far[4].wait_recv()
    rows = w_rows(w2, right)
    far.append(to_scene(rows, rows, w_s.at[1, 2], w_r.at[1, 2], left_chip))
    near[1].append(forward(1, right, 2))
    await_all(recv2.at[pl.ds(0, REG - 1)], a2a_r.at[2])

    came = recv2[...].astype(F32)
    for t in range(2):
        halo[t] = came[:, 8 * t:8 * t + 8].reshape(256, C).astype(BF)
    for t in range(2):
        for c in range(4):
            chunk = tiles[t, 8 * c:8 * c + 8].reshape(256, C)
            got = dot(table["body"][256:], chunk) + dot(table["sides"][...], halo[t, 64 * c:64 * c + 64])
            got = got.astype(BF)
            for at, blk in enumerate((0, 3)):
                x4[t, 4 * c + 1:4 * c + 5, :, :, blk * C:(blk + 1) * C] = (
                    got[at * 128:(at + 1) * 128].reshape(4, 2, 16, C))
        rim = dot(table["edges"][...], halo[t]).astype(BF)
        for sel, (pair, par) in enumerate(((0, 0), (0, 1), (17, 0))):
            for blk in range(4):
                start = sel * 64 + blk * 16
                x4[t, pair, par, :, blk * C:(blk + 1) * C] = rim[start:start + 16]
        side = dot(table["left"][...], halo[t])
        inner = dot(table["first_col"][...], own_rim[t])
        for i in range(3):
            for j in range(3):
                tap = 3 * i + j
                part = side[tap * LEFT:(tap + 1) * LEFT]
                if j == 2:
                    part = part + inner[i * LEFT:(i + 1) * LEFT]
                left_x[t * LEFT:(t + 1) * LEFT, tap * C:(tap + 1) * C] = part.astype(BF)

    far[5].wait_recv()
    near[1].append(forward(1, opposite, 3))
    own[0].wait()
    for copy in near[0]:
        copy.wait_recv()

    pre_left = dot(left_x[...], w1[...])
    row_id = lax.broadcasted_iota(jnp.int32, (LEFT, C), 0)
    hidden_left, above = [], []
    for t in range(2):
        p_row = jnp.floor(own_pos[t] * 0.25)
        has_left = jnp.where(own_pos[t] - 4.0 * p_row > 0.0, 1.0, 0.0)
        has_above = jnp.where(p_row > 0.0, 1.0, 0.0)
        above.append(has_above)
        v = pre_left[t * LEFT:(t + 1) * LEFT]
        keep = jnp.where(row_id == 0, has_left * has_above, has_left)
        hidden_left.append((v * sigmoid(v) * keep).astype(BF))

    def window(t, par, i, cp):
        row = par + i
        n = 17 - par
        return x4[t, row // 2:row // 2 + n, row % 2, :, cp * C:cp * C + 768].reshape(n * 16, 768)

    for t in range(2):
        for par in range(2):
            store = h_odd if par == 0 else h_even
            n = 17 - par
            for cp in range(2):
                patch = jnp.concatenate([window(t, par, i, cp) for i in range(3)], axis=1)
                pre = dot(patch, w1[...])
                sig = sigmoid(pre)
                act = pre * sig
                if par == 0:
                    own_row = lax.broadcasted_iota(jnp.int32, (272, C), 0) >= 16
                    act = jnp.where(own_row, act, act * above[t])
                act = act.astype(BF)
                if cp == 0:
                    store[t, :, :, C:2 * C] = act.reshape(n, 16, C)
                else:
                    store[t, :, :, 2 * C:] = act.reshape(n, 16, C)
                    moved = dot(table["shift"][:n * 16, :n * 16], act)
                    moved = moved + dot(table["from_left"][par, :n * 16], hidden_left[t])
                    store[t, :, :, :C] = moved.astype(BF).reshape(n, 16, C)
                if par == 0:
                    pre, sig = pre[16:], sig[16:]
                slopes[4 * t + 2 * par + cp] = sig * (1.0 + pre * (1.0 - sig))

    def hidden_rows(t, i):
        if i == 1:
            return h_even[t].reshape(256, 768)
        return h_odd[t, i // 2:i // 2 + 16].reshape(256, 768)

    def blocks(n):
        for yy in range(YN):
            for zz in range(ZN):
                start = OWN_ROWS * (zz * YN + yy)
                rows = g_f[start:start + OWN_ROWS, :]
                g[n, yy, zz] = jnp.concatenate([rows[:, :128], rows[:, 128:]], axis=0).astype(BF)

    def to_region(src, dst, send_sem, recv_sem, who):
        copy = pltpu.make_async_remote_copy(
            src_ref=src, dst_ref=dst, send_sem=send_sem, recv_sem=recv_sem,
            device_id={"region": who}, device_id_type=MESH)
        copy.start()
        return copy

    sent = []
    y_copies = {}

    def turn(oz):
        return 1 if oz % 2 == 0 else YN - 1

    def y_first(n):
        for kind in range(2):
            for oz in Z_ORDER:
                d = turn(oz)
                block = (y + 2) % YN if kind == 0 else (y + YN - d) % YN
                who = (y + d) % YN if kind == 0 else block
                buf = f_buf if kind == 0 else o_buf
                y_copies[n, kind, oz] = to_region(
                    g.at[n, block, (z + oz) % ZN], buf.at[n, oz],
                    y_s.at[kind, n, oz], y_r.at[kind, n, oz], z * YN + who)
                sent.append(y_copies[n, kind, oz])

    def y_second(n):
        for oz in Z_ORDER:
            who = (y + turn(oz)) % YN
            y_copies[n, 0, oz].wait_recv()
            summed = g[n, who, (z + oz) % ZN].astype(F32) + f_buf[n, oz].astype(F32)
            s_send[n, oz] = summed.astype(BF)
            y_copies[n, 2, oz] = to_region(
                s_send.at[n, oz], s_buf.at[n, oz], y_s.at[2, n, oz], y_r.at[2, n, oz], z * YN + who)
            sent.append(y_copies[n, 2, oz])

    def z_first(n):
        copies = []
        for oz in Z_ORDER:
            y_copies[n, 1, oz].wait_recv()
            y_copies[n, 2, oz].wait_recv()
            total = (g[n, y, (z + oz) % ZN].astype(F32) + o_buf[n, oz].astype(F32)) + s_buf[n, oz].astype(F32)
            if oz:
                z_send[n, oz - 1] = total.astype(BF)
                copies.append(to_region(
                    z_send.at[n, oz - 1], z_buf.at[n, oz - 1], zs.at[n, oz - 1], zr.at[n, oz - 1],
                    ((z + oz) % ZN) * YN + y))
        sent.extend(copies)
        return total, copies

    def z_second(n, total, copies):
        for at, copy in enumerate(copies):
            copy.wait_recv()
            total = total + z_buf[n, Z_ORDER[at] - 1].astype(F32)
        return total

    for i in range(3):
        for j in range(3):
            tap = 3 * i + j
            seen = jnp.concatenate([hidden_rows(t, i)[:, j * C:(j + 1) * C] for t in range(2)], axis=0)
            g_f[tap * C:(tap + 1) * C, :] = dot_l(seen, masked[...].reshape(512, C))
    blocks(1)
    y_first(1)

    own[1].wait()
    for copy in near[1]:
        copy.wait_recv()
    for t in range(2):
        patch = jnp.concatenate([hidden_rows(t, i) for i in range(3)], axis=1)
        feat[t] = dot(patch, w2[...]).astype(BF).reshape(16, 16, C)

    def second(tap):
        return w2[tap * C:(tap + 1) * C, :]

    up, down = slice(0, 256), slice(16, 272)
    for t in range(2):
        m0 = jnp.concatenate([masked[t], dot(table["below"][...], halo[t]).astype(BF)], axis=0)
        m1 = (dot(table["back"][...], masked[t]) + dot(table["beside"][...], halo[t])).astype(BF)
        spread = (
            dot_t(m0[up], second(7)) + dot_t(m0[down], second(1)),
            (dot_t(m0[up], second(8)) + dot_t(m1[up], second(6))
             + dot_t(m0[down], second(2)) + dot_t(m1[down], second(0))),
            dot_t(m0[up], second(4)),
            dot_t(m0[up], second(5)) + dot_t(m1[up], second(3)),
        )
        for n in range(4):
            group = 4 * t + n
            d_pre[group * 256:(group + 1) * 256, :] = (spread[n] * slopes[group]).astype(BF)

    y_second(1)

    def own_rows(t, par, i, cp, j):
        row = (2 if par == 0 else 1) + i
        lanes = (cp + j) * C
        return x4[t, row // 2:row // 2 + 16, row % 2, :, lanes:lanes + C].reshape(256, C)

    for i in range(3):
        for j in range(3):
            tap = 3 * i + j
            seen = jnp.concatenate(
                [own_rows(t, par, i, cp, j) for t in range(2) for par in range(2) for cp in range(2)], axis=0)
            g_f[tap * C:(tap + 1) * C, :] = dot_l(seen, d_pre[...])
    blocks(0)
    y_first(0)
    z_left = z_first(1)
    y_second(0)
    total_second = z_second(1, *z_left)
    total_first = z_second(0, *z_first(0))

    squares = jnp.sum(total_first * total_first + total_second * total_second, axis=0, keepdims=True)
    n_send[0] = squares
    all_to_all(3, lambda to: n_send.at[0], lambda me: n_buf.at[me])
    n_buf[r] = squares
    for n, total in enumerate((total_first, total_second)):
        turned = jnp.concatenate([total[:OWN_ROWS].T, total[OWN_ROWS:].T], axis=0)
        x_send[:, n] = turned.reshape(SC, 32, OWN_ROWS)
    x_copies = []
    for o in range(1, SC):
        to = (s + o) % SC
        x_copies.append(to_scene(x_send.at[to], x_buf.at[o - 1], xs.at[o - 1], xr.at[o - 1], to))
    await_all(n_buf.at[pl.ds(0, REG - 1)], a2a_r.at[3])
    sum_sq = jnp.sum(n_buf[...].reshape(REG, 128), keepdims=True)
    factor = (3.0 * C * math.sqrt(2.0) / SC) / (jnp.sqrt(sum_sq) + 0.01)
    c_send[0] = jnp.broadcast_to(factor, (1, 128))
    c_copies = []
    for o in range(1, SC):
        to = (s + o) % SC
        c_copies.append(to_scene(c_send.at[0], c_buf.at[o - 1], cs.at[o - 1], cr.at[o - 1], to))
    result = x_send[s] * factor.reshape(1, 1, 1)
    for o in range(1, SC):
        x_copies[o - 1].wait_recv()
        c_copies[o - 1].wait_recv()
        result = result + x_buf[o - 1] * c_buf[o - 1][:, :1].reshape(1, 1, 1)
    out[...] = result

    for copy in far + near[0] + near[1] + sent + x_copies + c_copies:
        copy.wait_send()
    await_all(pos_buf.at[pl.ds(0, 2 * REG - 2)], a2a_s.at[0])
    await_all(send1.at[pl.ds(0, REG - 1)], a2a_s.at[1])
    await_all(send2.at[pl.ds(0, REG - 1)], a2a_s.at[2])
    await_all(n_buf.at[pl.ds(0, REG - 1)], a2a_s.at[3])


NAMES = ("rim", "rim_grad", "body", "sides", "edges", "left", "first_col", "shift", "from_left",
         "back", "below", "beside")
TABLES = dict(zip(NAMES, place_tables()))


def level(positions, clear, tiles, cotangent, w1, w2):
    vmem = pl.BlockSpec(memory_space=pltpu.VMEM)
    anywhere = pl.BlockSpec(memory_space=pl.ANY)
    dma = pltpu.SemaphoreType.DMA
    tables = list(TABLES.values())
    part = (144, 128)
    return pl.pallas_call(
        level_kernel,
        name="level",
        out_shape=(jax.ShapeDtypeStruct((2, 16, 16, C), BF), jax.ShapeDtypeStruct((2, 32, OWN_ROWS), F32)),
        in_specs=[anywhere] * (6 + len(tables)),
        out_specs=(vmem, vmem),
        scratch_shapes=[pltpu.VMEM(t.shape, BF) for t in tables] + [
            pltpu.VMEM((1, 2), jnp.int32), pltpu.VMEM((1, 2), jnp.int32),
            pltpu.VMEM((2, 32, 32, C), BF), pltpu.VMEM((2, 16, 16, C), BF),
            dma((4,)), dma((len(tables),)),
            pltpu.VMEM((2, 1, 128), F32), pltpu.VMEM((2 * REG, 1, 128), F32),
            pltpu.VMEM((REG, 16, C), BF), pltpu.VMEM((REG, 16, C), BF),
            pltpu.VMEM((REG, 16, C), BF), pltpu.VMEM((REG, 16, C), BF),
            pltpu.VMEM((2, 256, C), BF), pltpu.VMEM((2, 256, C), BF), pltpu.VMEM((2, 256, C), BF),
            pltpu.VMEM((ROWS, C), BF), pltpu.VMEM((ROWS, C), BF),
            pltpu.VMEM((2, 18, 2, 16, 4 * C), BF),
            pltpu.VMEM((2, 17, 16, 3 * C), BF), pltpu.VMEM((2, 16, 16, 3 * C), BF),
            pltpu.VMEM((2 * LEFT, ROWS), BF),
            pltpu.VMEM((8, 256, C), F32),
            pltpu.VMEM((2048, C), BF),
            pltpu.VMEM((ROWS, C), F32),
            pltpu.VMEM((2, YN, ZN) + part, BF),
            pltpu.VMEM((2, ZN) + part, BF), pltpu.VMEM((2, ZN) + part, BF),
            pltpu.VMEM((2, ZN) + part, BF), pltpu.VMEM((2, ZN) + part, BF),
            pltpu.VMEM((2, ZN - 1) + part, BF), pltpu.VMEM((2, ZN - 1) + part, BF),
            pltpu.VMEM((1, 1, 128), F32), pltpu.VMEM((REG, 1, 128), F32),
            pltpu.VMEM((SC, 2, 32, OWN_ROWS), F32), pltpu.VMEM((SC - 1, 2, 32, OWN_ROWS), F32),
            pltpu.VMEM((1, 1, 128), F32), pltpu.VMEM((SC - 1, 1, 128), F32),
            dma((4,)), dma((4,)), dma((2, 3)), dma((2, 3)), dma((2, 4)), dma((2, 4)),
            dma((3, 2, ZN)), dma((3, 2, ZN)), dma((2, ZN - 1)), dma((2, ZN - 1)),
            dma((SC - 1,)), dma((SC - 1,)), dma((SC - 1,)), dma((SC - 1,)), dma((2,)),
        ],
        compiler_params=pltpu.CompilerParams(
            collective_id=0, has_side_effects=True, vmem_limit_bytes=VMEM_LIMIT),
    )(positions, clear, tiles, cotangent, w1, w2, *[jnp.asarray(t) for t in tables])


def local(tiles, cotangent, positions, clear, w_first, w_second):
    feat, out = level(positions, clear, tiles[0], cotangent[0], w_first, w_second)
    return feat[None], out[0].T, out[1].T


def solution(mesh):
    in_specs = (
        P("scene", "region", None, None, None),
        P("scene", "region", None, None, None),
        P("scene", "region"),
        P("scene", "region"),
        P("scene", None),
        P("scene", None),
    )
    out_specs = (P("scene", "region", None, None, None), P("region", "scene"), P("region", "scene"))
    return jax.shard_map(local, mesh=mesh, in_specs=in_specs, out_specs=out_specs, check_vma=False)
```

```python
import math

import jax
import jax.numpy as jnp
import ml_dtypes
import numpy as np
from jax import lax
from jax.experimental import pallas as pl
from jax.experimental.pallas import tpu as pltpu
from jax.sharding import PartitionSpec as P

MESH = pl.DeviceIdType.MESH
BF = jnp.bfloat16
F32 = jnp.float32
GW, GH = 4, 16
C = 256
REG, ZN, YN, SC = 32, 8, 4, 8
WROWS = 288
LEFT = 48
ROWS = 9 * C
OWN_ROWS = ROWS // REG
VMEM_LIMIT = 56 * 1024 * 1024


def hot(rows, cols, pairs):
    out = np.zeros((rows, cols), np.float32)
    for row, col in pairs:
        out[row, col] = 1.0
    return out.astype(ml_dtypes.bfloat16)


def place_tables():
    tile = lambda h, w: 32 * h + w
    corner = ((30, 30), (30, 31), (31, 30), (31, 31), (30, 0), (31, 0), (0, 30), (0, 31), (0, 0))
    rim = hot(256, 1024, [
        (8 * k + q, px) for k in range(32) for q, px in enumerate((
            tile(31, k), tile(30, k), tile(k, 31), tile(k, 30), tile(0, k), tile(k, 0)))
    ] + [(8 * k + 7, tile(*at)) for k, at in enumerate(corner)])
    rim_grad = hot(256, 256, [(8 * k + 6, k if k < 16 else 16 * (k - 16)) for k in range(32)] + [(79, 0)])

    cols = lambda blk, b: 2 * b - 1 + blk
    order = (1, 2, 0, 3)
    body = hot(512, 256, [
        (at * 128 + h * 16 + b, h * 32 + cols(blk, b))
        for at, blk in enumerate(order) for h in range(8) for b in range(16) if 0 <= cols(blk, b) < 32
    ])
    sides = hot(256, 64, [(h * 16, 8 * h + 2) for h in range(8)]
                + [(128 + h * 16 + 15, 8 * h + 5) for h in range(8)])
    edge_q = (1, 0, 4)
    corner_left, corner_right = (1, 3, 7), (4, 5, 8)

    def edge_source(sel, col):
        if col < 0:
            return 8 * corner_left[sel] + 7
        if col > 31:
            return 8 * corner_right[sel] + 7
        return 8 * col + edge_q[sel]

    edges = hot(192, 256, [
        (sel * 64 + blk * 16 + b, edge_source(sel, cols(blk, b)))
        for sel in range(3) for blk in range(4) for b in range(16)
    ])

    def left_source(hh, j):
        if 0 <= hh < 32:
            return 8 * hh + (3, 2)[j] if j < 2 else None
        sel = {-2: 0, -1: 1, 32: 2}[hh]
        if j < 2:
            return 8 * ((0, 1), (2, 3), (6, 7))[sel][j] + 7
        return edge_q[sel]

    left = hot(9 * LEFT, 256, [
        ((3 * i + j) * LEFT + g, left_source(g + i - 2, j))
        for i in range(3) for j in range(3) for g in range(33)
        if left_source(g + i - 2, j) is not None
    ])
    first_col = hot(3 * LEFT, 256, [
        (i * LEFT + g, 8 * (g + i - 2) + 5) for i in range(3) for g in range(33) if 0 <= g + i - 2 < 32
    ])
    shift = hot(272, 272, [(a * 16 + b, a * 16 + b - 1) for a in range(17) for b in range(1, 16)])
    from_left = np.stack([
        hot(272, LEFT, [(a * 16, 2 * a + par) for a in range(17 - par)]) for par in range(2)
    ])
    back = hot(272, 256, [(a * 16 + b, a * 16 + b + 1) for a in range(16) for b in range(15)])
    below = hot(16, 256, [(b, 8 * b + 6) for b in range(16)])
    beside = hot(272, 256, [(a * 16 + 15, 8 * (16 + a) + 6) for a in range(16)]
                 + [(256 + b, 8 * (b + 1) + 6) for b in range(15)] + [(271, 79)])
    return rim, rim_grad, body, sides, edges, left, first_col, shift, from_left, back, below, beside


def dot(a, b):
    return jnp.dot(a, b, preferred_element_type=F32)


def dot_t(a, b):
    return lax.dot_general(a, b, (((1,), (1,)), ((), ())), preferred_element_type=F32)


def dot_l(a, b):
    return lax.dot_general(a, b, (((0,), (0,)), ((), ())), preferred_element_type=F32)


def sigmoid(v):
    return 0.5 * jnp.tanh(0.5 * v) + 0.5


def route_rows(pos, r):
    lane = lax.broadcasted_iota(jnp.int32, (512, 128), 1).astype(F32)
    q = lax.broadcasted_iota(jnp.int32, (512, 128), 0) % 8
    zero = jnp.zeros((512, 128), F32)
    k = zero.astype(jnp.int32) + r
    grad_row = jnp.where(k < 16, 1.0, 0.0)
    corner_row = jnp.where(k < 6, -1.0, 1.0)
    corner_col = jnp.where((k < 4) | (k == 6) | (k == 7), -1.0, 1.0)
    d_row = jnp.where(q < 2, -1.0, jnp.where(q == 4, 1.0, zero))
    d_row = jnp.where(q == 6, grad_row, jnp.where(q == 7, corner_row, d_row))
    d_col = jnp.where((q == 2) | (q == 3), -1.0, jnp.where(q == 5, 1.0, zero))
    d_col = jnp.where(q == 6, 1.0 - grad_row, jnp.where(q == 7, corner_col, d_col))
    p_row = jnp.floor(pos * 0.25)
    n_row = p_row + d_row
    n_col = pos - 4.0 * p_row + d_col
    inside = (n_row >= 0.0) & (n_row < GH) & (n_col >= 0.0) & (n_col < GW)
    want = jnp.where(inside, 4.0 * n_row + n_col, -1.0)
    has = jnp.where(pos == lane, 1.0, 0.0).astype(BF)
    wants = jnp.where(want == lane, 1.0, 0.0).astype(BF)
    same = (lax.broadcasted_iota(jnp.int32, (512, 512), 0) % 8) == (
        lax.broadcasted_iota(jnp.int32, (512, 512), 1) % 8)
    return jnp.where(same, dot_t(wants, has), 0.0).astype(BF)


Z_ORDER = (4, 3, 5, 2, 6, 1, 7, 0)


def level_kernel(positions_hbm, clear_hbm, tiles_hbm, cotangent_hbm, w1_here, w2_here, *refs):
    names = list(TABLES)
    table_hbm = dict(zip(names, refs[:len(names)]))
    feat, out = refs[len(names):len(names) + 2]
    refs = refs[len(names) + 2:]
    table = dict(zip(names, refs[:len(names)]))
    (positions, clear, tiles, cotangent, in_sem, table_sem, pos_send, pos_buf, send1, recv1, send2, recv2, masked, own_rim, halo, w1, w2,
     x4, h_odd, h_even, left_x, slopes, d_pre, g_f, g, f_buf, o_buf, s_buf, s_send, z_send, z_buf,
     n_send, n_buf, x_send, x_buf, c_send, c_buf,
     a2a_s, a2a_r, w_s, w_r, v_s, v_r, y_s, y_r, zs, zr, xs, xr, cs, cr, own_sem) = refs[len(names):]

    s = lax.axis_index("scene")
    r = lax.axis_index("region")
    z, y = r // YN, r % YN
    sib = s + 1 - 2 * (s % 2)

    arrays = [pltpu.make_async_copy(src, dst, in_sem.at[n]) for n, (src, dst) in enumerate((
        (positions_hbm, positions), (clear_hbm, clear), (tiles_hbm, tiles), (cotangent_hbm, cotangent)))]
    for copy in arrays:
        copy.start()
    loads = {name: pltpu.make_async_copy(table_hbm[name], table[name], table_sem.at[n])
             for n, name in enumerate(names)}
    for name in names:
        loads[name].start()

    barrier = pltpu.get_barrier_semaphore()

    def far_first(o):
        step, turn_y = o // YN, o % YN
        dz = ZN // 2 + ((step + 1) // 2) * (1 - 2 * (step % 2))
        dy = YN // 2 + ((turn_y + 1) // 2) * (1 - 2 * (turn_y % 2))
        return ((z + dz) % ZN) * YN + (y + dy) % YN

    def greet(o, carry):
        pl.semaphore_signal(barrier, inc=1, device_id={"region": far_first(o)}, device_id_type=MESH)
        return carry

    lax.fori_loop(0, REG - 1, greet, 0)
    for o in range(1, SC):
        pl.semaphore_signal(barrier, inc=1, device_id={"scene": (s + o) % SC}, device_id_type=MESH)

    def w_rows(ref, who):
        return ref.at[pl.ds(pl.multiple_of(who * WROWS, 32), WROWS)]

    weights = ((w1_here, w1), (w2_here, w2))
    own = [pltpu.make_async_copy(src, w_rows(dst, s), own_sem.at[n]) for n, (src, dst) in enumerate(weights)]
    for copy in own:
        copy.start()

    def all_to_all(n, src, dst):
        def send(o, carry):
            to = far_first(o)
            pltpu.make_async_remote_copy(
                src_ref=src(to), dst_ref=dst(r), send_sem=a2a_s.at[n], recv_sem=a2a_r.at[n],
                device_id={"region": to}, device_id_type=MESH).start()
            return carry

        lax.fori_loop(0, REG - 1, send, 0)

    def await_all(buf, sem):
        pltpu.make_async_copy(buf, buf, sem).wait()

    for copy in arrays[:2]:
        copy.wait()
    own_pos = [positions[0:1, t:t + 1].astype(F32) for t in range(2)]
    for t in range(2):
        pos_send[t] = jnp.broadcast_to(own_pos[t], (1, 128))
    pl.semaphore_wait(barrier, REG - 1 + SC - 1)

    right, left_chip = (s + 2) % SC, (s + 6) % SC

    def to_scene(src, dst, send_sem, recv_sem, who):
        copy = pltpu.make_async_remote_copy(
            src_ref=src, dst_ref=dst, send_sem=send_sem, recv_sem=recv_sem,
            device_id={"scene": who}, device_id_type=MESH)
        copy.start()
        return copy

    all_to_all(0, lambda to: pos_send, lambda me: pos_buf.at[pl.ds(2 * me, 2)])
    far, near = [], []

    def send_weights(n):
        src, dst = weights[n]
        far.append(to_scene(src, w_rows(dst, s), w_s.at[n, 0], w_r.at[n, 0], right))
        far.append(to_scene(src, w_rows(dst, s), w_s.at[n, 1], w_r.at[n, 1], left_chip))
        near.append([to_scene(src, w_rows(dst, s), v_s.at[n, 0], v_r.at[n, 0], sib)])

    send_weights(0)

    for copy in arrays[2:]:
        copy.wait()
    for t in range(2):
        kept = clear[0:1, t:t + 1].astype(F32)
        masked[t] = (cotangent[t].reshape(256, C).astype(F32) * kept).astype(BF)
    loads["rim"].wait()
    loads["rim_grad"].wait()
    rims = []
    for t in range(2):
        rim = dot(table["rim"][...], tiles[t].reshape(1024, C)) + dot(table["rim_grad"][...], masked[t])
        own_rim[t] = rim.astype(BF)
        rims.append(rim.reshape(REG, 8, C))
    rims = jnp.concatenate(rims, axis=1).astype(BF)
    for half in range(2):
        send1[half] = rims[:, :, half * 128:(half + 1) * 128]
        all_to_all(1 + half, lambda to: send1.at[half, to], lambda me: recv1.at[half, me])
    for half in range(2):
        recv1[half, r] = send1[half, r]
    for t in range(2):
        pos_buf[2 * r + t] = pos_send[t]

    loads["body"].wait()
    for t in range(2):
        for c in range(4):
            chunk = tiles[t, 8 * c:8 * c + 8].reshape(256, C)
            got = dot(table["body"][:256], chunk).astype(BF)
            for at, blk in enumerate((1, 2)):
                x4[t, 4 * c + 1:4 * c + 5, :, :, blk * C:(blk + 1) * C] = (
                    got[at * 128:(at + 1) * 128].reshape(4, 2, 16, C))

    def forward(n, came, at):
        rows = w_rows(weights[n][1], came)
        return to_scene(rows, rows, v_s.at[n, at], v_r.at[n, at], sib)

    opposite = (s + 4) % SC
    far[0].wait_recv()
    rows = w_rows(w1, left_chip)
    far.append(to_scene(rows, rows, w_s.at[0, 2], w_r.at[0, 2], right))
    near[0].append(forward(0, left_chip, 1))
    far[1].wait_recv()
    near[0].append(forward(0, right, 2))
    send_weights(1)
    await_all(pos_buf.at[pl.ds(0, 2 * REG - 2)], a2a_r.at[0])
    route = route_rows(jnp.broadcast_to(pos_buf[...], (64, 8, 128)).reshape(512, 128), r)
    for half in range(2):
        await_all(recv1.at[half, pl.ds(0, REG - 1)], a2a_r.at[1 + half])
        send2[half] = dot(route, recv1[half].reshape(512, 128)).astype(BF).reshape(REG, 16, 128)
        all_to_all(3 + half, lambda to: send2.at[half, to], lambda me: recv2.at[half, me])
    for half in range(2):
        recv2[half, r] = send2[half, r]

    for name in names[3:]:
        loads[name].wait()
    far[2].wait_recv()
    near[0].append(forward(0, opposite, 3))
    far[3].wait_recv()
    near[1].append(forward(1, left_chip, 1))
    far[4].wait_recv()
    rows = w_rows(w2, right)
    far.append(to_scene(rows, rows, w_s.at[1, 2], w_r.at[1, 2], left_chip))
    near[1].append(forward(1, right, 2))
    for half in range(2):
        await_all(recv2.at[half, pl.ds(0, REG - 1)], a2a_r.at[3 + half])
        came = recv2[half].astype(F32)
        for t in range(2):
            halo[t, :, half * 128:(half + 1) * 128] = came[:, 8 * t:8 * t + 8].reshape(256, 128).astype(BF)
    for t in range(2):
        for c in range(4):
            chunk = tiles[t, 8 * c:8 * c + 8].reshape(256, C)
            got = dot(table["body"][256:], chunk) + dot(table["sides"][...], halo[t, 64 * c:64 * c + 64])
            got = got.astype(BF)
            for at, blk in enumerate((0, 3)):
                x4[t, 4 * c + 1:4 * c + 5, :, :, blk * C:(blk + 1) * C] = (
                    got[at * 128:(at + 1) * 128].reshape(4, 2, 16, C))
        rim = dot(table["edges"][...], halo[t]).astype(BF)
        for sel, (pair, par) in enumerate(((0, 0), (0, 1), (17, 0))):
            for blk in range(4):
                start = sel * 64 + blk * 16
                x4[t, pair, par, :, blk * C:(blk + 1) * C] = rim[start:start + 16]
        side = dot(table["left"][...], halo[t])
        inner = dot(table["first_col"][...], own_rim[t])
        for i in range(3):
            for j in range(3):
                tap = 3 * i + j
                part = side[tap * LEFT:(tap + 1) * LEFT]
                if j == 2:
                    part = part + inner[i * LEFT:(i + 1) * LEFT]
                left_x[t * LEFT:(t + 1) * LEFT, tap * C:(tap + 1) * C] = part.astype(BF)

    own[0].wait()
    for copy in near[0]:
        copy.wait_recv()

    pre_left = dot(left_x[...], w1[...])
    row_id = lax.broadcasted_iota(jnp.int32, (LEFT, C), 0)
    hidden_left, above = [], []
    for t in range(2):
        p_row = jnp.floor(own_pos[t] * 0.25)
        has_left = jnp.where(own_pos[t] - 4.0 * p_row > 0.0, 1.0, 0.0)
        has_above = jnp.where(p_row > 0.0, 1.0, 0.0)
        above.append(has_above)
        v = pre_left[t * LEFT:(t + 1) * LEFT]
        keep = jnp.where(row_id == 0, has_left * has_above, has_left)
        hidden_left.append((v * sigmoid(v) * keep).astype(BF))

    def window(t, par, i, cp):
        row = par + i
        n = 17 - par
        return x4[t, row // 2:row // 2 + n, row % 2, :, cp * C:cp * C + 768].reshape(n * 16, 768)

    for t in range(2):
        if t == 1:
            far[5].wait_recv()
            near[1].append(forward(1, opposite, 3))
        for par in range(2):
            store = h_odd if par == 0 else h_even
            n = 17 - par
            for cp in range(2):
                patch = jnp.concatenate([window(t, par, i, cp) for i in range(3)], axis=1)
                pre = dot(patch, w1[...])
                sig = sigmoid(pre)
                act = pre * sig
                if par == 0:
                    own_row = lax.broadcasted_iota(jnp.int32, (272, C), 0) >= 16
                    act = jnp.where(own_row, act, act * above[t])
                act = act.astype(BF)
                if cp == 0:
                    store[t, :, :, C:2 * C] = act.reshape(n, 16, C)
                else:
                    store[t, :, :, 2 * C:] = act.reshape(n, 16, C)
                    moved = dot(table["shift"][:n * 16, :n * 16], act)
                    moved = moved + dot(table["from_left"][par, :n * 16], hidden_left[t])
                    store[t, :, :, :C] = moved.astype(BF).reshape(n, 16, C)
                if par == 0:
                    pre, sig = pre[16:], sig[16:]
                slopes[4 * t + 2 * par + cp] = sig * (1.0 + pre * (1.0 - sig))

    def hidden_rows(t, i):
        if i == 1:
            return h_even[t].reshape(256, 768)
        return h_odd[t, i // 2:i // 2 + 16].reshape(256, 768)

    def blocks(n):
        for yy in range(YN):
            for zz in range(ZN):
                start = OWN_ROWS * (zz * YN + yy)
                rows = g_f[start:start + OWN_ROWS, :]
                g[n, yy, zz] = jnp.concatenate([rows[:, :128], rows[:, 128:]], axis=0).astype(BF)

    def to_region(src, dst, send_sem, recv_sem, who):
        copy = pltpu.make_async_remote_copy(
            src_ref=src, dst_ref=dst, send_sem=send_sem, recv_sem=recv_sem,
            device_id={"region": who}, device_id_type=MESH)
        copy.start()
        return copy

    sent = []
    y_copies = {}

    def turn(oz):
        return 1 if oz % 2 == 0 else YN - 1

    def y_first(n):
        for kind in range(2):
            for oz in Z_ORDER:
                d = turn(oz)
                block = (y + 2) % YN if kind == 0 else (y + YN - d) % YN
                who = (y + d) % YN if kind == 0 else block
                buf = f_buf if kind == 0 else o_buf
                y_copies[n, kind, oz] = to_region(
                    g.at[n, block, (z + oz) % ZN], buf.at[n, oz],
                    y_s.at[kind, n, oz], y_r.at[kind, n, oz], z * YN + who)
                sent.append(y_copies[n, kind, oz])

    def y_second(n):
        for oz in Z_ORDER:
            who = (y + turn(oz)) % YN
            y_copies[n, 0, oz].wait_recv()
            summed = g[n, who, (z + oz) % ZN].astype(F32) + f_buf[n, oz].astype(F32)
            s_send[n, oz] = summed.astype(BF)
            y_copies[n, 2, oz] = to_region(
                s_send.at[n, oz], s_buf.at[n, oz], y_s.at[2, n, oz], y_r.at[2, n, oz], z * YN + who)
            sent.append(y_copies[n, 2, oz])

    def z_first(n):
        copies = []
        for oz in Z_ORDER:
            y_copies[n, 1, oz].wait_recv()
            y_copies[n, 2, oz].wait_recv()
            total = (g[n, y, (z + oz) % ZN].astype(F32) + o_buf[n, oz].astype(F32)) + s_buf[n, oz].astype(F32)
            if oz:
                z_send[n, oz - 1] = total.astype(BF)
                copies.append(to_region(
                    z_send.at[n, oz - 1], z_buf.at[n, oz - 1], zs.at[n, oz - 1], zr.at[n, oz - 1],
                    ((z + oz) % ZN) * YN + y))
        sent.extend(copies)
        return total, copies

    def z_second(n, total, copies):
        for at, copy in enumerate(copies):
            copy.wait_recv()
            total = total + z_buf[n, Z_ORDER[at] - 1].astype(F32)
        return total

    for i in range(3):
        for j in range(3):
            tap = 3 * i + j
            seen = jnp.concatenate([hidden_rows(t, i)[:, j * C:(j + 1) * C] for t in range(2)], axis=0)
            g_f[tap * C:(tap + 1) * C, :] = dot_l(seen, masked[...].reshape(512, C))
    blocks(1)
    y_first(1)

    own[1].wait()
    for copy in near[1]:
        copy.wait_recv()
    for t in range(2):
        patch = jnp.concatenate([hidden_rows(t, i) for i in range(3)], axis=1)
        feat[t] = dot(patch, w2[...]).astype(BF).reshape(16, 16, C)

    def second(tap):
        return w2[tap * C:(tap + 1) * C, :]

    up, down = slice(0, 256), slice(16, 272)
    for t in range(2):
        m0 = jnp.concatenate([masked[t], dot(table["below"][...], halo[t]).astype(BF)], axis=0)
        m1 = (dot(table["back"][...], masked[t]) + dot(table["beside"][...], halo[t])).astype(BF)
        spread = (
            dot_t(m0[up], second(7)) + dot_t(m0[down], second(1)),
            (dot_t(m0[up], second(8)) + dot_t(m1[up], second(6))
             + dot_t(m0[down], second(2)) + dot_t(m1[down], second(0))),
            dot_t(m0[up], second(4)),
            dot_t(m0[up], second(5)) + dot_t(m1[up], second(3)),
        )
        for n in range(4):
            group = 4 * t + n
            d_pre[group * 256:(group + 1) * 256, :] = (spread[n] * slopes[group]).astype(BF)

    y_second(1)

    def own_rows(t, par, i, cp, j):
        row = (2 if par == 0 else 1) + i
        lanes = (cp + j) * C
        return x4[t, row // 2:row // 2 + 16, row % 2, :, lanes:lanes + C].reshape(256, C)

    for i in range(3):
        for j in range(3):
            tap = 3 * i + j
            seen = jnp.concatenate(
                [own_rows(t, par, i, cp, j) for t in range(2) for par in range(2) for cp in range(2)], axis=0)
            g_f[tap * C:(tap + 1) * C, :] = dot_l(seen, d_pre[...])
    blocks(0)
    y_first(0)
    z_left = z_first(1)
    y_second(0)
    total_second = z_second(1, *z_left)
    total_first = z_second(0, *z_first(0))

    squares = jnp.sum(total_first * total_first + total_second * total_second, axis=0, keepdims=True)
    n_send[0] = squares
    all_to_all(5, lambda to: n_send.at[0], lambda me: n_buf.at[me])
    n_buf[r] = squares
    for n, total in enumerate((total_first, total_second)):
        turned = jnp.concatenate([total[:OWN_ROWS].T, total[OWN_ROWS:].T], axis=0)
        x_send[:, n] = turned.reshape(SC, 32, OWN_ROWS)
    x_copies = []
    for o in range(1, SC):
        to = (s + o) % SC
        x_copies.append(to_scene(x_send.at[to], x_buf.at[o - 1], xs.at[o - 1], xr.at[o - 1], to))
    await_all(n_buf.at[pl.ds(0, REG - 1)], a2a_r.at[5])
    sum_sq = jnp.sum(n_buf[...].reshape(REG, 128), keepdims=True)
    factor = (3.0 * C * math.sqrt(2.0) / SC) / (jnp.sqrt(sum_sq) + 0.01)
    c_send[0] = jnp.broadcast_to(factor, (1, 128))
    c_copies = []
    for o in range(1, SC):
        to = (s + o) % SC
        c_copies.append(to_scene(c_send.at[0], c_buf.at[o - 1], cs.at[o - 1], cr.at[o - 1], to))
    result = x_send[s] * factor.reshape(1, 1, 1)
    for o in range(1, SC):
        x_copies[o - 1].wait_recv()
        c_copies[o - 1].wait_recv()
        result = result + x_buf[o - 1] * c_buf[o - 1][:, :1].reshape(1, 1, 1)
    out[...] = result

    for copy in far + near[0] + near[1] + sent + x_copies + c_copies:
        copy.wait_send()
    await_all(pos_buf.at[pl.ds(0, 2 * REG - 2)], a2a_s.at[0])
    for half in range(2):
        await_all(send1.at[half, pl.ds(0, REG - 1)], a2a_s.at[1 + half])
        await_all(send2.at[half, pl.ds(0, REG - 1)], a2a_s.at[3 + half])
    await_all(n_buf.at[pl.ds(0, REG - 1)], a2a_s.at[5])


NAMES = ("rim", "rim_grad", "body", "sides", "edges", "left", "first_col", "shift", "from_left",
         "back", "below", "beside")
TABLES = dict(zip(NAMES, place_tables()))


def level(positions, clear, tiles, cotangent, w1, w2):
    vmem = pl.BlockSpec(memory_space=pltpu.VMEM)
    anywhere = pl.BlockSpec(memory_space=pl.ANY)
    dma = pltpu.SemaphoreType.DMA
    tables = list(TABLES.values())
    part = (144, 128)
    return pl.pallas_call(
        level_kernel,
        name="level",
        out_shape=(jax.ShapeDtypeStruct((2, 16, 16, C), BF), jax.ShapeDtypeStruct((2, 32, OWN_ROWS), F32)),
        in_specs=[anywhere] * (6 + len(tables)),
        out_specs=(vmem, vmem),
        scratch_shapes=[pltpu.VMEM(t.shape, BF) for t in tables] + [
            pltpu.VMEM((1, 2), jnp.int32), pltpu.VMEM((1, 2), jnp.int32),
            pltpu.VMEM((2, 32, 32, C), BF), pltpu.VMEM((2, 16, 16, C), BF),
            dma((4,)), dma((len(tables),)),
            pltpu.VMEM((2, 1, 128), F32), pltpu.VMEM((2 * REG, 1, 128), F32),
            pltpu.VMEM((2, REG, 16, 128), BF), pltpu.VMEM((2, REG, 16, 128), BF),
            pltpu.VMEM((2, REG, 16, 128), BF), pltpu.VMEM((2, REG, 16, 128), BF),
            pltpu.VMEM((2, 256, C), BF), pltpu.VMEM((2, 256, C), BF), pltpu.VMEM((2, 256, C), BF),
            pltpu.VMEM((ROWS, C), BF), pltpu.VMEM((ROWS, C), BF),
            pltpu.VMEM((2, 18, 2, 16, 4 * C), BF),
            pltpu.VMEM((2, 17, 16, 3 * C), BF), pltpu.VMEM((2, 16, 16, 3 * C), BF),
            pltpu.VMEM((2 * LEFT, ROWS), BF),
            pltpu.VMEM((8, 256, C), F32),
            pltpu.VMEM((2048, C), BF),
            pltpu.VMEM((ROWS, C), F32),
            pltpu.VMEM((2, YN, ZN) + part, BF),
            pltpu.VMEM((2, ZN) + part, BF), pltpu.VMEM((2, ZN) + part, BF),
            pltpu.VMEM((2, ZN) + part, BF), pltpu.VMEM((2, ZN) + part, BF),
            pltpu.VMEM((2, ZN - 1) + part, BF), pltpu.VMEM((2, ZN - 1) + part, BF),
            pltpu.VMEM((1, 1, 128), F32), pltpu.VMEM((REG, 1, 128), F32),
            pltpu.VMEM((SC, 2, 32, OWN_ROWS), F32), pltpu.VMEM((SC - 1, 2, 32, OWN_ROWS), F32),
            pltpu.VMEM((1, 1, 128), F32), pltpu.VMEM((SC - 1, 1, 128), F32),
            dma((6,)), dma((6,)), dma((2, 3)), dma((2, 3)), dma((2, 4)), dma((2, 4)),
            dma((3, 2, ZN)), dma((3, 2, ZN)), dma((2, ZN - 1)), dma((2, ZN - 1)),
            dma((SC - 1,)), dma((SC - 1,)), dma((SC - 1,)), dma((SC - 1,)), dma((2,)),
        ],
        compiler_params=pltpu.CompilerParams(
            collective_id=0, has_side_effects=True, vmem_limit_bytes=VMEM_LIMIT),
    )(positions, clear, tiles, cotangent, w1, w2, *[jnp.asarray(t) for t in tables])


def local(tiles, cotangent, positions, clear, w_first, w_second):
    feat, out = level(positions, clear, tiles[0], cotangent[0], w_first, w_second)
    return feat[None], out[0].T, out[1].T


def solution(mesh):
    in_specs = (
        P("scene", "region", None, None, None),
        P("scene", "region", None, None, None),
        P("scene", "region"),
        P("scene", "region"),
        P("scene", None),
        P("scene", None),
    )
    out_specs = (P("scene", "region", None, None, None), P("region", "scene"), P("region", "scene"))
    return jax.shard_map(local, mesh=mesh, in_specs=in_specs, out_specs=out_specs, check_vma=False)
```

```python
import math

import jax
import jax.numpy as jnp
import ml_dtypes
import numpy as np
from jax import lax
from jax.experimental import pallas as pl
from jax.experimental.pallas import tpu as pltpu
from jax.sharding import PartitionSpec as P

MESH = pl.DeviceIdType.MESH
BF = jnp.bfloat16
F32 = jnp.float32
GW, GH = 4, 16
C = 256
REG, ZN, YN, SC = 32, 8, 4, 8
WROWS = 288
LEFT = 48
ROWS = 9 * C
OWN_ROWS = ROWS // REG
VMEM_LIMIT = 56 * 1024 * 1024


def hot(rows, cols, pairs):
    out = np.zeros((rows, cols), np.float32)
    for row, col in pairs:
        out[row, col] = 1.0
    return out.astype(ml_dtypes.bfloat16)


def place_tables():
    tile = lambda h, w: 32 * h + w
    corner = ((30, 30), (30, 31), (31, 30), (31, 31), (30, 0), (31, 0), (0, 30), (0, 31), (0, 0))
    rim = hot(256, 1024, [
        (8 * k + q, px) for k in range(32) for q, px in enumerate((
            tile(31, k), tile(30, k), tile(k, 31), tile(k, 30), tile(0, k), tile(k, 0)))
    ] + [(8 * k + 7, tile(*at)) for k, at in enumerate(corner)])
    rim_grad = hot(256, 256, [(8 * k + 6, k if k < 16 else 16 * (k - 16)) for k in range(32)] + [(79, 0)])

    cols = lambda blk, b: 2 * b - 1 + blk
    order = (1, 2, 0, 3)
    body = hot(512, 256, [
        (at * 128 + h * 16 + b, h * 32 + cols(blk, b))
        for at, blk in enumerate(order) for h in range(8) for b in range(16) if 0 <= cols(blk, b) < 32
    ])
    sides = hot(256, 64, [(h * 16, 8 * h + 2) for h in range(8)]
                + [(128 + h * 16 + 15, 8 * h + 5) for h in range(8)])
    edge_q = (1, 0, 4)
    corner_left, corner_right = (1, 3, 7), (4, 5, 8)

    def edge_source(sel, col):
        if col < 0:
            return 8 * corner_left[sel] + 7
        if col > 31:
            return 8 * corner_right[sel] + 7
        return 8 * col + edge_q[sel]

    edges = hot(192, 256, [
        (sel * 64 + blk * 16 + b, edge_source(sel, cols(blk, b)))
        for sel in range(3) for blk in range(4) for b in range(16)
    ])

    def left_source(hh, j):
        if 0 <= hh < 32:
            return 8 * hh + (3, 2)[j] if j < 2 else None
        sel = {-2: 0, -1: 1, 32: 2}[hh]
        if j < 2:
            return 8 * ((0, 1), (2, 3), (6, 7))[sel][j] + 7
        return edge_q[sel]

    left = hot(9 * LEFT, 256, [
        ((3 * i + j) * LEFT + g, left_source(g + i - 2, j))
        for i in range(3) for j in range(3) for g in range(33)
        if left_source(g + i - 2, j) is not None
    ])
    first_col = hot(3 * LEFT, 256, [
        (i * LEFT + g, 8 * (g + i - 2) + 5) for i in range(3) for g in range(33) if 0 <= g + i - 2 < 32
    ])
    shift = hot(272, 272, [(a * 16 + b, a * 16 + b - 1) for a in range(17) for b in range(1, 16)])
    from_left = np.stack([
        hot(272, LEFT, [(a * 16, 2 * a + par) for a in range(17 - par)]) for par in range(2)
    ])
    back = hot(272, 256, [(a * 16 + b, a * 16 + b + 1) for a in range(16) for b in range(15)])
    below = hot(16, 256, [(b, 8 * b + 6) for b in range(16)])
    beside = hot(272, 256, [(a * 16 + 15, 8 * (16 + a) + 6) for a in range(16)]
                 + [(256 + b, 8 * (b + 1) + 6) for b in range(15)] + [(271, 79)])
    return rim, rim_grad, body, sides, edges, left, first_col, shift, from_left, back, below, beside


def dot(a, b):
    return jnp.dot(a, b, preferred_element_type=F32)


def dot_t(a, b):
    return lax.dot_general(a, b, (((1,), (1,)), ((), ())), preferred_element_type=F32)


def dot_l(a, b):
    return lax.dot_general(a, b, (((0,), (0,)), ((), ())), preferred_element_type=F32)


def sigmoid(v):
    return 0.5 * jnp.tanh(0.5 * v) + 0.5


def route_rows(pos, r):
    lane = lax.broadcasted_iota(jnp.int32, (512, 128), 1).astype(F32)
    q = lax.broadcasted_iota(jnp.int32, (512, 128), 0) % 8
    zero = jnp.zeros((512, 128), F32)
    k = zero.astype(jnp.int32) + r
    grad_row = jnp.where(k < 16, 1.0, 0.0)
    corner_row = jnp.where(k < 6, -1.0, 1.0)
    corner_col = jnp.where((k < 4) | (k == 6) | (k == 7), -1.0, 1.0)
    d_row = jnp.where(q < 2, -1.0, jnp.where(q == 4, 1.0, zero))
    d_row = jnp.where(q == 6, grad_row, jnp.where(q == 7, corner_row, d_row))
    d_col = jnp.where((q == 2) | (q == 3), -1.0, jnp.where(q == 5, 1.0, zero))
    d_col = jnp.where(q == 6, 1.0 - grad_row, jnp.where(q == 7, corner_col, d_col))
    p_row = jnp.floor(pos * 0.25)
    n_row = p_row + d_row
    n_col = pos - 4.0 * p_row + d_col
    inside = (n_row >= 0.0) & (n_row < GH) & (n_col >= 0.0) & (n_col < GW)
    want = jnp.where(inside, 4.0 * n_row + n_col, -1.0)
    has = jnp.where(pos == lane, 1.0, 0.0).astype(BF)
    wants = jnp.where(want == lane, 1.0, 0.0).astype(BF)
    same = (lax.broadcasted_iota(jnp.int32, (512, 512), 0) % 8) == (
        lax.broadcasted_iota(jnp.int32, (512, 512), 1) % 8)
    return jnp.where(same, dot_t(wants, has), 0.0).astype(BF)


Z_PART = 32
Z_ORDER = (4, 3, 5, 2, 6, 1, 7, 0)


def level_kernel(positions_hbm, clear_hbm, tiles_hbm, cotangent_hbm, w1_here, w2_here, *refs):
    names = list(TABLES)
    table_hbm = dict(zip(names, refs[:len(names)]))
    feat_hbm, out = refs[len(names):len(names) + 2]
    refs = refs[len(names) + 2:]
    table = dict(zip(names, refs[:len(names)]))
    (positions, clear, tiles, cotangent, feat, feat_sem, in_sem, table_sem, pos_send, pos_buf, send1, recv1, send2, recv2, masked, own_rim, halo, w1, w2,
     x4, h_odd, h_even, left_x, slopes, d_pre, g_f, g, f_buf, o_buf, s_buf, s_send, z_send, z_buf,
     other_z, other_sum, other_send, other_y, n_send, n_buf, x_send, x_buf, c_send, c_buf,
     a2a_s, a2a_r, w_s, w_r, v_s, v_r, y_s, y_r, zs, zr, o_s, o_r, xs, xr, cs, cr, own_sem) = refs[len(names):]

    s = lax.axis_index("scene")
    r = lax.axis_index("region")
    z, y = r // YN, r % YN
    sib = s + 1 - 2 * (s % 2)

    arrays = [pltpu.make_async_copy(src, dst, in_sem.at[n]) for n, (src, dst) in enumerate((
        (positions_hbm, positions), (clear_hbm, clear), (tiles_hbm, tiles), (cotangent_hbm, cotangent)))]
    for copy in arrays:
        copy.start()
    loads = {name: pltpu.make_async_copy(table_hbm[name], table[name], table_sem.at[n])
             for n, name in enumerate(names)}
    for name in names:
        loads[name].start()

    barrier = pltpu.get_barrier_semaphore()

    def far_first(o):
        step, turn_y = o // YN, o % YN
        dz = ZN // 2 + ((step + 1) // 2) * (1 - 2 * (step % 2))
        dy = YN // 2 + ((turn_y + 1) // 2) * (1 - 2 * (turn_y % 2))
        return ((z + dz) % ZN) * YN + (y + dy) % YN

    def greet(o, carry):
        pl.semaphore_signal(barrier, inc=1, device_id={"region": far_first(o)}, device_id_type=MESH)
        return carry

    lax.fori_loop(0, REG - 1, greet, 0)
    for o in range(1, SC):
        pl.semaphore_signal(barrier, inc=1, device_id={"scene": (s + o) % SC}, device_id_type=MESH)

    def w_rows(ref, who):
        return ref.at[pl.ds(pl.multiple_of(who * WROWS, 32), WROWS)]

    weights = ((w1_here, w1), (w2_here, w2))
    own = [pltpu.make_async_copy(src, w_rows(dst, s), own_sem.at[n]) for n, (src, dst) in enumerate(weights)]
    for copy in own:
        copy.start()

    def all_to_all(n, src, dst):
        def send(o, carry):
            to = far_first(o)
            pltpu.make_async_remote_copy(
                src_ref=src(to), dst_ref=dst(r), send_sem=a2a_s.at[n], recv_sem=a2a_r.at[n],
                device_id={"region": to}, device_id_type=MESH).start()
            return carry

        lax.fori_loop(0, REG - 1, send, 0)

    def await_all(buf, sem):
        pltpu.make_async_copy(buf, buf, sem).wait()

    for copy in arrays[:2]:
        copy.wait()
    own_pos = [positions[0:1, t:t + 1].astype(F32) for t in range(2)]
    for t in range(2):
        pos_send[t] = jnp.broadcast_to(own_pos[t], (1, 128))
    pl.semaphore_wait(barrier, REG - 1 + SC - 1)

    right, left_chip = (s + 2) % SC, (s + 6) % SC

    def to_scene(src, dst, send_sem, recv_sem, who):
        copy = pltpu.make_async_remote_copy(
            src_ref=src, dst_ref=dst, send_sem=send_sem, recv_sem=recv_sem,
            device_id={"scene": who}, device_id_type=MESH)
        copy.start()
        return copy

    all_to_all(0, lambda to: pos_send, lambda me: pos_buf.at[pl.ds(2 * me, 2)])
    far, near = [], []

    def send_weights(n):
        src, dst = weights[n]
        far.append(to_scene(src, w_rows(dst, s), w_s.at[n, 0], w_r.at[n, 0], right))
        far.append(to_scene(src, w_rows(dst, s), w_s.at[n, 1], w_r.at[n, 1], left_chip))
        near.append([to_scene(src, w_rows(dst, s), v_s.at[n, 0], v_r.at[n, 0], sib)])

    send_weights(0)

    for copy in arrays[2:]:
        copy.wait()
    for t in range(2):
        kept = clear[0:1, t:t + 1].astype(F32)
        masked[t] = (cotangent[t].reshape(256, C).astype(F32) * kept).astype(BF)
    loads["rim"].wait()
    loads["rim_grad"].wait()
    rims = []
    for t in range(2):
        rim = dot(table["rim"][...], tiles[t].reshape(1024, C)) + dot(table["rim_grad"][...], masked[t])
        own_rim[t] = rim.astype(BF)
        rims.append(rim.reshape(REG, 8, C))
    rims = jnp.concatenate(rims, axis=1).astype(BF)
    for half in range(2):
        send1[half] = rims[:, :, half * 128:(half + 1) * 128]
        all_to_all(1 + half, lambda to: send1.at[half, to], lambda me: recv1.at[half, me])
    for half in range(2):
        recv1[half, r] = send1[half, r]
    for t in range(2):
        pos_buf[2 * r + t] = pos_send[t]

    loads["body"].wait()
    for t in range(2):
        for c in range(4):
            chunk = tiles[t, 8 * c:8 * c + 8].reshape(256, C)
            got = dot(table["body"][:256], chunk).astype(BF)
            for at, blk in enumerate((1, 2)):
                x4[t, 4 * c + 1:4 * c + 5, :, :, blk * C:(blk + 1) * C] = (
                    got[at * 128:(at + 1) * 128].reshape(4, 2, 16, C))

    def forward(n, came, at):
        rows = w_rows(weights[n][1], came)
        return to_scene(rows, rows, v_s.at[n, at], v_r.at[n, at], sib)

    opposite = (s + 4) % SC
    far[0].wait_recv()
    rows = w_rows(w1, left_chip)
    far.append(to_scene(rows, rows, w_s.at[0, 2], w_r.at[0, 2], right))
    near[0].append(forward(0, left_chip, 1))
    far[1].wait_recv()
    near[0].append(forward(0, right, 2))
    send_weights(1)
    await_all(pos_buf.at[pl.ds(0, 2 * REG - 2)], a2a_r.at[0])
    route = route_rows(jnp.broadcast_to(pos_buf[...], (64, 8, 128)).reshape(512, 128), r)
    for half in range(2):
        await_all(recv1.at[half, pl.ds(0, REG - 1)], a2a_r.at[1 + half])
        send2[half] = dot(route, recv1[half].reshape(512, 128)).astype(BF).reshape(REG, 16, 128)
        all_to_all(3 + half, lambda to: send2.at[half, to], lambda me: recv2.at[half, me])
    for half in range(2):
        recv2[half, r] = send2[half, r]

    for name in names[3:]:
        loads[name].wait()
    far[2].wait_recv()
    near[0].append(forward(0, opposite, 3))
    far[3].wait_recv()
    near[1].append(forward(1, left_chip, 1))
    far[4].wait_recv()
    rows = w_rows(w2, right)
    far.append(to_scene(rows, rows, w_s.at[1, 2], w_r.at[1, 2], left_chip))
    near[1].append(forward(1, right, 2))
    for half in range(2):
        await_all(recv2.at[half, pl.ds(0, REG - 1)], a2a_r.at[3 + half])
        came = recv2[half].astype(F32)
        for t in range(2):
            halo[t, :, half * 128:(half + 1) * 128] = came[:, 8 * t:8 * t + 8].reshape(256, 128).astype(BF)
    for t in range(2):
        for c in range(4):
            chunk = tiles[t, 8 * c:8 * c + 8].reshape(256, C)
            got = dot(table["body"][256:], chunk) + dot(table["sides"][...], halo[t, 64 * c:64 * c + 64])
            got = got.astype(BF)
            for at, blk in enumerate((0, 3)):
                x4[t, 4 * c + 1:4 * c + 5, :, :, blk * C:(blk + 1) * C] = (
                    got[at * 128:(at + 1) * 128].reshape(4, 2, 16, C))
        rim = dot(table["edges"][...], halo[t]).astype(BF)
        for sel, (pair, par) in enumerate(((0, 0), (0, 1), (17, 0))):
            for blk in range(4):
                start = sel * 64 + blk * 16
                x4[t, pair, par, :, blk * C:(blk + 1) * C] = rim[start:start + 16]
        side = dot(table["left"][...], halo[t])
        inner = dot(table["first_col"][...], own_rim[t])
        for i in range(3):
            for j in range(3):
                tap = 3 * i + j
                part = side[tap * LEFT:(tap + 1) * LEFT]
                if j == 2:
                    part = part + inner[i * LEFT:(i + 1) * LEFT]
                left_x[t * LEFT:(t + 1) * LEFT, tap * C:(tap + 1) * C] = part.astype(BF)

    own[0].wait()
    for copy in near[0]:
        copy.wait_recv()

    pre_left = dot(left_x[...], w1[...])
    row_id = lax.broadcasted_iota(jnp.int32, (LEFT, C), 0)
    hidden_left, above = [], []
    for t in range(2):
        p_row = jnp.floor(own_pos[t] * 0.25)
        has_left = jnp.where(own_pos[t] - 4.0 * p_row > 0.0, 1.0, 0.0)
        has_above = jnp.where(p_row > 0.0, 1.0, 0.0)
        above.append(has_above)
        v = pre_left[t * LEFT:(t + 1) * LEFT]
        keep = jnp.where(row_id == 0, has_left * has_above, has_left)
        hidden_left.append((v * sigmoid(v) * keep).astype(BF))

    def window(t, par, i, cp):
        row = par + i
        n = 17 - par
        return x4[t, row // 2:row // 2 + n, row % 2, :, cp * C:cp * C + 768].reshape(n * 16, 768)

    for t in range(2):
        if t == 1:
            far[5].wait_recv()
            near[1].append(forward(1, opposite, 3))
        for par in range(2):
            store = h_odd if par == 0 else h_even
            n = 17 - par
            for cp in range(2):
                patch = jnp.concatenate([window(t, par, i, cp) for i in range(3)], axis=1)
                pre = dot(patch, w1[...])
                sig = sigmoid(pre)
                act = pre * sig
                if par == 0:
                    own_row = lax.broadcasted_iota(jnp.int32, (272, C), 0) >= 16
                    act = jnp.where(own_row, act, act * above[t])
                act = act.astype(BF)
                if cp == 0:
                    store[t, :, :, C:2 * C] = act.reshape(n, 16, C)
                else:
                    store[t, :, :, 2 * C:] = act.reshape(n, 16, C)
                    moved = dot(table["shift"][:n * 16, :n * 16], act)
                    moved = moved + dot(table["from_left"][par, :n * 16], hidden_left[t])
                    store[t, :, :, :C] = moved.astype(BF).reshape(n, 16, C)
                if par == 0:
                    pre, sig = pre[16:], sig[16:]
                slopes[4 * t + 2 * par + cp] = sig * (1.0 + pre * (1.0 - sig))

    def hidden_rows(t, i):
        if i == 1:
            return h_even[t].reshape(256, 768)
        return h_odd[t, i // 2:i // 2 + 16].reshape(256, 768)

    def blocks(n):
        for yy in range(YN):
            for zz in range(ZN):
                start = OWN_ROWS * (zz * YN + yy)
                rows = g_f[start:start + OWN_ROWS, :]
                g[n, yy, zz] = jnp.concatenate([rows[:, :128], rows[:, 128:]], axis=0).astype(BF)

    def to_region(src, dst, send_sem, recv_sem, who):
        copy = pltpu.make_async_remote_copy(
            src_ref=src, dst_ref=dst, send_sem=send_sem, recv_sem=recv_sem,
            device_id={"region": who}, device_id_type=MESH)
        copy.start()
        return copy

    sent = []
    y_copies = {}
    held = (144, 144 - Z_PART)

    def turn(oz):
        return 1 if oz % 2 == 0 else YN - 1

    def y_first(n):
        for kind in range(2):
            for oz in Z_ORDER:
                d = turn(oz)
                block = (y + 2) % YN if kind == 0 else (y + YN - d) % YN
                who = (y + d) % YN if kind == 0 else block
                buf = f_buf if kind == 0 else o_buf
                y_copies[n, kind, oz] = to_region(
                    g.at[n, block, (z + oz) % ZN, pl.ds(0, held[n])], buf.at[n, oz, pl.ds(0, held[n])],
                    y_s.at[kind, n, oz], y_r.at[kind, n, oz], z * YN + who)
                sent.append(y_copies[n, kind, oz])

    def y_second(n):
        for oz in Z_ORDER:
            who = (y + turn(oz)) % YN
            y_copies[n, 0, oz].wait_recv()
            summed = g[n, who, (z + oz) % ZN, :held[n]].astype(F32) + f_buf[n, oz, :held[n]].astype(F32)
            s_send[n, oz, :held[n]] = summed.astype(BF)
            y_copies[n, 2, oz] = to_region(
                s_send.at[n, oz, pl.ds(0, held[n])], s_buf.at[n, oz, pl.ds(0, held[n])], y_s.at[2, n, oz], y_r.at[2, n, oz], z * YN + who)
            sent.append(y_copies[n, 2, oz])

    def z_first(n):
        copies = []
        for oz in Z_ORDER:
            y_copies[n, 1, oz].wait_recv()
            y_copies[n, 2, oz].wait_recv()
            total = g[n, y, (z + oz) % ZN, :held[n]].astype(F32) + o_buf[n, oz, :held[n]].astype(F32)
            total = total + s_buf[n, oz, :held[n]].astype(F32)
            if oz:
                z_send[n, oz - 1, :held[n]] = total.astype(BF)
                copies.append(to_region(
                    z_send.at[n, oz - 1, pl.ds(0, held[n])], z_buf.at[n, oz - 1, pl.ds(0, held[n])], zs.at[n, oz - 1], zr.at[n, oz - 1],
                    ((z + oz) % ZN) * YN + y))
        sent.extend(copies)
        return total, copies

    def z_second(n, total, copies):
        for at, copy in enumerate(copies):
            copy.wait_recv()
            total = total + z_buf[n, Z_ORDER[at] - 1, :held[n]].astype(F32)
        return total

    def other_first():
        copies = [to_region(
            g.at[1, :, (z + oz) % ZN, pl.ds(held[1], Z_PART)], other_z.at[oz - 1],
            o_s.at[oz - 1], o_r.at[oz - 1], ((z + oz) % ZN) * YN + y) for oz in Z_ORDER[:-1]]
        sent.extend(copies)
        return copies

    def other_second(copies):
        total = g[1, :, z, held[1]:].astype(F32)
        for at, copy in enumerate(copies):
            copy.wait_recv()
            total = total + other_z[Z_ORDER[at] - 1].astype(F32)
        other_sum[...] = total
        other_send[...] = total.astype(BF)
        copies = [to_region(
            other_send.at[(y + o) % YN], other_y.at[o - 1], o_s.at[ZN + o - 2], o_r.at[ZN + o - 2],
            z * YN + (y + o) % YN) for o in range(1, YN)]
        sent.extend(copies)
        return copies

    def other_third(copies):
        total = other_sum[y]
        for at, copy in enumerate(copies):
            copy.wait_recv()
            total = total + other_y[at].astype(F32)
        return total

    for i in range(3):
        for j in range(3):
            tap = 3 * i + j
            seen = jnp.concatenate([hidden_rows(t, i)[:, j * C:(j + 1) * C] for t in range(2)], axis=0)
            g_f[tap * C:(tap + 1) * C, :] = dot_l(seen, masked[...].reshape(512, C))
    blocks(1)
    y_first(1)
    other = other_first()

    own[1].wait()
    for copy in near[1]:
        copy.wait_recv()
    for t in range(2):
        patch = jnp.concatenate([hidden_rows(t, i) for i in range(3)], axis=1)
        feat[t] = dot(patch, w2[...]).astype(BF).reshape(16, 16, C)
    feat_copy = pltpu.make_async_copy(feat, feat_hbm, feat_sem)
    feat_copy.start()

    def second(tap):
        return w2[tap * C:(tap + 1) * C, :]

    up, down = slice(0, 256), slice(16, 272)
    for t in range(2):
        m0 = jnp.concatenate([masked[t], dot(table["below"][...], halo[t]).astype(BF)], axis=0)
        m1 = (dot(table["back"][...], masked[t]) + dot(table["beside"][...], halo[t])).astype(BF)
        spread = (
            dot_t(m0[up], second(7)) + dot_t(m0[down], second(1)),
            (dot_t(m0[up], second(8)) + dot_t(m1[up], second(6))
             + dot_t(m0[down], second(2)) + dot_t(m1[down], second(0))),
            dot_t(m0[up], second(4)),
            dot_t(m0[up], second(5)) + dot_t(m1[up], second(3)),
        )
        for n in range(4):
            group = 4 * t + n
            d_pre[group * 256:(group + 1) * 256, :] = (spread[n] * slopes[group]).astype(BF)

    y_second(1)

    def own_rows(t, par, i, cp, j):
        row = (2 if par == 0 else 1) + i
        lanes = (cp + j) * C
        return x4[t, row // 2:row // 2 + 16, row % 2, :, lanes:lanes + C].reshape(256, C)

    for i in range(3):
        for j in range(3):
            tap = 3 * i + j
            seen = jnp.concatenate(
                [own_rows(t, par, i, cp, j) for t in range(2) for par in range(2) for cp in range(2)], axis=0)
            g_f[tap * C:(tap + 1) * C, :] = dot_l(seen, d_pre[...])
    blocks(0)
    y_first(0)
    other = other_second(other)
    z_left = z_first(1)
    y_second(0)
    total_second = jnp.concatenate([z_second(1, *z_left), other_third(other)], axis=0)
    total_first = z_second(0, *z_first(0))

    squares = jnp.sum(total_first * total_first + total_second * total_second, axis=0, keepdims=True)
    n_send[0] = squares
    all_to_all(5, lambda to: n_send.at[0], lambda me: n_buf.at[me])
    n_buf[r] = squares
    for n, total in enumerate((total_first, total_second)):
        turned = jnp.concatenate([total[:OWN_ROWS].T, total[OWN_ROWS:].T], axis=0)
        x_send[:, n] = turned.reshape(SC, 32, OWN_ROWS)
    x_copies = []
    for o in range(1, SC):
        to = (s + o) % SC
        x_copies.append(to_scene(x_send.at[to], x_buf.at[o - 1], xs.at[o - 1], xr.at[o - 1], to))
    await_all(n_buf.at[pl.ds(0, REG - 1)], a2a_r.at[5])
    sum_sq = jnp.sum(n_buf[...].reshape(REG, 128), keepdims=True)
    factor = (3.0 * C * math.sqrt(2.0) / SC) / (jnp.sqrt(sum_sq) + 0.01)
    c_send[0] = jnp.broadcast_to(factor, (1, 128))
    c_copies = []
    for o in range(1, SC):
        to = (s + o) % SC
        c_copies.append(to_scene(c_send.at[0], c_buf.at[o - 1], cs.at[o - 1], cr.at[o - 1], to))
    result = x_send[s] * factor.reshape(1, 1, 1)
    for o in range(1, SC):
        x_copies[o - 1].wait_recv()
        c_copies[o - 1].wait_recv()
        result = result + x_buf[o - 1] * c_buf[o - 1][:, :1].reshape(1, 1, 1)
    out[...] = result
    feat_copy.wait()

    for copy in far + near[0] + near[1] + sent + x_copies + c_copies:
        copy.wait_send()
    await_all(pos_buf.at[pl.ds(0, 2 * REG - 2)], a2a_s.at[0])
    for half in range(2):
        await_all(send1.at[half, pl.ds(0, REG - 1)], a2a_s.at[1 + half])
        await_all(send2.at[half, pl.ds(0, REG - 1)], a2a_s.at[3 + half])
    await_all(n_buf.at[pl.ds(0, REG - 1)], a2a_s.at[5])


NAMES = ("rim", "rim_grad", "body", "sides", "edges", "left", "first_col", "shift", "from_left",
         "back", "below", "beside")
TABLES = dict(zip(NAMES, place_tables()))


def level(positions, clear, tiles, cotangent, w1, w2):
    vmem = pl.BlockSpec(memory_space=pltpu.VMEM)
    anywhere = pl.BlockSpec(memory_space=pl.ANY)
    dma = pltpu.SemaphoreType.DMA
    tables = list(TABLES.values())
    part = (144, 128)
    return pl.pallas_call(
        level_kernel,
        name="level",
        out_shape=(jax.ShapeDtypeStruct((2, 16, 16, C), BF), jax.ShapeDtypeStruct((2, 32, OWN_ROWS), F32)),
        in_specs=[anywhere] * (6 + len(tables)),
        out_specs=(anywhere, vmem),
        scratch_shapes=[pltpu.VMEM(t.shape, BF) for t in tables] + [
            pltpu.VMEM((1, 2), jnp.int32), pltpu.VMEM((1, 2), jnp.int32),
            pltpu.VMEM((2, 32, 32, C), BF), pltpu.VMEM((2, 16, 16, C), BF),
            pltpu.VMEM((2, 16, 16, C), BF), dma, dma((4,)), dma((len(tables),)),
            pltpu.VMEM((2, 1, 128), F32), pltpu.VMEM((2 * REG, 1, 128), F32),
            pltpu.VMEM((2, REG, 16, 128), BF), pltpu.VMEM((2, REG, 16, 128), BF),
            pltpu.VMEM((2, REG, 16, 128), BF), pltpu.VMEM((2, REG, 16, 128), BF),
            pltpu.VMEM((2, 256, C), BF), pltpu.VMEM((2, 256, C), BF), pltpu.VMEM((2, 256, C), BF),
            pltpu.VMEM((ROWS, C), BF), pltpu.VMEM((ROWS, C), BF),
            pltpu.VMEM((2, 18, 2, 16, 4 * C), BF),
            pltpu.VMEM((2, 17, 16, 3 * C), BF), pltpu.VMEM((2, 16, 16, 3 * C), BF),
            pltpu.VMEM((2 * LEFT, ROWS), BF),
            pltpu.VMEM((8, 256, C), F32),
            pltpu.VMEM((2048, C), BF),
            pltpu.VMEM((ROWS, C), F32),
            pltpu.VMEM((2, YN, ZN) + part, BF),
            pltpu.VMEM((2, ZN) + part, BF), pltpu.VMEM((2, ZN) + part, BF),
            pltpu.VMEM((2, ZN) + part, BF), pltpu.VMEM((2, ZN) + part, BF),
            pltpu.VMEM((2, ZN - 1) + part, BF), pltpu.VMEM((2, ZN - 1) + part, BF),
            pltpu.VMEM((ZN - 1, YN, Z_PART, 128), BF), pltpu.VMEM((YN, Z_PART, 128), F32),
            pltpu.VMEM((YN, Z_PART, 128), BF), pltpu.VMEM((YN - 1, Z_PART, 128), BF),
            pltpu.VMEM((1, 1, 128), F32), pltpu.VMEM((REG, 1, 128), F32),
            pltpu.VMEM((SC, 2, 32, OWN_ROWS), F32), pltpu.VMEM((SC - 1, 2, 32, OWN_ROWS), F32),
            pltpu.VMEM((1, 1, 128), F32), pltpu.VMEM((SC - 1, 1, 128), F32),
            dma((6,)), dma((6,)), dma((2, 3)), dma((2, 3)), dma((2, 4)), dma((2, 4)),
            dma((3, 2, ZN)), dma((3, 2, ZN)), dma((2, ZN - 1)), dma((2, ZN - 1)), dma((ZN + YN - 2,)), dma((ZN + YN - 2,)),
            dma((SC - 1,)), dma((SC - 1,)), dma((SC - 1,)), dma((SC - 1,)), dma((2,)),
        ],
        compiler_params=pltpu.CompilerParams(
            collective_id=0, has_side_effects=True, vmem_limit_bytes=VMEM_LIMIT),
    )(positions, clear, tiles, cotangent, w1, w2, *[jnp.asarray(t) for t in tables])


def finish_kernel(feat_in, out_in, feat, first, second):
    feat[...] = feat_in[...]
    first[...] = out_in[0]
    second[...] = out_in[1]


def finish(feat, out):
    vmem = pl.BlockSpec(memory_space=pltpu.VMEM)
    share = jax.ShapeDtypeStruct((32, OWN_ROWS), F32)
    return pl.pallas_call(
        finish_kernel,
        name="finish",
        out_shape=(jax.ShapeDtypeStruct(feat.shape, BF), share, share),
        in_specs=[vmem, vmem],
        out_specs=(vmem, vmem, vmem),
    )(feat, out)


def local(tiles, cotangent, positions, clear, w_first, w_second):
    feat, out = level(positions, clear, tiles[0], cotangent[0], w_first, w_second)
    feat, first, second = finish(feat, out)
    return feat[None], first.T, second.T


def solution(mesh):
    in_specs = (
        P("scene", "region", None, None, None),
        P("scene", "region", None, None, None),
        P("scene", "region"),
        P("scene", "region"),
        P("scene", None),
        P("scene", None),
    )
    out_specs = (P("scene", "region", None, None, None), P("region", "scene"), P("region", "scene"))
    return jax.shard_map(local, mesh=mesh, in_specs=in_specs, out_specs=out_specs, check_vma=False)
```

```python
import math

import jax
import jax.numpy as jnp
import ml_dtypes
import numpy as np
from jax import lax
from jax.experimental import pallas as pl
from jax.experimental.pallas import tpu as pltpu
from jax.sharding import PartitionSpec as P

MESH = pl.DeviceIdType.MESH
BF = jnp.bfloat16
F32 = jnp.float32
GW, GH = 4, 16
C = 256
REG, ZN, YN, SC = 32, 8, 4, 8
WROWS = 288
LEFT = 48
ROWS = 9 * C
OWN_ROWS = ROWS // REG
VMEM_LIMIT = 56 * 1024 * 1024


def hot(rows, cols, pairs):
    out = np.zeros((rows, cols), np.float32)
    for row, col in pairs:
        out[row, col] = 1.0
    return out.astype(ml_dtypes.bfloat16)


def place_tables():
    tile = lambda h, w: 32 * h + w
    corner = ((30, 30), (30, 31), (31, 30), (31, 31), (30, 0), (31, 0), (0, 30), (0, 31), (0, 0))
    rim = hot(256, 1024, [
        (8 * k + q, px) for k in range(32) for q, px in enumerate((
            tile(31, k), tile(30, k), tile(k, 31), tile(k, 30), tile(0, k), tile(k, 0)))
    ] + [(8 * k + 7, tile(*at)) for k, at in enumerate(corner)])
    rim_grad = hot(256, 256, [(8 * k + 6, k if k < 16 else 16 * (k - 16)) for k in range(32)] + [(79, 0)])

    cols = lambda blk, b: 2 * b - 1 + blk
    order = (1, 2, 0, 3)
    body = hot(512, 256, [
        (at * 128 + h * 16 + b, h * 32 + cols(blk, b))
        for at, blk in enumerate(order) for h in range(8) for b in range(16) if 0 <= cols(blk, b) < 32
    ])
    sides = hot(256, 64, [(h * 16, 8 * h + 2) for h in range(8)]
                + [(128 + h * 16 + 15, 8 * h + 5) for h in range(8)])
    edge_q = (1, 0, 4)
    corner_left, corner_right = (1, 3, 7), (4, 5, 8)

    def edge_source(sel, col):
        if col < 0:
            return 8 * corner_left[sel] + 7
        if col > 31:
            return 8 * corner_right[sel] + 7
        return 8 * col + edge_q[sel]

    edges = hot(192, 256, [
        (sel * 64 + blk * 16 + b, edge_source(sel, cols(blk, b)))
        for sel in range(3) for blk in range(4) for b in range(16)
    ])

    def left_source(hh, j):
        if 0 <= hh < 32:
            return 8 * hh + (3, 2)[j] if j < 2 else None
        sel = {-2: 0, -1: 1, 32: 2}[hh]
        if j < 2:
            return 8 * ((0, 1), (2, 3), (6, 7))[sel][j] + 7
        return edge_q[sel]

    left = hot(9 * LEFT, 256, [
        ((3 * i + j) * LEFT + g, left_source(g + i - 2, j))
        for i in range(3) for j in range(3) for g in range(33)
        if left_source(g + i - 2, j) is not None
    ])
    first_col = hot(3 * LEFT, 256, [
        (i * LEFT + g, 8 * (g + i - 2) + 5) for i in range(3) for g in range(33) if 0 <= g + i - 2 < 32
    ])
    shift = hot(272, 272, [(a * 16 + b, a * 16 + b - 1) for a in range(17) for b in range(1, 16)])
    from_left = np.stack([
        hot(272, LEFT, [(a * 16, 2 * a + par) for a in range(17 - par)]) for par in range(2)
    ])
    back = hot(272, 256, [(a * 16 + b, a * 16 + b + 1) for a in range(16) for b in range(15)])
    below = hot(16, 256, [(b, 8 * b + 6) for b in range(16)])
    beside = hot(272, 256, [(a * 16 + 15, 8 * (16 + a) + 6) for a in range(16)]
                 + [(256 + b, 8 * (b + 1) + 6) for b in range(15)] + [(271, 79)])
    return rim, rim_grad, body, sides, edges, left, first_col, shift, from_left, back, below, beside


def dot(a, b):
    return jnp.dot(a, b, preferred_element_type=F32)


def dot_t(a, b):
    return lax.dot_general(a, b, (((1,), (1,)), ((), ())), preferred_element_type=F32)


def dot_l(a, b):
    return lax.dot_general(a, b, (((0,), (0,)), ((), ())), preferred_element_type=F32)


def sigmoid(v):
    return 0.5 * jnp.tanh(0.5 * v) + 0.5


def route_rows(pos, r):
    lane = lax.broadcasted_iota(jnp.int32, (512, 128), 1).astype(F32)
    q = lax.broadcasted_iota(jnp.int32, (512, 128), 0) % 8
    zero = jnp.zeros((512, 128), F32)
    k = zero.astype(jnp.int32) + r
    grad_row = jnp.where(k < 16, 1.0, 0.0)
    corner_row = jnp.where(k < 6, -1.0, 1.0)
    corner_col = jnp.where((k < 4) | (k == 6) | (k == 7), -1.0, 1.0)
    d_row = jnp.where(q < 2, -1.0, jnp.where(q == 4, 1.0, zero))
    d_row = jnp.where(q == 6, grad_row, jnp.where(q == 7, corner_row, d_row))
    d_col = jnp.where((q == 2) | (q == 3), -1.0, jnp.where(q == 5, 1.0, zero))
    d_col = jnp.where(q == 6, 1.0 - grad_row, jnp.where(q == 7, corner_col, d_col))
    p_row = jnp.floor(pos * 0.25)
    n_row = p_row + d_row
    n_col = pos - 4.0 * p_row + d_col
    inside = (n_row >= 0.0) & (n_row < GH) & (n_col >= 0.0) & (n_col < GW)
    want = jnp.where(inside, 4.0 * n_row + n_col, -1.0)
    has = jnp.where(pos == lane, 1.0, 0.0).astype(BF)
    wants = jnp.where(want == lane, 1.0, 0.0).astype(BF)
    same = (lax.broadcasted_iota(jnp.int32, (512, 512), 0) % 8) == (
        lax.broadcasted_iota(jnp.int32, (512, 512), 1) % 8)
    return jnp.where(same, dot_t(wants, has), 0.0).astype(BF)


Z_PART = 32
Z_ORDER = (4, 3, 5, 2, 6, 1, 7, 0)


def level_kernel(positions_hbm, clear_hbm, tiles_hbm, cotangent_hbm, w1_here, w2_here, *refs):
    names = list(TABLES)
    table_hbm = dict(zip(names, refs[:len(names)]))
    feat_hbm, out = refs[len(names):len(names) + 2]
    refs = refs[len(names) + 2:]
    table = dict(zip(names, refs[:len(names)]))
    (positions, clear, tiles, cotangent, feat, feat_sem, in_sem, table_sem, pos_send, pos_buf, send1, recv1, send2, recv2, masked, own_rim, halo, w1, w2,
     x4, h_odd, h_even, left_x, slopes, d_pre, g_f, g, f_buf, o_buf, s_buf, s_send, z_send, z_buf,
     other_z, other_sum, other_send, other_y, n_send, n_buf, x_send, x_buf, c_send, c_buf,
     a2a_s, a2a_r, w_s, w_r, v_s, v_r, y_s, y_r, zs, zr, o_s, o_r, xs, xr, cs, cr, own_sem) = refs[len(names):]

    s = lax.axis_index("scene")
    r = lax.axis_index("region")
    z, y = r // YN, r % YN
    sib = s + 1 - 2 * (s % 2)

    barrier = pltpu.get_barrier_semaphore()

    def far_first(o):
        step, turn_y = o // YN, o % YN
        dz = ZN // 2 + ((step + 1) // 2) * (1 - 2 * (step % 2))
        dy = YN // 2 + ((turn_y + 1) // 2) * (1 - 2 * (turn_y % 2))
        return ((z + dz) % ZN) * YN + (y + dy) % YN

    def greet(o, carry):
        pl.semaphore_signal(barrier, inc=1, device_id={"region": far_first(o)}, device_id_type=MESH)
        return carry

    lax.fori_loop(0, REG - 1, greet, 0)
    for o in range(1, SC):
        pl.semaphore_signal(barrier, inc=1, device_id={"scene": (s + o) % SC}, device_id_type=MESH)

    arrays = [pltpu.make_async_copy(src, dst, in_sem.at[n]) for n, (src, dst) in enumerate((
        (positions_hbm, positions), (clear_hbm, clear), (tiles_hbm, tiles), (cotangent_hbm, cotangent)))]
    for copy in arrays:
        copy.start()
    loads = {name: pltpu.make_async_copy(table_hbm[name], table[name], table_sem.at[n])
             for n, name in enumerate(names)}
    for name in names:
        loads[name].start()

    def w_rows(ref, who):
        return ref.at[pl.ds(pl.multiple_of(who * WROWS, 32), WROWS)]

    weights = ((w1_here, w1), (w2_here, w2))
    own = [pltpu.make_async_copy(src, w_rows(dst, s), own_sem.at[n]) for n, (src, dst) in enumerate(weights)]
    for copy in own:
        copy.start()

    def all_to_all(n, src, dst):
        def send(o, carry):
            to = far_first(o)
            pltpu.make_async_remote_copy(
                src_ref=src(to), dst_ref=dst(r), send_sem=a2a_s.at[n], recv_sem=a2a_r.at[n],
                device_id={"region": to}, device_id_type=MESH).start()
            return carry

        lax.fori_loop(0, REG - 1, send, 0)

    def await_all(buf, sem):
        pltpu.make_async_copy(buf, buf, sem).wait()

    for copy in arrays[:2]:
        copy.wait()
    own_pos = [positions[0:1, t:t + 1].astype(F32) for t in range(2)]
    for t in range(2):
        pos_send[t] = jnp.broadcast_to(own_pos[t], (1, 128))
    pl.semaphore_wait(barrier, REG - 1 + SC - 1)

    right, left_chip = (s + 2) % SC, (s + 6) % SC

    def to_scene(src, dst, send_sem, recv_sem, who):
        copy = pltpu.make_async_remote_copy(
            src_ref=src, dst_ref=dst, send_sem=send_sem, recv_sem=recv_sem,
            device_id={"scene": who}, device_id_type=MESH)
        copy.start()
        return copy

    all_to_all(0, lambda to: pos_send, lambda me: pos_buf.at[pl.ds(2 * me, 2)])
    far, near = [], []

    def send_weights(n):
        src, dst = weights[n]
        far.append(to_scene(src, w_rows(dst, s), w_s.at[n, 0], w_r.at[n, 0], right))
        far.append(to_scene(src, w_rows(dst, s), w_s.at[n, 1], w_r.at[n, 1], left_chip))
        near.append([to_scene(src, w_rows(dst, s), v_s.at[n, 0], v_r.at[n, 0], sib)])

    send_weights(0)

    for copy in arrays[2:]:
        copy.wait()
    for t in range(2):
        kept = clear[0:1, t:t + 1].astype(F32)
        masked[t] = (cotangent[t].reshape(256, C).astype(F32) * kept).astype(BF)
    loads["rim"].wait()
    loads["rim_grad"].wait()
    rims = []
    for t in range(2):
        rim = dot(table["rim"][...], tiles[t].reshape(1024, C)) + dot(table["rim_grad"][...], masked[t])
        own_rim[t] = rim.astype(BF)
        rims.append(rim.reshape(REG, 8, C))
    rims = jnp.concatenate(rims, axis=1).astype(BF)
    for half in range(2):
        send1[half] = rims[:, :, half * 128:(half + 1) * 128]
        all_to_all(1 + half, lambda to: send1.at[half, to], lambda me: recv1.at[half, me])
    for half in range(2):
        recv1[half, r] = send1[half, r]
    for t in range(2):
        pos_buf[2 * r + t] = pos_send[t]

    loads["body"].wait()
    for t in range(2):
        for c in range(4):
            chunk = tiles[t, 8 * c:8 * c + 8].reshape(256, C)
            got = dot(table["body"][:256], chunk).astype(BF)
            for at, blk in enumerate((1, 2)):
                x4[t, 4 * c + 1:4 * c + 5, :, :, blk * C:(blk + 1) * C] = (
                    got[at * 128:(at + 1) * 128].reshape(4, 2, 16, C))

    def forward(n, came, at):
        rows = w_rows(weights[n][1], came)
        return to_scene(rows, rows, v_s.at[n, at], v_r.at[n, at], sib)

    opposite = (s + 4) % SC
    far[0].wait_recv()
    rows = w_rows(w1, left_chip)
    far.append(to_scene(rows, rows, w_s.at[0, 2], w_r.at[0, 2], right))
    near[0].append(forward(0, left_chip, 1))
    far[1].wait_recv()
    near[0].append(forward(0, right, 2))
    send_weights(1)
    await_all(pos_buf.at[pl.ds(0, 2 * REG - 2)], a2a_r.at[0])
    route = route_rows(jnp.broadcast_to(pos_buf[...], (64, 8, 128)).reshape(512, 128), r)
    for half in range(2):
        await_all(recv1.at[half, pl.ds(0, REG - 1)], a2a_r.at[1 + half])
        send2[half] = dot(route, recv1[half].reshape(512, 128)).astype(BF).reshape(REG, 16, 128)
        all_to_all(3 + half, lambda to: send2.at[half, to], lambda me: recv2.at[half, me])
    for half in range(2):
        recv2[half, r] = send2[half, r]

    for name in names[3:]:
        loads[name].wait()
    far[2].wait_recv()
    near[0].append(forward(0, opposite, 3))
    far[3].wait_recv()
    near[1].append(forward(1, left_chip, 1))
    far[4].wait_recv()
    rows = w_rows(w2, right)
    far.append(to_scene(rows, rows, w_s.at[1, 2], w_r.at[1, 2], left_chip))
    near[1].append(forward(1, right, 2))
    for half in range(2):
        await_all(recv2.at[half, pl.ds(0, REG - 1)], a2a_r.at[3 + half])
        came = recv2[half].astype(F32)
        for t in range(2):
            halo[t, :, half * 128:(half + 1) * 128] = came[:, 8 * t:8 * t + 8].reshape(256, 128).astype(BF)
    for t in range(2):
        for c in range(4):
            chunk = tiles[t, 8 * c:8 * c + 8].reshape(256, C)
            got = dot(table["body"][256:], chunk) + dot(table["sides"][...], halo[t, 64 * c:64 * c + 64])
            got = got.astype(BF)
            for at, blk in enumerate((0, 3)):
                x4[t, 4 * c + 1:4 * c + 5, :, :, blk * C:(blk + 1) * C] = (
                    got[at * 128:(at + 1) * 128].reshape(4, 2, 16, C))
        rim = dot(table["edges"][...], halo[t]).astype(BF)
        for sel, (pair, par) in enumerate(((0, 0), (0, 1), (17, 0))):
            for blk in range(4):
                start = sel * 64 + blk * 16
                x4[t, pair, par, :, blk * C:(blk + 1) * C] = rim[start:start + 16]
        side = dot(table["left"][...], halo[t])
        inner = dot(table["first_col"][...], own_rim[t])
        for i in range(3):
            for j in range(3):
                tap = 3 * i + j
                part = side[tap * LEFT:(tap + 1) * LEFT]
                if j == 2:
                    part = part + inner[i * LEFT:(i + 1) * LEFT]
                left_x[t * LEFT:(t + 1) * LEFT, tap * C:(tap + 1) * C] = part.astype(BF)

    own[0].wait()
    for copy in near[0]:
        copy.wait_recv()

    pre_left = dot(left_x[...], w1[...])
    row_id = lax.broadcasted_iota(jnp.int32, (LEFT, C), 0)
    hidden_left, above = [], []
    for t in range(2):
        p_row = jnp.floor(own_pos[t] * 0.25)
        has_left = jnp.where(own_pos[t] - 4.0 * p_row > 0.0, 1.0, 0.0)
        has_above = jnp.where(p_row > 0.0, 1.0, 0.0)
        above.append(has_above)
        v = pre_left[t * LEFT:(t + 1) * LEFT]
        keep = jnp.where(row_id == 0, has_left * has_above, has_left)
        hidden_left.append((v * sigmoid(v) * keep).astype(BF))

    def window(t, par, i, cp):
        row = par + i
        n = 17 - par
        return x4[t, row // 2:row // 2 + n, row % 2, :, cp * C:cp * C + 768].reshape(n * 16, 768)

    for t in range(2):
        if t == 1:
            far[5].wait_recv()
            near[1].append(forward(1, opposite, 3))
        for par in range(2):
            store = h_odd if par == 0 else h_even
            n = 17 - par
            for cp in range(2):
                patch = jnp.concatenate([window(t, par, i, cp) for i in range(3)], axis=1)
                pre = dot(patch, w1[...])
                sig = sigmoid(pre)
                act = pre * sig
                if par == 0:
                    own_row = lax.broadcasted_iota(jnp.int32, (272, C), 0) >= 16
                    act = jnp.where(own_row, act, act * above[t])
                act = act.astype(BF)
                if cp == 0:
                    store[t, :, :, C:2 * C] = act.reshape(n, 16, C)
                else:
                    store[t, :, :, 2 * C:] = act.reshape(n, 16, C)
                    moved = dot(table["shift"][:n * 16, :n * 16], act)
                    moved = moved + dot(table["from_left"][par, :n * 16], hidden_left[t])
                    store[t, :, :, :C] = moved.astype(BF).reshape(n, 16, C)
                if par == 0:
                    pre, sig = pre[16:], sig[16:]
                slopes[4 * t + 2 * par + cp] = sig * (1.0 + pre * (1.0 - sig))

    def hidden_rows(t, i):
        if i == 1:
            return h_even[t].reshape(256, 768)
        return h_odd[t, i // 2:i // 2 + 16].reshape(256, 768)

    def blocks(n):
        for yy in range(YN):
            for zz in range(ZN):
                start = OWN_ROWS * (zz * YN + yy)
                rows = g_f[start:start + OWN_ROWS, :]
                g[n, yy, zz] = jnp.concatenate([rows[:, :128], rows[:, 128:]], axis=0).astype(BF)

    def to_region(src, dst, send_sem, recv_sem, who):
        copy = pltpu.make_async_remote_copy(
            src_ref=src, dst_ref=dst, send_sem=send_sem, recv_sem=recv_sem,
            device_id={"region": who}, device_id_type=MESH)
        copy.start()
        return copy

    sent = []
    y_copies = {}
    held = (144, 144 - Z_PART)

    def turn(oz):
        return 1 if oz % 2 == 0 else YN - 1

    def y_first(n):
        for kind in range(2):
            for oz in Z_ORDER:
                d = turn(oz)
                block = (y + 2) % YN if kind == 0 else (y + YN - d) % YN
                who = (y + d) % YN if kind == 0 else block
                buf = f_buf if kind == 0 else o_buf
                y_copies[n, kind, oz] = to_region(
                    g.at[n, block, (z + oz) % ZN, pl.ds(0, held[n])], buf.at[n, oz, pl.ds(0, held[n])],
                    y_s.at[kind, n, oz], y_r.at[kind, n, oz], z * YN + who)
                sent.append(y_copies[n, kind, oz])

    def y_second(n):
        for oz in Z_ORDER:
            who = (y + turn(oz)) % YN
            y_copies[n, 0, oz].wait_recv()
            summed = g[n, who, (z + oz) % ZN, :held[n]].astype(F32) + f_buf[n, oz, :held[n]].astype(F32)
            s_send[n, oz, :held[n]] = summed.astype(BF)
            y_copies[n, 2, oz] = to_region(
                s_send.at[n, oz, pl.ds(0, held[n])], s_buf.at[n, oz, pl.ds(0, held[n])], y_s.at[2, n, oz], y_r.at[2, n, oz], z * YN + who)
            sent.append(y_copies[n, 2, oz])

    def z_first(n):
        copies = []
        for oz in Z_ORDER:
            y_copies[n, 1, oz].wait_recv()
            y_copies[n, 2, oz].wait_recv()
            total = g[n, y, (z + oz) % ZN, :held[n]].astype(F32) + o_buf[n, oz, :held[n]].astype(F32)
            total = total + s_buf[n, oz, :held[n]].astype(F32)
            if oz:
                z_send[n, oz - 1, :held[n]] = total.astype(BF)
                copies.append(to_region(
                    z_send.at[n, oz - 1, pl.ds(0, held[n])], z_buf.at[n, oz - 1, pl.ds(0, held[n])], zs.at[n, oz - 1], zr.at[n, oz - 1],
                    ((z + oz) % ZN) * YN + y))
        sent.extend(copies)
        return total, copies

    def z_second(n, total, copies):
        for at, copy in enumerate(copies):
            copy.wait_recv()
            total = total + z_buf[n, Z_ORDER[at] - 1, :held[n]].astype(F32)
        return total

    def other_first():
        copies = [to_region(
            g.at[1, :, (z + oz) % ZN, pl.ds(held[1], Z_PART)], other_z.at[oz - 1],
            o_s.at[oz - 1], o_r.at[oz - 1], ((z + oz) % ZN) * YN + y) for oz in Z_ORDER[:-1]]
        sent.extend(copies)
        return copies

    def other_second(copies):
        total = g[1, :, z, held[1]:].astype(F32)
        for at, copy in enumerate(copies):
            copy.wait_recv()
            total = total + other_z[Z_ORDER[at] - 1].astype(F32)
        other_sum[...] = total
        other_send[...] = total.astype(BF)
        copies = [to_region(
            other_send.at[(y + o) % YN], other_y.at[o - 1], o_s.at[ZN + o - 2], o_r.at[ZN + o - 2],
            z * YN + (y + o) % YN) for o in range(1, YN)]
        sent.extend(copies)
        return copies

    def other_third(copies):
        total = other_sum[y]
        for at, copy in enumerate(copies):
            copy.wait_recv()
            total = total + other_y[at].astype(F32)
        return total

    for i in range(3):
        for j in range(3):
            tap = 3 * i + j
            seen = jnp.concatenate([hidden_rows(t, i)[:, j * C:(j + 1) * C] for t in range(2)], axis=0)
            g_f[tap * C:(tap + 1) * C, :] = dot_l(seen, masked[...].reshape(512, C))
    blocks(1)
    y_first(1)
    other = other_first()

    own[1].wait()
    for copy in near[1]:
        copy.wait_recv()
    for t in range(2):
        patch = jnp.concatenate([hidden_rows(t, i) for i in range(3)], axis=1)
        feat[t] = dot(patch, w2[...]).astype(BF).reshape(16, 16, C)
    feat_copy = pltpu.make_async_copy(feat, feat_hbm, feat_sem)
    feat_copy.start()

    def second(tap):
        return w2[tap * C:(tap + 1) * C, :]

    up, down = slice(0, 256), slice(16, 272)
    for t in range(2):
        m0 = jnp.concatenate([masked[t], dot(table["below"][...], halo[t]).astype(BF)], axis=0)
        m1 = (dot(table["back"][...], masked[t]) + dot(table["beside"][...], halo[t])).astype(BF)
        spread = (
            dot_t(m0[up], second(7)) + dot_t(m0[down], second(1)),
            (dot_t(m0[up], second(8)) + dot_t(m1[up], second(6))
             + dot_t(m0[down], second(2)) + dot_t(m1[down], second(0))),
            dot_t(m0[up], second(4)),
            dot_t(m0[up], second(5)) + dot_t(m1[up], second(3)),
        )
        for n in range(4):
            group = 4 * t + n
            d_pre[group * 256:(group + 1) * 256, :] = (spread[n] * slopes[group]).astype(BF)

    y_second(1)

    def own_rows(t, par, i, cp, j):
        row = (2 if par == 0 else 1) + i
        lanes = (cp + j) * C
        return x4[t, row // 2:row // 2 + 16, row % 2, :, lanes:lanes + C].reshape(256, C)

    for i in range(3):
        for j in range(3):
            tap = 3 * i + j
            seen = jnp.concatenate(
                [own_rows(t, par, i, cp, j) for t in range(2) for par in range(2) for cp in range(2)], axis=0)
            g_f[tap * C:(tap + 1) * C, :] = dot_l(seen, d_pre[...])
    blocks(0)
    y_first(0)
    other = other_second(other)
    z_left = z_first(1)
    y_second(0)
    total_second = jnp.concatenate([z_second(1, *z_left), other_third(other)], axis=0)

    def share(n, total):
        both = jnp.concatenate([total[:OWN_ROWS].T, total[OWN_ROWS:].T], axis=0)
        x_send[:, n] = both.reshape(SC, 32, OWN_ROWS)

    z_left = z_first(0)
    share(1, total_second)
    squares = jnp.sum(total_second * total_second, axis=0, keepdims=True)
    total_first = z_second(0, *z_left)
    squares = squares + jnp.sum(total_first * total_first, axis=0, keepdims=True)
    n_send[0] = squares
    all_to_all(5, lambda to: n_send.at[0], lambda me: n_buf.at[me])
    n_buf[r] = squares
    share(0, total_first)
    x_copies = []
    for o in range(1, SC):
        to = (s + o) % SC
        x_copies.append(to_scene(x_send.at[to], x_buf.at[o - 1], xs.at[o - 1], xr.at[o - 1], to))
    await_all(n_buf.at[pl.ds(0, REG - 1)], a2a_r.at[5])
    sum_sq = jnp.sum(n_buf[...].reshape(REG, 128), keepdims=True)
    factor = (3.0 * C * math.sqrt(2.0) / SC) / (jnp.sqrt(sum_sq) + 0.01)
    c_send[0] = jnp.broadcast_to(factor, (1, 128))
    c_copies = []
    for o in range(1, SC):
        to = (s + o) % SC
        c_copies.append(to_scene(c_send.at[0], c_buf.at[o - 1], cs.at[o - 1], cr.at[o - 1], to))
    result = x_send[s] * factor.reshape(1, 1, 1)
    for o in range(1, SC):
        x_copies[o - 1].wait_recv()
        c_copies[o - 1].wait_recv()
        result = result + x_buf[o - 1] * c_buf[o - 1][:, :1].reshape(1, 1, 1)
    out[...] = result
    feat_copy.wait()

    for copy in far + near[0] + near[1] + sent + x_copies + c_copies:
        copy.wait_send()
    await_all(pos_buf.at[pl.ds(0, 2 * REG - 2)], a2a_s.at[0])
    for half in range(2):
        await_all(send1.at[half, pl.ds(0, REG - 1)], a2a_s.at[1 + half])
        await_all(send2.at[half, pl.ds(0, REG - 1)], a2a_s.at[3 + half])
    await_all(n_buf.at[pl.ds(0, REG - 1)], a2a_s.at[5])


NAMES = ("rim", "rim_grad", "body", "sides", "edges", "left", "first_col", "shift", "from_left",
         "back", "below", "beside")
TABLES = dict(zip(NAMES, place_tables()))


def level(positions, clear, tiles, cotangent, w1, w2):
    vmem = pl.BlockSpec(memory_space=pltpu.VMEM)
    anywhere = pl.BlockSpec(memory_space=pl.ANY)
    dma = pltpu.SemaphoreType.DMA
    tables = list(TABLES.values())
    part = (144, 128)
    return pl.pallas_call(
        level_kernel,
        name="level",
        out_shape=(jax.ShapeDtypeStruct((2, 16, 16, C), BF), jax.ShapeDtypeStruct((2, 32, OWN_ROWS), F32)),
        in_specs=[anywhere] * (6 + len(tables)),
        out_specs=(anywhere, vmem),
        scratch_shapes=[pltpu.VMEM(t.shape, BF) for t in tables] + [
            pltpu.VMEM((1, 2), jnp.int32), pltpu.VMEM((1, 2), jnp.int32),
            pltpu.VMEM((2, 32, 32, C), BF), pltpu.VMEM((2, 16, 16, C), BF),
            pltpu.VMEM((2, 16, 16, C), BF), dma, dma((4,)), dma((len(tables),)),
            pltpu.VMEM((2, 1, 128), F32), pltpu.VMEM((2 * REG, 1, 128), F32),
            pltpu.VMEM((2, REG, 16, 128), BF), pltpu.VMEM((2, REG, 16, 128), BF),
            pltpu.VMEM((2, REG, 16, 128), BF), pltpu.VMEM((2, REG, 16, 128), BF),
            pltpu.VMEM((2, 256, C), BF), pltpu.VMEM((2, 256, C), BF), pltpu.VMEM((2, 256, C), BF),
            pltpu.VMEM((ROWS, C), BF), pltpu.VMEM((ROWS, C), BF),
            pltpu.VMEM((2, 18, 2, 16, 4 * C), BF),
            pltpu.VMEM((2, 17, 16, 3 * C), BF), pltpu.VMEM((2, 16, 16, 3 * C), BF),
            pltpu.VMEM((2 * LEFT, ROWS), BF),
            pltpu.VMEM((8, 256, C), F32),
            pltpu.VMEM((2048, C), BF),
            pltpu.VMEM((ROWS, C), F32),
            pltpu.VMEM((2, YN, ZN) + part, BF),
            pltpu.VMEM((2, ZN) + part, BF), pltpu.VMEM((2, ZN) + part, BF),
            pltpu.VMEM((2, ZN) + part, BF), pltpu.VMEM((2, ZN) + part, BF),
            pltpu.VMEM((2, ZN - 1) + part, BF), pltpu.VMEM((2, ZN - 1) + part, BF),
            pltpu.VMEM((ZN - 1, YN, Z_PART, 128), BF), pltpu.VMEM((YN, Z_PART, 128), F32),
            pltpu.VMEM((YN, Z_PART, 128), BF), pltpu.VMEM((YN - 1, Z_PART, 128), BF),
            pltpu.VMEM((1, 1, 128), F32), pltpu.VMEM((REG, 1, 128), F32),
            pltpu.VMEM((SC, 2, 32, OWN_ROWS), F32), pltpu.VMEM((SC - 1, 2, 32, OWN_ROWS), F32),
            pltpu.VMEM((1, 1, 128), F32), pltpu.VMEM((SC - 1, 1, 128), F32),
            dma((6,)), dma((6,)), dma((2, 3)), dma((2, 3)), dma((2, 4)), dma((2, 4)),
            dma((3, 2, ZN)), dma((3, 2, ZN)), dma((2, ZN - 1)), dma((2, ZN - 1)), dma((ZN + YN - 2,)), dma((ZN + YN - 2,)),
            dma((SC - 1,)), dma((SC - 1,)), dma((SC - 1,)), dma((SC - 1,)), dma((2,)),
        ],
        compiler_params=pltpu.CompilerParams(
            collective_id=0, has_side_effects=True, vmem_limit_bytes=VMEM_LIMIT),
    )(positions, clear, tiles, cotangent, w1, w2, *[jnp.asarray(t) for t in tables])


def finish_kernel(feat_in, out_in, feat, first, second):
    feat[...] = feat_in[...]
    first[...] = out_in[0]
    second[...] = out_in[1]


def finish(feat, out):
    vmem = pl.BlockSpec(memory_space=pltpu.VMEM)
    share = jax.ShapeDtypeStruct((32, OWN_ROWS), F32)
    return pl.pallas_call(
        finish_kernel,
        name="finish",
        out_shape=(jax.ShapeDtypeStruct(feat.shape, BF), share, share),
        in_specs=[vmem, vmem],
        out_specs=(vmem, vmem, vmem),
    )(feat, out)


def local(tiles, cotangent, positions, clear, w_first, w_second):
    feat, out = level(positions, clear, tiles[0], cotangent[0], w_first, w_second)
    feat, first, second = finish(feat, out)
    return feat[None], first.T, second.T


def solution(mesh):
    in_specs = (
        P("scene", "region", None, None, None),
        P("scene", "region", None, None, None),
        P("scene", "region"),
        P("scene", "region"),
        P("scene", None),
        P("scene", None),
    )
    out_specs = (P("scene", "region", None, None, None), P("region", "scene"), P("region", "scene"))
    return jax.shard_map(local, mesh=mesh, in_specs=in_specs, out_specs=out_specs, check_vma=False)
```

```python
import math

import jax
import jax.numpy as jnp
import ml_dtypes
import numpy as np
from jax import lax
from jax.experimental import pallas as pl
from jax.experimental.pallas import tpu as pltpu
from jax.sharding import PartitionSpec as P

MESH = pl.DeviceIdType.MESH
BF = jnp.bfloat16
F32 = jnp.float32
GW, GH = 4, 16
C = 256
REG, ZN, YN, SC = 32, 8, 4, 8
WROWS = 288
LEFT = 48
ROWS = 9 * C
OWN_ROWS = ROWS // REG
VMEM_LIMIT = 56 * 1024 * 1024


def hot(rows, cols, pairs):
    out = np.zeros((rows, cols), np.float32)
    for row, col in pairs:
        out[row, col] = 1.0
    return out.astype(ml_dtypes.bfloat16)


def place_tables():
    tile = lambda h, w: 32 * h + w
    corner = ((30, 30), (30, 31), (31, 30), (31, 31), (30, 0), (31, 0), (0, 30), (0, 31), (0, 0))
    rim = hot(256, 1024, [
        (8 * k + q, px) for k in range(32) for q, px in enumerate((
            tile(31, k), tile(30, k), tile(k, 31), tile(k, 30), tile(0, k), tile(k, 0)))
    ] + [(8 * k + 7, tile(*at)) for k, at in enumerate(corner)])
    rim_grad = hot(256, 256, [(8 * k + 6, k if k < 16 else 16 * (k - 16)) for k in range(32)] + [(79, 0)])

    cols = lambda blk, b: 2 * b - 1 + blk
    order = (1, 2, 0, 3)
    body = hot(512, 256, [
        (at * 128 + h * 16 + b, h * 32 + cols(blk, b))
        for at, blk in enumerate(order) for h in range(8) for b in range(16) if 0 <= cols(blk, b) < 32
    ])
    sides = hot(256, 64, [(h * 16, 8 * h + 2) for h in range(8)]
                + [(128 + h * 16 + 15, 8 * h + 5) for h in range(8)])
    edge_q = (1, 0, 4)
    corner_left, corner_right = (1, 3, 7), (4, 5, 8)

    def edge_source(sel, col):
        if col < 0:
            return 8 * corner_left[sel] + 7
        if col > 31:
            return 8 * corner_right[sel] + 7
        return 8 * col + edge_q[sel]

    edges = hot(192, 256, [
        (sel * 64 + blk * 16 + b, edge_source(sel, cols(blk, b)))
        for sel in range(3) for blk in range(4) for b in range(16)
    ])

    def left_source(hh, j):
        if 0 <= hh < 32:
            return 8 * hh + (3, 2)[j] if j < 2 else None
        sel = {-2: 0, -1: 1, 32: 2}[hh]
        if j < 2:
            return 8 * ((0, 1), (2, 3), (6, 7))[sel][j] + 7
        return edge_q[sel]

    left = hot(9 * LEFT, 256, [
        ((3 * i + j) * LEFT + g, left_source(g + i - 2, j))
        for i in range(3) for j in range(3) for g in range(33)
        if left_source(g + i - 2, j) is not None
    ])
    first_col = hot(3 * LEFT, 256, [
        (i * LEFT + g, 8 * (g + i - 2) + 5) for i in range(3) for g in range(33) if 0 <= g + i - 2 < 32
    ])
    shift = hot(272, 272, [(a * 16 + b, a * 16 + b - 1) for a in range(17) for b in range(1, 16)])
    from_left = np.stack([
        hot(272, LEFT, [(a * 16, 2 * a + par) for a in range(17 - par)]) for par in range(2)
    ])
    back = hot(272, 256, [(a * 16 + b, a * 16 + b + 1) for a in range(16) for b in range(15)])
    below = hot(16, 256, [(b, 8 * b + 6) for b in range(16)])
    beside = hot(272, 256, [(a * 16 + 15, 8 * (16 + a) + 6) for a in range(16)]
                 + [(256 + b, 8 * (b + 1) + 6) for b in range(15)] + [(271, 79)])
    return rim, rim_grad, body, sides, edges, left, first_col, shift, from_left, back, below, beside


def dot(a, b):
    return jnp.dot(a, b, preferred_element_type=F32)


def dot_t(a, b):
    return lax.dot_general(a, b, (((1,), (1,)), ((), ())), preferred_element_type=F32)


def dot_l(a, b):
    return lax.dot_general(a, b, (((0,), (0,)), ((), ())), preferred_element_type=F32)


def sigmoid(v):
    return 0.5 * jnp.tanh(0.5 * v) + 0.5


def route_rows(pos, r):
    lane = lax.broadcasted_iota(jnp.int32, (512, 128), 1).astype(F32)
    q = lax.broadcasted_iota(jnp.int32, (512, 128), 0) % 8
    zero = jnp.zeros((512, 128), F32)
    k = zero.astype(jnp.int32) + r
    grad_row = jnp.where(k < 16, 1.0, 0.0)
    corner_row = jnp.where(k < 6, -1.0, 1.0)
    corner_col = jnp.where((k < 4) | (k == 6) | (k == 7), -1.0, 1.0)
    d_row = jnp.where(q < 2, -1.0, jnp.where(q == 4, 1.0, zero))
    d_row = jnp.where(q == 6, grad_row, jnp.where(q == 7, corner_row, d_row))
    d_col = jnp.where((q == 2) | (q == 3), -1.0, jnp.where(q == 5, 1.0, zero))
    d_col = jnp.where(q == 6, 1.0 - grad_row, jnp.where(q == 7, corner_col, d_col))
    p_row = jnp.floor(pos * 0.25)
    n_row = p_row + d_row
    n_col = pos - 4.0 * p_row + d_col
    inside = (n_row >= 0.0) & (n_row < GH) & (n_col >= 0.0) & (n_col < GW)
    want = jnp.where(inside, 4.0 * n_row + n_col, -1.0)
    has = jnp.where(pos == lane, 1.0, 0.0).astype(BF)
    wants = jnp.where(want == lane, 1.0, 0.0).astype(BF)
    same = (lax.broadcasted_iota(jnp.int32, (512, 512), 0) % 8) == (
        lax.broadcasted_iota(jnp.int32, (512, 512), 1) % 8)
    return jnp.where(same, dot_t(wants, has), 0.0).astype(BF)


Z_PART = 32
Z_ORDER = (4, 3, 5, 2, 6, 1, 7, 0)


def level_kernel(positions_hbm, clear_hbm, tiles_hbm, cotangent_hbm, w1_here, w2_here, *refs):
    names = list(TABLES)
    table_hbm = dict(zip(names, refs[:len(names)]))
    feat_hbm, out = refs[len(names):len(names) + 2]
    refs = refs[len(names) + 2:]
    table = dict(zip(names, refs[:len(names)]))
    (positions, clear, tiles, cotangent, feat, feat_sem, in_sem, table_sem, pos_send, pos_buf, send1, recv1, send2, recv2, masked, own_rim, halo, w1, w2,
     x4, h_odd, h_even, left_x, slopes, d_pre, g_f, g, f_buf, o_buf, s_buf, s_send, z_send, z_buf,
     other_z, other_sum, other_send, other_y, n_send, n_buf, x_send, x_buf, c_send, c_buf,
     a2a_s, a2a_r, w_s, w_r, v_s, v_r, y_s, y_r, zs, zr, o_s, o_r, xs, xr, cs, cr, own_sem) = refs[len(names):]

    s = lax.axis_index("scene")
    r = lax.axis_index("region")
    z, y = r // YN, r % YN
    sib = s + 1 - 2 * (s % 2)

    barrier = pltpu.get_barrier_semaphore()

    def far_first(o):
        step, turn_y = o // YN, o % YN
        dz = ZN // 2 + ((step + 1) // 2) * (1 - 2 * (step % 2))
        dy = YN // 2 + ((turn_y + 1) // 2) * (1 - 2 * (turn_y % 2))
        return ((z + dz) % ZN) * YN + (y + dy) % YN

    def greet(o, carry):
        pl.semaphore_signal(barrier, inc=1, device_id={"region": far_first(o)}, device_id_type=MESH)
        return carry

    lax.fori_loop(0, REG - 1, greet, 0)
    for o in range(1, SC):
        pl.semaphore_signal(barrier, inc=1, device_id={"scene": (s + o) % SC}, device_id_type=MESH)

    arrays = [pltpu.make_async_copy(src, dst, in_sem.at[n]) for n, (src, dst) in enumerate((
        (positions_hbm, positions), (clear_hbm, clear), (tiles_hbm, tiles), (cotangent_hbm, cotangent)))]
    for copy in arrays:
        copy.start()
    loads = {name: pltpu.make_async_copy(table_hbm[name], table[name], table_sem.at[n])
             for n, name in enumerate(names)}
    for name in names:
        loads[name].start()

    def w_rows(ref, who):
        return ref.at[pl.ds(pl.multiple_of(who * WROWS, 32), WROWS)]

    weights = ((w1_here, w1), (w2_here, w2))
    own = [pltpu.make_async_copy(src, w_rows(dst, s), own_sem.at[n]) for n, (src, dst) in enumerate(weights)]
    for copy in own:
        copy.start()

    def all_to_all(n, src, dst):
        def send(o, carry):
            to = far_first(o)
            pltpu.make_async_remote_copy(
                src_ref=src(to), dst_ref=dst(r), send_sem=a2a_s.at[n], recv_sem=a2a_r.at[n],
                device_id={"region": to}, device_id_type=MESH).start()
            return carry

        lax.fori_loop(0, REG - 1, send, 0)

    def await_all(buf, sem):
        pltpu.make_async_copy(buf, buf, sem).wait()

    for copy in arrays[:2]:
        copy.wait()
    own_pos = [positions[0:1, t:t + 1].astype(F32) for t in range(2)]
    for t in range(2):
        pos_send[t] = jnp.broadcast_to(own_pos[t], (1, 128))
    pl.semaphore_wait(barrier, REG - 1 + SC - 1)

    right, left_chip = (s + 2) % SC, (s + 6) % SC

    def to_scene(src, dst, send_sem, recv_sem, who):
        copy = pltpu.make_async_remote_copy(
            src_ref=src, dst_ref=dst, send_sem=send_sem, recv_sem=recv_sem,
            device_id={"scene": who}, device_id_type=MESH)
        copy.start()
        return copy

    all_to_all(0, lambda to: pos_send, lambda me: pos_buf.at[pl.ds(2 * me, 2)])
    far, near = [], []

    def send_weights(n):
        src, dst = weights[n]
        far.append(to_scene(src, w_rows(dst, s), w_s.at[n, 0], w_r.at[n, 0], right))
        far.append(to_scene(src, w_rows(dst, s), w_s.at[n, 1], w_r.at[n, 1], left_chip))
        near.append([to_scene(src, w_rows(dst, s), v_s.at[n, 0], v_r.at[n, 0], sib)])

    send_weights(0)

    for copy in arrays[2:]:
        copy.wait()
    for t in range(2):
        kept = clear[0:1, t:t + 1].astype(F32)
        masked[t] = (cotangent[t].reshape(256, C).astype(F32) * kept).astype(BF)
    loads["rim"].wait()
    loads["rim_grad"].wait()
    rims = []
    for t in range(2):
        rim = dot(table["rim"][...], tiles[t].reshape(1024, C)) + dot(table["rim_grad"][...], masked[t])
        own_rim[t] = rim.astype(BF)
        rims.append(rim.reshape(REG, 8, C))
    rims = jnp.concatenate(rims, axis=1).astype(BF)
    for half in range(2):
        send1[half] = rims[:, :, half * 128:(half + 1) * 128]
        all_to_all(1 + half, lambda to: send1.at[half, to], lambda me: recv1.at[half, me])
    for half in range(2):
        recv1[half, r] = send1[half, r]
    for t in range(2):
        pos_buf[2 * r + t] = pos_send[t]

    loads["body"].wait()
    for t in range(2):
        for c in range(4):
            chunk = tiles[t, 8 * c:8 * c + 8].reshape(256, C)
            got = dot(table["body"][:256], chunk).astype(BF)
            for at, blk in enumerate((1, 2)):
                x4[t, 4 * c + 1:4 * c + 5, :, :, blk * C:(blk + 1) * C] = (
                    got[at * 128:(at + 1) * 128].reshape(4, 2, 16, C))

    def forward(n, came, at):
        rows = w_rows(weights[n][1], came)
        return to_scene(rows, rows, v_s.at[n, at], v_r.at[n, at], sib)

    opposite = (s + 4) % SC
    far[0].wait_recv()
    rows = w_rows(w1, left_chip)
    far.append(to_scene(rows, rows, w_s.at[0, 2], w_r.at[0, 2], right))
    near[0].append(forward(0, left_chip, 1))
    far[1].wait_recv()
    near[0].append(forward(0, right, 2))
    send_weights(1)
    await_all(pos_buf.at[pl.ds(0, 2 * REG - 2)], a2a_r.at[0])
    route = route_rows(jnp.broadcast_to(pos_buf[...], (64, 8, 128)).reshape(512, 128), r)
    for half in range(2):
        await_all(recv1.at[half, pl.ds(0, REG - 1)], a2a_r.at[1 + half])
        send2[half] = dot(route, recv1[half].reshape(512, 128)).astype(BF).reshape(REG, 16, 128)
        all_to_all(3 + half, lambda to: send2.at[half, to], lambda me: recv2.at[half, me])
    for half in range(2):
        recv2[half, r] = send2[half, r]

    for name in names[3:]:
        loads[name].wait()
    far[2].wait_recv()
    near[0].append(forward(0, opposite, 3))
    far[3].wait_recv()
    near[1].append(forward(1, left_chip, 1))
    far[4].wait_recv()
    rows = w_rows(w2, right)
    far.append(to_scene(rows, rows, w_s.at[1, 2], w_r.at[1, 2], left_chip))
    near[1].append(forward(1, right, 2))
    for half in range(2):
        await_all(recv2.at[half, pl.ds(0, REG - 1)], a2a_r.at[3 + half])
        came = recv2[half].astype(F32)
        for t in range(2):
            halo[t, :, half * 128:(half + 1) * 128] = came[:, 8 * t:8 * t + 8].reshape(256, 128).astype(BF)
    for t in range(2):
        for c in range(4):
            chunk = tiles[t, 8 * c:8 * c + 8].reshape(256, C)
            got = dot(table["body"][256:], chunk) + dot(table["sides"][...], halo[t, 64 * c:64 * c + 64])
            got = got.astype(BF)
            for at, blk in enumerate((0, 3)):
                x4[t, 4 * c + 1:4 * c + 5, :, :, blk * C:(blk + 1) * C] = (
                    got[at * 128:(at + 1) * 128].reshape(4, 2, 16, C))
        rim = dot(table["edges"][...], halo[t]).astype(BF)
        for sel, (pair, par) in enumerate(((0, 0), (0, 1), (17, 0))):
            for blk in range(4):
                start = sel * 64 + blk * 16
                x4[t, pair, par, :, blk * C:(blk + 1) * C] = rim[start:start + 16]
        side = dot(table["left"][...], halo[t])
        inner = dot(table["first_col"][...], own_rim[t])
        for i in range(3):
            for j in range(3):
                tap = 3 * i + j
                part = side[tap * LEFT:(tap + 1) * LEFT]
                if j == 2:
                    part = part + inner[i * LEFT:(i + 1) * LEFT]
                left_x[t * LEFT:(t + 1) * LEFT, tap * C:(tap + 1) * C] = part.astype(BF)

    own[0].wait()
    for copy in near[0]:
        copy.wait_recv()

    pre_left = dot(left_x[...], w1[...])
    row_id = lax.broadcasted_iota(jnp.int32, (LEFT, C), 0)
    hidden_left, above = [], []
    for t in range(2):
        p_row = jnp.floor(own_pos[t] * 0.25)
        has_left = jnp.where(own_pos[t] - 4.0 * p_row > 0.0, 1.0, 0.0)
        has_above = jnp.where(p_row > 0.0, 1.0, 0.0)
        above.append(has_above)
        v = pre_left[t * LEFT:(t + 1) * LEFT]
        keep = jnp.where(row_id == 0, has_left * has_above, has_left)
        hidden_left.append((v * sigmoid(v) * keep).astype(BF))

    def window(t, par, i, cp):
        row = par + i
        n = 17 - par
        return x4[t, row // 2:row // 2 + n, row % 2, :, cp * C:cp * C + 768].reshape(n * 16, 768)

    for t in range(2):
        if t == 1:
            far[5].wait_recv()
            near[1].append(forward(1, opposite, 3))
        for par in range(2):
            store = h_odd if par == 0 else h_even
            n = 17 - par
            for cp in range(2):
                patch = jnp.concatenate([window(t, par, i, cp) for i in range(3)], axis=1)
                pre = dot(patch, w1[...])
                sig = sigmoid(pre)
                act = pre * sig
                if par == 0:
                    own_row = lax.broadcasted_iota(jnp.int32, (272, C), 0) >= 16
                    act = jnp.where(own_row, act, act * above[t])
                act = act.astype(BF)
                if cp == 0:
                    store[t, :, :, C:2 * C] = act.reshape(n, 16, C)
                else:
                    store[t, :, :, 2 * C:] = act.reshape(n, 16, C)
                    moved = dot(table["shift"][:n * 16, :n * 16], act)
                    moved = moved + dot(table["from_left"][par, :n * 16], hidden_left[t])
                    store[t, :, :, :C] = moved.astype(BF).reshape(n, 16, C)
                if par == 0:
                    pre, sig = pre[16:], sig[16:]
                slopes[4 * t + 2 * par + cp] = sig * (1.0 + pre * (1.0 - sig))

    def hidden_rows(t, i):
        if i == 1:
            return h_even[t].reshape(256, 768)
        return h_odd[t, i // 2:i // 2 + 16].reshape(256, 768)

    def blocks(n):
        for yy in range(YN):
            for zz in range(ZN):
                start = OWN_ROWS * (zz * YN + yy)
                rows = g_f[start:start + OWN_ROWS, :]
                g[n, yy, zz] = jnp.concatenate([rows[:, :128], rows[:, 128:]], axis=0).astype(BF)

    def to_region(src, dst, send_sem, recv_sem, who):
        copy = pltpu.make_async_remote_copy(
            src_ref=src, dst_ref=dst, send_sem=send_sem, recv_sem=recv_sem,
            device_id={"region": who}, device_id_type=MESH)
        copy.start()
        return copy

    sent = []
    y_copies = {}
    held = (144, 144 - Z_PART)

    def turn(oz):
        return 1 if oz % 2 == 0 else YN - 1

    def y_first(n):
        for kind in range(2):
            for oz in Z_ORDER:
                d = turn(oz)
                block = (y + 2) % YN if kind == 0 else (y + YN - d) % YN
                who = (y + d) % YN if kind == 0 else block
                buf = f_buf if kind == 0 else o_buf
                y_copies[n, kind, oz] = to_region(
                    g.at[n, block, (z + oz) % ZN, pl.ds(0, held[n])], buf.at[n, oz, pl.ds(0, held[n])],
                    y_s.at[kind, n, oz], y_r.at[kind, n, oz], z * YN + who)
                sent.append(y_copies[n, kind, oz])

    def y_second(n):
        for oz in Z_ORDER:
            who = (y + turn(oz)) % YN
            y_copies[n, 0, oz].wait_recv()
            summed = g[n, who, (z + oz) % ZN, :held[n]].astype(F32) + f_buf[n, oz, :held[n]].astype(F32)
            s_send[n, oz, :held[n]] = summed.astype(BF)
            y_copies[n, 2, oz] = to_region(
                s_send.at[n, oz, pl.ds(0, held[n])], s_buf.at[n, oz, pl.ds(0, held[n])], y_s.at[2, n, oz], y_r.at[2, n, oz], z * YN + who)
            sent.append(y_copies[n, 2, oz])

    def z_first(n):
        copies = []
        for oz in Z_ORDER:
            y_copies[n, 1, oz].wait_recv()
            y_copies[n, 2, oz].wait_recv()
            total = g[n, y, (z + oz) % ZN, :held[n]].astype(F32) + o_buf[n, oz, :held[n]].astype(F32)
            total = total + s_buf[n, oz, :held[n]].astype(F32)
            if oz:
                z_send[n, oz - 1, :held[n]] = total.astype(BF)
                copies.append(to_region(
                    z_send.at[n, oz - 1, pl.ds(0, held[n])], z_buf.at[n, oz - 1, pl.ds(0, held[n])], zs.at[n, oz - 1], zr.at[n, oz - 1],
                    ((z + oz) % ZN) * YN + y))
        sent.extend(copies)
        return total, copies

    def z_second(n, total, copies):
        for at, copy in enumerate(copies):
            copy.wait_recv()
            total = total + z_buf[n, Z_ORDER[at] - 1, :held[n]].astype(F32)
        return total

    def other_first():
        copies = [to_region(
            g.at[1, :, (z + oz) % ZN, pl.ds(held[1], Z_PART)], other_z.at[oz - 1],
            o_s.at[oz - 1], o_r.at[oz - 1], ((z + oz) % ZN) * YN + y) for oz in Z_ORDER[:-1]]
        sent.extend(copies)
        return copies

    def other_second(copies):
        total = g[1, :, z, held[1]:].astype(F32)
        for at, copy in enumerate(copies):
            copy.wait_recv()
            total = total + other_z[Z_ORDER[at] - 1].astype(F32)
        other_sum[...] = total
        other_send[...] = total.astype(BF)
        copies = [to_region(
            other_send.at[(y + o) % YN], other_y.at[o - 1], o_s.at[ZN + o - 2], o_r.at[ZN + o - 2],
            z * YN + (y + o) % YN) for o in range(1, YN)]
        sent.extend(copies)
        return copies

    def other_third(copies):
        total = other_sum[y]
        for at, copy in enumerate(copies):
            copy.wait_recv()
            total = total + other_y[at].astype(F32)
        return total

    for i in range(3):
        for j in range(3):
            tap = 3 * i + j
            seen = jnp.concatenate([hidden_rows(t, i)[:, j * C:(j + 1) * C] for t in range(2)], axis=0)
            g_f[tap * C:(tap + 1) * C, :] = dot_l(seen, masked[...].reshape(512, C))
    blocks(1)
    y_first(1)
    other = other_first()

    own[1].wait()
    for copy in near[1]:
        copy.wait_recv()
    for t in range(2):
        patch = jnp.concatenate([hidden_rows(t, i) for i in range(3)], axis=1)
        feat[t] = dot(patch, w2[...]).astype(BF).reshape(16, 16, C)
    feat_copy = pltpu.make_async_copy(feat, feat_hbm, feat_sem)
    feat_copy.start()

    def second(tap):
        return w2[tap * C:(tap + 1) * C, :]

    up, down = slice(0, 256), slice(16, 272)
    for t in range(2):
        m0 = jnp.concatenate([masked[t], dot(table["below"][...], halo[t]).astype(BF)], axis=0)
        m1 = (dot(table["back"][...], masked[t]) + dot(table["beside"][...], halo[t])).astype(BF)
        spread = (
            dot_t(m0[up], second(7)) + dot_t(m0[down], second(1)),
            (dot_t(m0[up], second(8)) + dot_t(m1[up], second(6))
             + dot_t(m0[down], second(2)) + dot_t(m1[down], second(0))),
            dot_t(m0[up], second(4)),
            dot_t(m0[up], second(5)) + dot_t(m1[up], second(3)),
        )
        for n in range(4):
            group = 4 * t + n
            d_pre[group * 256:(group + 1) * 256, :] = (spread[n] * slopes[group]).astype(BF)

    def own_rows(t, par, i, cp, j):
        row = (2 if par == 0 else 1) + i
        lanes = (cp + j) * C
        return x4[t, row // 2:row // 2 + 16, row % 2, :, lanes:lanes + C].reshape(256, C)

    for i in range(3):
        if i == 2:
            y_second(1)
        for j in range(3):
            tap = 3 * i + j
            seen = jnp.concatenate(
                [own_rows(t, par, i, cp, j) for t in range(2) for par in range(2) for cp in range(2)], axis=0)
            g_f[tap * C:(tap + 1) * C, :] = dot_l(seen, d_pre[...])
    blocks(0)
    y_first(0)
    other = other_second(other)
    z_left = z_first(1)
    y_second(0)
    total_second = jnp.concatenate([z_second(1, *z_left), other_third(other)], axis=0)

    def share(n, total):
        both = jnp.concatenate([total[:OWN_ROWS].T, total[OWN_ROWS:].T], axis=0)
        x_send[:, n] = both.reshape(SC, 32, OWN_ROWS)

    z_left = z_first(0)
    share(1, total_second)
    squares = jnp.sum(total_second * total_second, axis=0, keepdims=True)
    total_first = z_second(0, *z_left)
    squares = squares + jnp.sum(total_first * total_first, axis=0, keepdims=True)
    n_send[0] = squares
    all_to_all(5, lambda to: n_send.at[0], lambda me: n_buf.at[me])
    n_buf[r] = squares
    share(0, total_first)
    x_copies = []
    for o in range(1, SC):
        to = (s + o) % SC
        x_copies.append(to_scene(x_send.at[to], x_buf.at[o - 1], xs.at[o - 1], xr.at[o - 1], to))
    await_all(n_buf.at[pl.ds(0, REG - 1)], a2a_r.at[5])
    sum_sq = jnp.sum(n_buf[...].reshape(REG, 128), keepdims=True)
    factor = (3.0 * C * math.sqrt(2.0) / SC) / (jnp.sqrt(sum_sq) + 0.01)
    c_send[0] = jnp.broadcast_to(factor, (1, 128))
    c_copies = []
    for o in range(1, SC):
        to = (s + o) % SC
        c_copies.append(to_scene(c_send.at[0], c_buf.at[o - 1], cs.at[o - 1], cr.at[o - 1], to))
    result = x_send[s] * factor.reshape(1, 1, 1)
    for o in range(1, SC):
        x_copies[o - 1].wait_recv()
        c_copies[o - 1].wait_recv()
        result = result + x_buf[o - 1] * c_buf[o - 1][:, :1].reshape(1, 1, 1)
    out[...] = result
    feat_copy.wait()

    for copy in far + near[0] + near[1] + sent + x_copies + c_copies:
        copy.wait_send()
    await_all(pos_buf.at[pl.ds(0, 2 * REG - 2)], a2a_s.at[0])
    for half in range(2):
        await_all(send1.at[half, pl.ds(0, REG - 1)], a2a_s.at[1 + half])
        await_all(send2.at[half, pl.ds(0, REG - 1)], a2a_s.at[3 + half])
    await_all(n_buf.at[pl.ds(0, REG - 1)], a2a_s.at[5])


NAMES = ("rim", "rim_grad", "body", "sides", "edges", "left", "first_col", "shift", "from_left",
         "back", "below", "beside")
TABLES = dict(zip(NAMES, place_tables()))


def level(positions, clear, tiles, cotangent, w1, w2):
    vmem = pl.BlockSpec(memory_space=pltpu.VMEM)
    anywhere = pl.BlockSpec(memory_space=pl.ANY)
    dma = pltpu.SemaphoreType.DMA
    tables = list(TABLES.values())
    part = (144, 128)
    return pl.pallas_call(
        level_kernel,
        name="level",
        out_shape=(jax.ShapeDtypeStruct((2, 16, 16, C), BF), jax.ShapeDtypeStruct((2, 32, OWN_ROWS), F32)),
        in_specs=[anywhere] * (6 + len(tables)),
        out_specs=(anywhere, vmem),
        scratch_shapes=[pltpu.VMEM(t.shape, BF) for t in tables] + [
            pltpu.VMEM((1, 2), jnp.int32), pltpu.VMEM((1, 2), jnp.int32),
            pltpu.VMEM((2, 32, 32, C), BF), pltpu.VMEM((2, 16, 16, C), BF),
            pltpu.VMEM((2, 16, 16, C), BF), dma, dma((4,)), dma((len(tables),)),
            pltpu.VMEM((2, 1, 128), F32), pltpu.VMEM((2 * REG, 1, 128), F32),
            pltpu.VMEM((2, REG, 16, 128), BF), pltpu.VMEM((2, REG, 16, 128), BF),
            pltpu.VMEM((2, REG, 16, 128), BF), pltpu.VMEM((2, REG, 16, 128), BF),
            pltpu.VMEM((2, 256, C), BF), pltpu.VMEM((2, 256, C), BF), pltpu.VMEM((2, 256, C), BF),
            pltpu.VMEM((ROWS, C), BF), pltpu.VMEM((ROWS, C), BF),
            pltpu.VMEM((2, 18, 2, 16, 4 * C), BF),
            pltpu.VMEM((2, 17, 16, 3 * C), BF), pltpu.VMEM((2, 16, 16, 3 * C), BF),
            pltpu.VMEM((2 * LEFT, ROWS), BF),
            pltpu.VMEM((8, 256, C), F32),
            pltpu.VMEM((2048, C), BF),
            pltpu.VMEM((ROWS, C), F32),
            pltpu.VMEM((2, YN, ZN) + part, BF),
            pltpu.VMEM((2, ZN) + part, BF), pltpu.VMEM((2, ZN) + part, BF),
            pltpu.VMEM((2, ZN) + part, BF), pltpu.VMEM((2, ZN) + part, BF),
            pltpu.VMEM((2, ZN - 1) + part, BF), pltpu.VMEM((2, ZN - 1) + part, BF),
            pltpu.VMEM((ZN - 1, YN, Z_PART, 128), BF), pltpu.VMEM((YN, Z_PART, 128), F32),
            pltpu.VMEM((YN, Z_PART, 128), BF), pltpu.VMEM((YN - 1, Z_PART, 128), BF),
            pltpu.VMEM((1, 1, 128), F32), pltpu.VMEM((REG, 1, 128), F32),
            pltpu.VMEM((SC, 2, 32, OWN_ROWS), F32), pltpu.VMEM((SC - 1, 2, 32, OWN_ROWS), F32),
            pltpu.VMEM((1, 1, 128), F32), pltpu.VMEM((SC - 1, 1, 128), F32),
            dma((6,)), dma((6,)), dma((2, 3)), dma((2, 3)), dma((2, 4)), dma((2, 4)),
            dma((3, 2, ZN)), dma((3, 2, ZN)), dma((2, ZN - 1)), dma((2, ZN - 1)), dma((ZN + YN - 2,)), dma((ZN + YN - 2,)),
            dma((SC - 1,)), dma((SC - 1,)), dma((SC - 1,)), dma((SC - 1,)), dma((2,)),
        ],
        compiler_params=pltpu.CompilerParams(
            collective_id=0, has_side_effects=True, vmem_limit_bytes=VMEM_LIMIT),
    )(positions, clear, tiles, cotangent, w1, w2, *[jnp.asarray(t) for t in tables])


def finish_kernel(feat_in, out_in, feat, first, second):
    feat[...] = feat_in[...]
    first[...] = out_in[0]
    second[...] = out_in[1]


def finish(feat, out):
    vmem = pl.BlockSpec(memory_space=pltpu.VMEM)
    share = jax.ShapeDtypeStruct((32, OWN_ROWS), F32)
    return pl.pallas_call(
        finish_kernel,
        name="finish",
        out_shape=(jax.ShapeDtypeStruct(feat.shape, BF), share, share),
        in_specs=[vmem, vmem],
        out_specs=(vmem, vmem, vmem),
    )(feat, out)


def local(tiles, cotangent, positions, clear, w_first, w_second):
    feat, out = level(positions, clear, tiles[0], cotangent[0], w_first, w_second)
    feat, first, second = finish(feat, out)
    return feat[None], first.T, second.T


def solution(mesh):
    in_specs = (
        P("scene", "region", None, None, None),
        P("scene", "region", None, None, None),
        P("scene", "region"),
        P("scene", "region"),
        P("scene", None),
        P("scene", None),
    )
    out_specs = (P("scene", "region", None, None, None), P("region", "scene"), P("region", "scene"))
    return jax.shard_map(local, mesh=mesh, in_specs=in_specs, out_specs=out_specs, check_vma=False)
```

```python
import math

import jax
import jax.numpy as jnp
import ml_dtypes
import numpy as np
from jax import lax
from jax.experimental import pallas as pl
from jax.experimental.pallas import tpu as pltpu
from jax.sharding import PartitionSpec as P

MESH = pl.DeviceIdType.MESH
BF = jnp.bfloat16
F32 = jnp.float32
GW, GH = 4, 16
C = 256
REG, ZN, YN, SC = 32, 8, 4, 8
WROWS = 288
LEFT = 48
ROWS = 9 * C
OWN_ROWS = ROWS // REG
VMEM_LIMIT = 56 * 1024 * 1024


def hot(rows, cols, pairs):
    out = np.zeros((rows, cols), np.float32)
    for row, col in pairs:
        out[row, col] = 1.0
    return out.astype(ml_dtypes.bfloat16)


def place_tables():
    tile = lambda h, w: 32 * h + w
    corner = ((30, 30), (30, 31), (31, 30), (31, 31), (30, 0), (31, 0), (0, 30), (0, 31), (0, 0))
    rim = hot(256, 1024, [
        (8 * k + q, px) for k in range(32) for q, px in enumerate((
            tile(31, k), tile(30, k), tile(k, 31), tile(k, 30), tile(0, k), tile(k, 0)))
    ] + [(8 * k + 7, tile(*at)) for k, at in enumerate(corner)])
    rim_grad = hot(256, 256, [(8 * k + 6, k if k < 16 else 16 * (k - 16)) for k in range(32)] + [(79, 0)])

    cols = lambda blk, b: 2 * b - 1 + blk
    order = (1, 2, 0, 3)
    body = hot(512, 256, [
        (at * 128 + h * 16 + b, h * 32 + cols(blk, b))
        for at, blk in enumerate(order) for h in range(8) for b in range(16) if 0 <= cols(blk, b) < 32
    ])
    sides = hot(256, 64, [(h * 16, 8 * h + 2) for h in range(8)]
                + [(128 + h * 16 + 15, 8 * h + 5) for h in range(8)])
    edge_q = (1, 0, 4)
    corner_left, corner_right = (1, 3, 7), (4, 5, 8)

    def edge_source(sel, col):
        if col < 0:
            return 8 * corner_left[sel] + 7
        if col > 31:
            return 8 * corner_right[sel] + 7
        return 8 * col + edge_q[sel]

    edges = hot(192, 256, [
        (sel * 64 + blk * 16 + b, edge_source(sel, cols(blk, b)))
        for sel in range(3) for blk in range(4) for b in range(16)
    ])

    def left_source(hh, j):
        if 0 <= hh < 32:
            return 8 * hh + (3, 2)[j] if j < 2 else None
        sel = {-2: 0, -1: 1, 32: 2}[hh]
        if j < 2:
            return 8 * ((0, 1), (2, 3), (6, 7))[sel][j] + 7
        return edge_q[sel]

    left = hot(9 * LEFT, 256, [
        ((3 * i + j) * LEFT + g, left_source(g + i - 2, j))
        for i in range(3) for j in range(3) for g in range(33)
        if left_source(g + i - 2, j) is not None
    ])
    first_col = hot(3 * LEFT, 256, [
        (i * LEFT + g, 8 * (g + i - 2) + 5) for i in range(3) for g in range(33) if 0 <= g + i - 2 < 32
    ])
    shift = hot(272, 272, [(a * 16 + b, a * 16 + b - 1) for a in range(17) for b in range(1, 16)])
    from_left = np.stack([
        hot(272, LEFT, [(a * 16, 2 * a + par) for a in range(17 - par)]) for par in range(2)
    ])
    back = hot(272, 256, [(a * 16 + b, a * 16 + b + 1) for a in range(16) for b in range(15)])
    below = hot(16, 256, [(b, 8 * b + 6) for b in range(16)])
    beside = hot(272, 256, [(a * 16 + 15, 8 * (16 + a) + 6) for a in range(16)]
                 + [(256 + b, 8 * (b + 1) + 6) for b in range(15)] + [(271, 79)])
    return rim, rim_grad, body, sides, edges, left, first_col, shift, from_left, back, below, beside


def dot(a, b):
    return jnp.dot(a, b, preferred_element_type=F32)


def dot_t(a, b):
    return lax.dot_general(a, b, (((1,), (1,)), ((), ())), preferred_element_type=F32)


def dot_l(a, b):
    return lax.dot_general(a, b, (((0,), (0,)), ((), ())), preferred_element_type=F32)


def sigmoid(v):
    return 0.5 * jnp.tanh(0.5 * v) + 0.5


def route_rows(pos, r):
    lane = lax.broadcasted_iota(jnp.int32, (512, 128), 1).astype(F32)
    q = lax.broadcasted_iota(jnp.int32, (512, 128), 0) % 8
    zero = jnp.zeros((512, 128), F32)
    k = zero.astype(jnp.int32) + r
    grad_row = jnp.where(k < 16, 1.0, 0.0)
    corner_row = jnp.where(k < 6, -1.0, 1.0)
    corner_col = jnp.where((k < 4) | (k == 6) | (k == 7), -1.0, 1.0)
    d_row = jnp.where(q < 2, -1.0, jnp.where(q == 4, 1.0, zero))
    d_row = jnp.where(q == 6, grad_row, jnp.where(q == 7, corner_row, d_row))
    d_col = jnp.where((q == 2) | (q == 3), -1.0, jnp.where(q == 5, 1.0, zero))
    d_col = jnp.where(q == 6, 1.0 - grad_row, jnp.where(q == 7, corner_col, d_col))
    p_row = jnp.floor(pos * 0.25)
    n_row = p_row + d_row
    n_col = pos - 4.0 * p_row + d_col
    inside = (n_row >= 0.0) & (n_row < GH) & (n_col >= 0.0) & (n_col < GW)
    want = jnp.where(inside, 4.0 * n_row + n_col, -1.0)
    has = jnp.where(pos == lane, 1.0, 0.0).astype(BF)
    wants = jnp.where(want == lane, 1.0, 0.0).astype(BF)
    same = (lax.broadcasted_iota(jnp.int32, (512, 512), 0) % 8) == (
        lax.broadcasted_iota(jnp.int32, (512, 512), 1) % 8)
    return jnp.where(same, dot_t(wants, has), 0.0).astype(BF)


Z_PART = 16
Z_ORDER = (4, 3, 5, 2, 6, 1, 7, 0)


def level_kernel(positions_hbm, clear_hbm, tiles_hbm, cotangent_hbm, w1_here, w2_here, *refs):
    names = list(TABLES)
    table_hbm = dict(zip(names, refs[:len(names)]))
    feat_hbm, out = refs[len(names):len(names) + 2]
    refs = refs[len(names) + 2:]
    table = dict(zip(names, refs[:len(names)]))
    (positions, clear, tiles, cotangent, feat, feat_sem, in_sem, table_sem, pos_send, pos_buf, send1, recv1, send2, recv2, masked, own_rim, halo, w1, w2,
     x4, h_odd, h_even, left_x, slopes, d_pre, g_f, g, f_buf, o_buf, s_buf, s_send, z_send, z_buf,
     other_z, other_sum, other_send, other_y, n_send, n_buf, x_send, x_buf, c_send, c_buf,
     a2a_s, a2a_r, w_s, w_r, v_s, v_r, y_s, y_r, zs, zr, o_s, o_r, xs, xr, cs, cr, own_sem) = refs[len(names):]

    s = lax.axis_index("scene")
    r = lax.axis_index("region")
    z, y = r // YN, r % YN
    sib = s + 1 - 2 * (s % 2)

    barrier = pltpu.get_barrier_semaphore()

    def far_first(o):
        step, turn_y = o // YN, o % YN
        dz = ZN // 2 + ((step + 1) // 2) * (1 - 2 * (step % 2))
        dy = YN // 2 + ((turn_y + 1) // 2) * (1 - 2 * (turn_y % 2))
        return ((z + dz) % ZN) * YN + (y + dy) % YN

    def greet(o, carry):
        pl.semaphore_signal(barrier, inc=1, device_id={"region": far_first(o)}, device_id_type=MESH)
        return carry

    lax.fori_loop(0, REG - 1, greet, 0)
    for o in range(1, SC):
        pl.semaphore_signal(barrier, inc=1, device_id={"scene": (s + o) % SC}, device_id_type=MESH)

    arrays = [pltpu.make_async_copy(src, dst, in_sem.at[n]) for n, (src, dst) in enumerate((
        (positions_hbm, positions), (clear_hbm, clear), (tiles_hbm, tiles), (cotangent_hbm, cotangent)))]
    for copy in arrays:
        copy.start()
    loads = {name: pltpu.make_async_copy(table_hbm[name], table[name], table_sem.at[n])
             for n, name in enumerate(names)}
    for name in names:
        loads[name].start()

    def w_rows(ref, who):
        return ref.at[pl.ds(pl.multiple_of(who * WROWS, 32), WROWS)]

    weights = ((w1_here, w1), (w2_here, w2))
    own = [pltpu.make_async_copy(src, w_rows(dst, s), own_sem.at[n]) for n, (src, dst) in enumerate(weights)]
    for copy in own:
        copy.start()

    def all_to_all(n, src, dst):
        def send(o, carry):
            to = far_first(o)
            pltpu.make_async_remote_copy(
                src_ref=src(to), dst_ref=dst(r), send_sem=a2a_s.at[n], recv_sem=a2a_r.at[n],
                device_id={"region": to}, device_id_type=MESH).start()
            return carry

        lax.fori_loop(0, REG - 1, send, 0)

    def await_all(buf, sem):
        pltpu.make_async_copy(buf, buf, sem).wait()

    for copy in arrays[:2]:
        copy.wait()
    own_pos = [positions[0:1, t:t + 1].astype(F32) for t in range(2)]
    for t in range(2):
        pos_send[t] = jnp.broadcast_to(own_pos[t], (1, 128))
    pl.semaphore_wait(barrier, REG - 1 + SC - 1)

    right, left_chip = (s + 2) % SC, (s + 6) % SC

    def to_scene(src, dst, send_sem, recv_sem, who):
        copy = pltpu.make_async_remote_copy(
            src_ref=src, dst_ref=dst, send_sem=send_sem, recv_sem=recv_sem,
            device_id={"scene": who}, device_id_type=MESH)
        copy.start()
        return copy

    all_to_all(0, lambda to: pos_send, lambda me: pos_buf.at[pl.ds(2 * me, 2)])
    far, near = [], []

    def send_weights(n):
        src, dst = weights[n]
        far.append(to_scene(src, w_rows(dst, s), w_s.at[n, 0], w_r.at[n, 0], right))
        far.append(to_scene(src, w_rows(dst, s), w_s.at[n, 1], w_r.at[n, 1], left_chip))
        near.append([to_scene(src, w_rows(dst, s), v_s.at[n, 0], v_r.at[n, 0], sib)])

    send_weights(0)

    for copy in arrays[2:]:
        copy.wait()
    for t in range(2):
        kept = clear[0:1, t:t + 1].astype(F32)
        masked[t] = (cotangent[t].reshape(256, C).astype(F32) * kept).astype(BF)
    loads["rim"].wait()
    loads["rim_grad"].wait()
    rims = []
    for t in range(2):
        rim = dot(table["rim"][...], tiles[t].reshape(1024, C)) + dot(table["rim_grad"][...], masked[t])
        own_rim[t] = rim.astype(BF)
        rims.append(rim.reshape(REG, 8, C))
    rims = jnp.concatenate(rims, axis=1).astype(BF)
    for half in range(2):
        send1[half] = rims[:, :, half * 128:(half + 1) * 128]
        all_to_all(1 + half, lambda to: send1.at[half, to], lambda me: recv1.at[half, me])
    for half in range(2):
        recv1[half, r] = send1[half, r]
    for t in range(2):
        pos_buf[2 * r + t] = pos_send[t]

    loads["body"].wait()
    for t in range(2):
        for c in range(4):
            chunk = tiles[t, 8 * c:8 * c + 8].reshape(256, C)
            got = dot(table["body"][:256], chunk).astype(BF)
            for at, blk in enumerate((1, 2)):
                x4[t, 4 * c + 1:4 * c + 5, :, :, blk * C:(blk + 1) * C] = (
                    got[at * 128:(at + 1) * 128].reshape(4, 2, 16, C))

    def forward(n, came, at):
        rows = w_rows(weights[n][1], came)
        return to_scene(rows, rows, v_s.at[n, at], v_r.at[n, at], sib)

    opposite = (s + 4) % SC
    far[0].wait_recv()
    rows = w_rows(w1, left_chip)
    far.append(to_scene(rows, rows, w_s.at[0, 2], w_r.at[0, 2], right))
    near[0].append(forward(0, left_chip, 1))
    far[1].wait_recv()
    near[0].append(forward(0, right, 2))
    send_weights(1)
    await_all(pos_buf.at[pl.ds(0, 2 * REG - 2)], a2a_r.at[0])
    route = route_rows(jnp.broadcast_to(pos_buf[...], (64, 8, 128)).reshape(512, 128), r)
    for half in range(2):
        await_all(recv1.at[half, pl.ds(0, REG - 1)], a2a_r.at[1 + half])
        send2[half] = dot(route, recv1[half].reshape(512, 128)).astype(BF).reshape(REG, 16, 128)
        all_to_all(3 + half, lambda to: send2.at[half, to], lambda me: recv2.at[half, me])
    for half in range(2):
        recv2[half, r] = send2[half, r]

    for name in names[3:]:
        loads[name].wait()
    far[2].wait_recv()
    near[0].append(forward(0, opposite, 3))
    far[3].wait_recv()
    near[1].append(forward(1, left_chip, 1))
    far[4].wait_recv()
    rows = w_rows(w2, right)
    far.append(to_scene(rows, rows, w_s.at[1, 2], w_r.at[1, 2], left_chip))
    near[1].append(forward(1, right, 2))
    for half in range(2):
        await_all(recv2.at[half, pl.ds(0, REG - 1)], a2a_r.at[3 + half])
        came = recv2[half].astype(F32)
        for t in range(2):
            halo[t, :, half * 128:(half + 1) * 128] = came[:, 8 * t:8 * t + 8].reshape(256, 128).astype(BF)
    for t in range(2):
        for c in range(4):
            chunk = tiles[t, 8 * c:8 * c + 8].reshape(256, C)
            got = dot(table["body"][256:], chunk) + dot(table["sides"][...], halo[t, 64 * c:64 * c + 64])
            got = got.astype(BF)
            for at, blk in enumerate((0, 3)):
                x4[t, 4 * c + 1:4 * c + 5, :, :, blk * C:(blk + 1) * C] = (
                    got[at * 128:(at + 1) * 128].reshape(4, 2, 16, C))
        rim = dot(table["edges"][...], halo[t]).astype(BF)
        for sel, (pair, par) in enumerate(((0, 0), (0, 1), (17, 0))):
            for blk in range(4):
                start = sel * 64 + blk * 16
                x4[t, pair, par, :, blk * C:(blk + 1) * C] = rim[start:start + 16]
        side = dot(table["left"][...], halo[t])
        inner = dot(table["first_col"][...], own_rim[t])
        for i in range(3):
            for j in range(3):
                tap = 3 * i + j
                part = side[tap * LEFT:(tap + 1) * LEFT]
                if j == 2:
                    part = part + inner[i * LEFT:(i + 1) * LEFT]
                left_x[t * LEFT:(t + 1) * LEFT, tap * C:(tap + 1) * C] = part.astype(BF)

    own[0].wait()
    for copy in near[0]:
        copy.wait_recv()

    pre_left = dot(left_x[...], w1[...])
    row_id = lax.broadcasted_iota(jnp.int32, (LEFT, C), 0)
    hidden_left, above = [], []
    for t in range(2):
        p_row = jnp.floor(own_pos[t] * 0.25)
        has_left = jnp.where(own_pos[t] - 4.0 * p_row > 0.0, 1.0, 0.0)
        has_above = jnp.where(p_row > 0.0, 1.0, 0.0)
        above.append(has_above)
        v = pre_left[t * LEFT:(t + 1) * LEFT]
        keep = jnp.where(row_id == 0, has_left * has_above, has_left)
        hidden_left.append((v * sigmoid(v) * keep).astype(BF))

    def window(t, par, i, cp):
        row = par + i
        n = 17 - par
        return x4[t, row // 2:row // 2 + n, row % 2, :, cp * C:cp * C + 768].reshape(n * 16, 768)

    for t in range(2):
        if t == 1:
            far[5].wait_recv()
            near[1].append(forward(1, opposite, 3))
        for par in range(2):
            store = h_odd if par == 0 else h_even
            n = 17 - par
            for cp in range(2):
                patch = jnp.concatenate([window(t, par, i, cp) for i in range(3)], axis=1)
                pre = dot(patch, w1[...])
                sig = sigmoid(pre)
                act = pre * sig
                if par == 0:
                    own_row = lax.broadcasted_iota(jnp.int32, (272, C), 0) >= 16
                    act = jnp.where(own_row, act, act * above[t])
                act = act.astype(BF)
                if cp == 0:
                    store[t, :, :, C:2 * C] = act.reshape(n, 16, C)
                else:
                    store[t, :, :, 2 * C:] = act.reshape(n, 16, C)
                    moved = dot(table["shift"][:n * 16, :n * 16], act)
                    moved = moved + dot(table["from_left"][par, :n * 16], hidden_left[t])
                    store[t, :, :, :C] = moved.astype(BF).reshape(n, 16, C)
                if par == 0:
                    pre, sig = pre[16:], sig[16:]
                slopes[4 * t + 2 * par + cp] = sig * (1.0 + pre * (1.0 - sig))

    def hidden_rows(t, i):
        if i == 1:
            return h_even[t].reshape(256, 768)
        return h_odd[t, i // 2:i // 2 + 16].reshape(256, 768)

    def blocks(n):
        for yy in range(YN):
            for zz in range(ZN):
                start = OWN_ROWS * (zz * YN + yy)
                rows = g_f[start:start + OWN_ROWS, :]
                g[n, yy, zz] = jnp.concatenate([rows[:, :128], rows[:, 128:]], axis=0).astype(BF)

    def to_region(src, dst, send_sem, recv_sem, who):
        copy = pltpu.make_async_remote_copy(
            src_ref=src, dst_ref=dst, send_sem=send_sem, recv_sem=recv_sem,
            device_id={"region": who}, device_id_type=MESH)
        copy.start()
        return copy

    sent = []
    y_copies = {}
    held = (144, 144 - Z_PART)

    def turn(oz):
        return 1 if oz % 2 == 0 else YN - 1

    def y_first(n):
        for kind in range(2):
            for oz in Z_ORDER:
                d = turn(oz)
                block = (y + 2) % YN if kind == 0 else (y + YN - d) % YN
                who = (y + d) % YN if kind == 0 else block
                buf = f_buf if kind == 0 else o_buf
                y_copies[n, kind, oz] = to_region(
                    g.at[n, block, (z + oz) % ZN, pl.ds(0, held[n])], buf.at[n, oz, pl.ds(0, held[n])],
                    y_s.at[kind, n, oz], y_r.at[kind, n, oz], z * YN + who)
                sent.append(y_copies[n, kind, oz])

    def y_second(n):
        for oz in Z_ORDER:
            who = (y + turn(oz)) % YN
            y_copies[n, 0, oz].wait_recv()
            summed = g[n, who, (z + oz) % ZN, :held[n]].astype(F32) + f_buf[n, oz, :held[n]].astype(F32)
            s_send[n, oz, :held[n]] = summed.astype(BF)
            y_copies[n, 2, oz] = to_region(
                s_send.at[n, oz, pl.ds(0, held[n])], s_buf.at[n, oz, pl.ds(0, held[n])], y_s.at[2, n, oz], y_r.at[2, n, oz], z * YN + who)
            sent.append(y_copies[n, 2, oz])

    def z_first(n):
        copies = []
        for oz in Z_ORDER:
            y_copies[n, 1, oz].wait_recv()
            y_copies[n, 2, oz].wait_recv()
            total = g[n, y, (z + oz) % ZN, :held[n]].astype(F32) + o_buf[n, oz, :held[n]].astype(F32)
            total = total + s_buf[n, oz, :held[n]].astype(F32)
            if oz:
                z_send[n, oz - 1, :held[n]] = total.astype(BF)
                copies.append(to_region(
                    z_send.at[n, oz - 1, pl.ds(0, held[n])], z_buf.at[n, oz - 1, pl.ds(0, held[n])], zs.at[n, oz - 1], zr.at[n, oz - 1],
                    ((z + oz) % ZN) * YN + y))
        sent.extend(copies)
        return total, copies

    def z_second(n, total, copies):
        for at, copy in enumerate(copies):
            copy.wait_recv()
            total = total + z_buf[n, Z_ORDER[at] - 1, :held[n]].astype(F32)
        return total

    def other_first():
        copies = [to_region(
            g.at[1, :, (z + oz) % ZN, pl.ds(held[1], Z_PART)], other_z.at[oz - 1],
            o_s.at[oz - 1], o_r.at[oz - 1], ((z + oz) % ZN) * YN + y) for oz in Z_ORDER[:-1]]
        sent.extend(copies)
        return copies

    def other_second(copies):
        total = g[1, :, z, held[1]:].astype(F32)
        for at, copy in enumerate(copies):
            copy.wait_recv()
            total = total + other_z[Z_ORDER[at] - 1].astype(F32)
        other_sum[...] = total
        other_send[...] = total.astype(BF)
        copies = [to_region(
            other_send.at[(y + o) % YN], other_y.at[o - 1], o_s.at[ZN + o - 2], o_r.at[ZN + o - 2],
            z * YN + (y + o) % YN) for o in range(1, YN)]
        sent.extend(copies)
        return copies

    def other_third(copies):
        total = other_sum[y]
        for at, copy in enumerate(copies):
            copy.wait_recv()
            total = total + other_y[at].astype(F32)
        return total

    for i in range(3):
        for j in range(3):
            tap = 3 * i + j
            seen = jnp.concatenate([hidden_rows(t, i)[:, j * C:(j + 1) * C] for t in range(2)], axis=0)
            g_f[tap * C:(tap + 1) * C, :] = dot_l(seen, masked[...].reshape(512, C))
    blocks(1)
    y_first(1)
    other = other_first()

    own[1].wait()
    for copy in near[1]:
        copy.wait_recv()
    for t in range(2):
        patch = jnp.concatenate([hidden_rows(t, i) for i in range(3)], axis=1)
        feat[t] = dot(patch, w2[...]).astype(BF).reshape(16, 16, C)
    feat_copy = pltpu.make_async_copy(feat, feat_hbm, feat_sem)
    feat_copy.start()

    def second(tap):
        return w2[tap * C:(tap + 1) * C, :]

    up, down = slice(0, 256), slice(16, 272)
    for t in range(2):
        m0 = jnp.concatenate([masked[t], dot(table["below"][...], halo[t]).astype(BF)], axis=0)
        m1 = (dot(table["back"][...], masked[t]) + dot(table["beside"][...], halo[t])).astype(BF)
        spread = (
            dot_t(m0[up], second(7)) + dot_t(m0[down], second(1)),
            (dot_t(m0[up], second(8)) + dot_t(m1[up], second(6))
             + dot_t(m0[down], second(2)) + dot_t(m1[down], second(0))),
            dot_t(m0[up], second(4)),
            dot_t(m0[up], second(5)) + dot_t(m1[up], second(3)),
        )
        for n in range(4):
            group = 4 * t + n
            d_pre[group * 256:(group + 1) * 256, :] = (spread[n] * slopes[group]).astype(BF)

    y_second(1)

    def own_rows(t, par, i, cp, j):
        row = (2 if par == 0 else 1) + i
        lanes = (cp + j) * C
        return x4[t, row // 2:row // 2 + 16, row % 2, :, lanes:lanes + C].reshape(256, C)

    for i in range(3):
        for j in range(3):
            tap = 3 * i + j
            seen = jnp.concatenate(
                [own_rows(t, par, i, cp, j) for t in range(2) for par in range(2) for cp in range(2)], axis=0)
            g_f[tap * C:(tap + 1) * C, :] = dot_l(seen, d_pre[...])
    blocks(0)
    y_first(0)
    other = other_second(other)
    z_left = z_first(1)
    y_second(0)
    total_second = jnp.concatenate([z_second(1, *z_left), other_third(other)], axis=0)

    def share(n, total):
        both = jnp.concatenate([total[:OWN_ROWS].T, total[OWN_ROWS:].T], axis=0)
        x_send[:, n] = both.reshape(SC, 32, OWN_ROWS)

    z_left = z_first(0)
    share(1, total_second)
    squares = jnp.sum(total_second * total_second, axis=0, keepdims=True)
    total_first = z_second(0, *z_left)
    squares = squares + jnp.sum(total_first * total_first, axis=0, keepdims=True)
    n_send[0] = squares
    all_to_all(5, lambda to: n_send.at[0], lambda me: n_buf.at[me])
    n_buf[r] = squares
    share(0, total_first)
    x_copies = []
    for o in range(1, SC):
        to = (s + o) % SC
        x_copies.append(to_scene(x_send.at[to], x_buf.at[o - 1], xs.at[o - 1], xr.at[o - 1], to))
    await_all(n_buf.at[pl.ds(0, REG - 1)], a2a_r.at[5])
    sum_sq = jnp.sum(n_buf[...].reshape(REG, 128), keepdims=True)
    factor = (3.0 * C * math.sqrt(2.0) / SC) / (jnp.sqrt(sum_sq) + 0.01)
    c_send[0] = jnp.broadcast_to(factor, (1, 128))
    c_copies = []
    for o in range(1, SC):
        to = (s + o) % SC
        c_copies.append(to_scene(c_send.at[0], c_buf.at[o - 1], cs.at[o - 1], cr.at[o - 1], to))
    result = x_send[s] * factor.reshape(1, 1, 1)
    for o in range(1, SC):
        x_copies[o - 1].wait_recv()
        c_copies[o - 1].wait_recv()
        result = result + x_buf[o - 1] * c_buf[o - 1][:, :1].reshape(1, 1, 1)
    out[...] = result
    feat_copy.wait()

    for copy in far + near[0] + near[1] + sent + x_copies + c_copies:
        copy.wait_send()
    await_all(pos_buf.at[pl.ds(0, 2 * REG - 2)], a2a_s.at[0])
    for half in range(2):
        await_all(send1.at[half, pl.ds(0, REG - 1)], a2a_s.at[1 + half])
        await_all(send2.at[half, pl.ds(0, REG - 1)], a2a_s.at[3 + half])
    await_all(n_buf.at[pl.ds(0, REG - 1)], a2a_s.at[5])


NAMES = ("rim", "rim_grad", "body", "sides", "edges", "left", "first_col", "shift", "from_left",
         "back", "below", "beside")
TABLES = dict(zip(NAMES, place_tables()))


def level(positions, clear, tiles, cotangent, w1, w2):
    vmem = pl.BlockSpec(memory_space=pltpu.VMEM)
    anywhere = pl.BlockSpec(memory_space=pl.ANY)
    dma = pltpu.SemaphoreType.DMA
    tables = list(TABLES.values())
    part = (144, 128)
    return pl.pallas_call(
        level_kernel,
        name="level",
        out_shape=(jax.ShapeDtypeStruct((2, 16, 16, C), BF), jax.ShapeDtypeStruct((2, 32, OWN_ROWS), F32)),
        in_specs=[anywhere] * (6 + len(tables)),
        out_specs=(anywhere, vmem),
        scratch_shapes=[pltpu.VMEM(t.shape, BF) for t in tables] + [
            pltpu.VMEM((1, 2), jnp.int32), pltpu.VMEM((1, 2), jnp.int32),
            pltpu.VMEM((2, 32, 32, C), BF), pltpu.VMEM((2, 16, 16, C), BF),
            pltpu.VMEM((2, 16, 16, C), BF), dma, dma((4,)), dma((len(tables),)),
            pltpu.VMEM((2, 1, 128), F32), pltpu.VMEM((2 * REG, 1, 128), F32),
            pltpu.VMEM((2, REG, 16, 128), BF), pltpu.VMEM((2, REG, 16, 128), BF),
            pltpu.VMEM((2, REG, 16, 128), BF), pltpu.VMEM((2, REG, 16, 128), BF),
            pltpu.VMEM((2, 256, C), BF), pltpu.VMEM((2, 256, C), BF), pltpu.VMEM((2, 256, C), BF),
            pltpu.VMEM((ROWS, C), BF), pltpu.VMEM((ROWS, C), BF),
            pltpu.VMEM((2, 18, 2, 16, 4 * C), BF),
            pltpu.VMEM((2, 17, 16, 3 * C), BF), pltpu.VMEM((2, 16, 16, 3 * C), BF),
            pltpu.VMEM((2 * LEFT, ROWS), BF),
            pltpu.VMEM((8, 256, C), F32),
            pltpu.VMEM((2048, C), BF),
            pltpu.VMEM((ROWS, C), F32),
            pltpu.VMEM((2, YN, ZN) + part, BF),
            pltpu.VMEM((2, ZN) + part, BF), pltpu.VMEM((2, ZN) + part, BF),
            pltpu.VMEM((2, ZN) + part, BF), pltpu.VMEM((2, ZN) + part, BF),
            pltpu.VMEM((2, ZN - 1) + part, BF), pltpu.VMEM((2, ZN - 1) + part, BF),
            pltpu.VMEM((ZN - 1, YN, Z_PART, 128), BF), pltpu.VMEM((YN, Z_PART, 128), F32),
            pltpu.VMEM((YN, Z_PART, 128), BF), pltpu.VMEM((YN - 1, Z_PART, 128), BF),
            pltpu.VMEM((1, 1, 128), F32), pltpu.VMEM((REG, 1, 128), F32),
            pltpu.VMEM((SC, 2, 32, OWN_ROWS), F32), pltpu.VMEM((SC - 1, 2, 32, OWN_ROWS), F32),
            pltpu.VMEM((1, 1, 128), F32), pltpu.VMEM((SC - 1, 1, 128), F32),
            dma((6,)), dma((6,)), dma((2, 3)), dma((2, 3)), dma((2, 4)), dma((2, 4)),
            dma((3, 2, ZN)), dma((3, 2, ZN)), dma((2, ZN - 1)), dma((2, ZN - 1)), dma((ZN + YN - 2,)), dma((ZN + YN - 2,)),
            dma((SC - 1,)), dma((SC - 1,)), dma((SC - 1,)), dma((SC - 1,)), dma((2,)),
        ],
        compiler_params=pltpu.CompilerParams(
            collective_id=0, has_side_effects=True, vmem_limit_bytes=VMEM_LIMIT),
    )(positions, clear, tiles, cotangent, w1, w2, *[jnp.asarray(t) for t in tables])


def finish_kernel(feat_in, out_in, feat, first, second):
    feat[...] = feat_in[...]
    first[...] = out_in[0]
    second[...] = out_in[1]


def finish(feat, out):
    vmem = pl.BlockSpec(memory_space=pltpu.VMEM)
    share = jax.ShapeDtypeStruct((32, OWN_ROWS), F32)
    return pl.pallas_call(
        finish_kernel,
        name="finish",
        out_shape=(jax.ShapeDtypeStruct(feat.shape, BF), share, share),
        in_specs=[vmem, vmem],
        out_specs=(vmem, vmem, vmem),
    )(feat, out)


def local(tiles, cotangent, positions, clear, w_first, w_second):
    feat, out = level(positions, clear, tiles[0], cotangent[0], w_first, w_second)
    feat, first, second = finish(feat, out)
    return feat[None], first.T, second.T


def solution(mesh):
    in_specs = (
        P("scene", "region", None, None, None),
        P("scene", "region", None, None, None),
        P("scene", "region"),
        P("scene", "region"),
        P("scene", None),
        P("scene", None),
    )
    out_specs = (P("scene", "region", None, None, None), P("region", "scene"), P("region", "scene"))
    return jax.shard_map(local, mesh=mesh, in_specs=in_specs, out_specs=out_specs, check_vma=False)
```
